32 devices in a mesh: grp: 2 (over y), seq: 4 (over z), dp: 2 (over x), pipe: 2 (over core).
Axes of the slice: x: 2, y: 2, z: 4, core: 2. Of those that a mesh axis runs over, the one named last changes fastest.
Arguments:
- embeddings: bfloat16 [4, 512, 1664], P(('grp', 'dp'), 'seq'), parts along dimension 0, may hold values from -650 to 650
- upstream: bfloat16 [4, 512, 1664], P(('grp', 'dp'), 'seq'), parts along dimension 0, may hold values from -6 to 6
- attn_weights: bfloat16 [4, 1664, 832], P(None, ('seq', 'dp'), 'pipe'), may hold values from -1.2747549 to 1.2747549
Outputs:
- input_grads: bfloat16 [4, 512, 1664], P(('grp', 'dp'), 'seq'), parts along dimension 0
- weight_grads: float32 [8, 1664, 832], P('grp', ('seq', 'dp'), 'pipe'), parts along dimension 0
The draws below stay inside these ranges and needn't reach their ends.
There are 2 independent parts, one for each index of `grp`. The reference program is written for one: setup_inputs(seed, part) draws one part's arguments, and reference() takes and returns one part's arrays. A program takes and returns all parts, laid end to end along the dimension named above; an argument that names none is the same for every part. Nothing has to cross between parts.
All inputs are finite; a program needn't handle non-finite values.
Results may differ from the reference program's by a relative error of at most 0.014.
The reference program's roundings to bfloat16 on the way count: a program that leaves them out, or rounds other values in their place, can miss the bound.
Values may be sent and summed in bfloat16 or wider, within the bound.
No kernel may reach another device: no remote copies, remote signals or barrier semaphores. Data moves between devices by JAX's collectives and lax.ppermute only.
A program may use at most 128 MiB of HBM per device.

```python
import math
import jax
import jax.numpy as jnp
from jax import lax

D = 1664
HD = 104
HEADS = 8
TOK_DEV = 128
PATCHES = 512
IMAGES = 2
N_SEQ = 4


def draw_embeddings(key, part):
    pieces = jax.random.split(key, 3)
    spread = math.log(10.0)
    row_scale = jnp.exp(jax.random.uniform(pieces[1], (IMAGES, PATCHES, 1), jnp.float32, 0.0, spread))
    col_scale = jnp.exp(jax.random.uniform(pieces[2], (1, 1, D), jnp.float32, 0.0, spread))
    core = jnp.clip(jax.random.normal(pieces[0], (IMAGES, PATCHES, D), jnp.float32), -4.0, 4.0)
    value = core * row_scale * col_scale
    return value.astype(jnp.bfloat16)


def draw_attn_weights(key, part):
    pieces = jax.random.split(key, 1)
    fan_in = jnp.array([D, D, D, HEADS * HD], jnp.float32)
    scaling = (fan_in ** (-0.5))[:, None, None]
    base = jnp.clip(jax.random.normal(pieces[0], (4, D, HEADS * HD), jnp.float32), -6.0, 6.0)
    return (base * scaling).astype(jnp.bfloat16)


def strengthened(values, rng, source, target, shards_of, factor):
    owner, partner = [(jnp.arange(values.shape[axis_at]) // (values.shape[axis_at] // shards_of)).reshape([-1 if axis == axis_at else 1 for axis in range(values.ndim)]) for axis_at in (source, target)]
    chosen = jax.random.permutation(rng, shards_of)[partner]
    strong = (owner == chosen) | (owner == (partner + shards_of // 2) % shards_of)
    return jnp.where(strong, factor * values, values)


def level_of(stream_key, dims, cuts, least, top_value):
    def one(dim, shards_of):
        steps = jax.random.uniform(jax.random.fold_in(jax.random.fold_in(stream_key, 6), dim), (shards_of,), jnp.float32, least / len(cuts), top_value / len(cuts))
        return jnp.repeat(jnp.exp(steps), dims[dim] // shards_of).reshape((-1,) + (1,) * (len(dims) - dim - 1))

    level = one(*cuts[0])
    for cut in cuts[1:]:
        level = level * one(*cut)
    return level


def bell_draw_with(stream_key, shape, deviation, bound, cuts, heavy, dtype=jnp.bfloat16):
    values = deviation * jax.random.normal(stream_key, shape, jnp.float32)
    if cuts:
        values = values * level_of(stream_key, shape, cuts, -0.22, 0.18)
    return jnp.clip(strengthened(values, jax.random.fold_in(stream_key, 3), *heavy), -bound, bound).astype(dtype)


def setup_inputs(seed: int = 0, part: int = 0) -> dict:
    keys = jax.random.split(jax.random.key(seed), 4)
    own_keys = jax.random.split(jax.random.fold_in(keys[3], part), 4)
    return {
        "embeddings": draw_embeddings(jax.random.fold_in(jax.random.fold_in(keys[3], part), 71), part),
        "upstream": bell_draw_with(own_keys[1], (IMAGES, PATCHES, D), 1.0, 6.0, ((0, 2), (1, 4)), (1, 2, 4, 2.0)),
        "attn_weights": draw_attn_weights(jax.random.fold_in(keys[3], 71), part),
    }


EPSILON = 1e-06

def one_image(tokens, upstream, attn_weights):
    features = tokens.astype(jnp.float32)
    row_mean = lax.optimization_barrier(jnp.mean(features, axis=1, keepdims=True))
    mean_removed = features - row_mean
    variance = lax.optimization_barrier(jnp.mean(mean_removed * mean_removed, axis=1, keepdims=True))
    inverse_deviation = lax.rsqrt(variance + EPSILON)
    standardized_input = mean_removed * inverse_deviation
    normalized_rows = standardized_input.astype(jnp.bfloat16)
    weights_f = attn_weights.astype(jnp.float32)
    proj = jnp.einsum('td,cdh->cth', normalized_rows.astype(jnp.float32), weights_f[:3]).astype(jnp.bfloat16)
    patch_count = tokens.shape[0]
    score_scale = HD ** (-0.5)
    per_head = proj.reshape(3, patch_count, HEADS, HD).transpose(2, 0, 1, 3)
    grad_att = jnp.dot(upstream, attn_weights[3], preferred_element_type=jnp.float32).astype(jnp.bfloat16)
    grad_heads = grad_att.reshape(patch_count, HEADS, HD).transpose(1, 0, 2)

    def one_head(pair):
        triple, grad_out = pair
        query_rows, key_rows, value_rows = (triple[0], triple[1], triple[2])
        scores = jnp.dot(query_rows, key_rows.T, preferred_element_type=jnp.float32) * score_scale
        row_max = lax.optimization_barrier(jnp.max(scores, axis=1, keepdims=True))
        log_total = row_max + jnp.log(lax.optimization_barrier(jnp.sum(jnp.exp(scores - row_max), axis=1, keepdims=True)))
        probs = jnp.exp(scores - log_total).astype(jnp.bfloat16)
        attended = jnp.dot(probs, value_rows, preferred_element_type=jnp.float32).astype(jnp.bfloat16)
        row_delta = lax.optimization_barrier(jnp.sum(grad_out.astype(jnp.float32) * attended.astype(jnp.float32), axis=1, keepdims=True))
        dprobs = jnp.dot(grad_out, value_rows.T, preferred_element_type=jnp.float32)
        dscores = (probs.astype(jnp.float32) * (dprobs - row_delta) * score_scale).astype(jnp.bfloat16)
        grad_q = jnp.dot(dscores, key_rows, preferred_element_type=jnp.float32).astype(jnp.bfloat16)
        ds_blocks = dscores.reshape(N_SEQ, TOK_DEV, patch_count).astype(jnp.float32)
        pr_blocks = probs.reshape(N_SEQ, TOK_DEV, patch_count).astype(jnp.float32)
        q_blocks = query_rows.reshape(N_SEQ, TOK_DEV, HD).astype(jnp.float32)
        g_blocks = grad_out.reshape(N_SEQ, TOK_DEV, HD).astype(jnp.float32)
        k_terms = jnp.einsum('nqk,nqd->nkd', ds_blocks, q_blocks)
        v_terms = jnp.einsum('nqk,nqd->nkd', pr_blocks, g_blocks)
        k_terms = lax.optimization_barrier(k_terms.astype(jnp.bfloat16)).astype(jnp.float32)
        v_terms = lax.optimization_barrier(v_terms.astype(jnp.bfloat16)).astype(jnp.float32)
        grad_k = lax.optimization_barrier(jnp.sum(k_terms, axis=0)).astype(jnp.bfloat16)
        grad_v = lax.optimization_barrier(jnp.sum(v_terms, axis=0)).astype(jnp.bfloat16)
        return jnp.stack([attended, grad_q, grad_k, grad_v])
    results = lax.map(one_head, (per_head, grad_heads))
    merged = results.transpose(1, 2, 0, 3).reshape(4, patch_count, HEADS * HD)
    attended = merged[0]
    grads_qkv = merged[1:].astype(jnp.float32)
    terms_qkv = jnp.einsum('td,cth->cdh', normalized_rows.astype(jnp.float32), grads_qkv)
    term_out = jnp.dot(upstream.T, attended, preferred_element_type=jnp.float32)
    terms = jnp.concatenate([terms_qkv, term_out[None]], axis=0)
    normalized_gradient = jnp.einsum('cth,cdh->td', grads_qkv, weights_f[:3])
    leading_term = lax.optimization_barrier(jnp.mean(normalized_gradient, axis=1, keepdims=True))
    trailing_term = lax.optimization_barrier(jnp.mean(normalized_gradient * standardized_input, axis=1, keepdims=True))
    input_gradient = upstream.astype(jnp.float32) + inverse_deviation * (normalized_gradient - leading_term - standardized_input * trailing_term)
    return (input_gradient.astype(jnp.bfloat16), terms)

def reference(embeddings, upstream, attn_weights):

    def per_image(pair):
        return one_image(pair[0], pair[1], attn_weights)
    input_grads, terms = lax.map(per_image, (embeddings, upstream))
    grad_factor = 1.0 / math.sqrt(IMAGES * PATCHES)
    weight_grads = lax.optimization_barrier(jnp.sum(terms, axis=0)) * grad_factor
    return (input_grads, weight_grads)
```

```python
import functools
import math

import jax
import jax.numpy as jnp
from jax import lax
from jax.experimental import pallas as pl
from jax.experimental.pallas import tpu as pltpu
from jax.sharding import PartitionSpec as P

HD = 104
SLOT = 128

EPSILON = 1e-06
BF = jnp.bfloat16
F32 = jnp.float32
PARAMS = pltpu.CompilerParams(vmem_limit_bytes=56 * 1024 * 1024)
VMEM_SPEC = pl.BlockSpec(memory_space=pltpu.VMEM)
ANY_SPEC = pl.BlockSpec(memory_space=pl.ANY)


def standardize(features):
    row_mean = jnp.mean(features, axis=1, keepdims=True)
    mean_removed = features - row_mean
    variance = jnp.mean(mean_removed * mean_removed, axis=1, keepdims=True)
    inverse_deviation = lax.rsqrt(variance + EPSILON)
    return mean_removed * inverse_deviation, inverse_deviation


def nt(a, b):
    return lax.dot_general(a, b, (((1,), (1,)), ((), ())), preferred_element_type=F32)


def tn(a, b):
    return lax.dot_general(a, b, (((0,), (0,)), ((), ())), preferred_element_type=F32)


def nn(a, b):
    return jnp.dot(a, b, preferred_element_type=F32)


def pack_kernel(n, w_ref, *refs):
    outs, staged = refs[:n], refs[n]
    me = lax.axis_index("seq")
    rows = w_ref.shape[1]
    fill = jnp.zeros((rows, SLOT - HD), BF)
    for head in range(n):
        for mat in range(4):
            block = w_ref[mat, :, head * HD : (head + 1) * HD]
            staged[head, :, mat * SLOT : (mat + 1) * SLOT] = jnp.concatenate([block, fill], axis=1)
    for k in range(n):
        outs[k][...] = staged[me ^ k]


def norm_kernel(x_ref, up_ref, normed_ref, send_ref):
    core = lax.axis_index("pipe")
    normed = standardize(x_ref[...].astype(F32))[0].astype(BF)
    normed_ref[...] = normed

    @pl.when(core == 0)
    def _():
        send_ref[...] = normed

    @pl.when(core != 0)
    def _():
        send_ref[...] = up_ref[...]


def head_kernel(n, *refs):
    normed_ref, up_ref = refs[:2]
    got = refs[2 : 1 + n]
    swapped = refs[1 + n : 2 * n]
    w_own = refs[2 * n : 3 * n]
    w_other = refs[3 * n : 4 * n]
    keep_ref, give_ref, grads_ref, x_full, up_full = refs[4 * n : 4 * n + 5]
    w_full, term_k, term_v, sems, wsems = refs[4 * n + 5 :]
    me = lax.axis_index("seq")
    image = lax.axis_index("dp")
    core = lax.axis_index("pipe")
    rows = normed_ref.shape[0]
    share = w_own[0].shape[0]
    local = [(normed_ref, x_full), (up_ref, up_full)]

    weight_copies = []
    for k in range(n):
        for which, (source, at) in enumerate(((w_own[k], image), (w_other[k], 1 - image))):
            first = pl.multiple_of(((me ^ k) * 2 + at) * share, 16)
            copy = pltpu.make_async_copy(
                source, w_full.at[pl.ds(first, share), :], wsems.at[k, which]
            )
            copy.start()
            weight_copies.append(copy)
    copies = []
    for which, (source, target) in enumerate(local):
        copy = pltpu.make_async_copy(source, target.at[pl.ds(0, rows), :], sems.at[which, 0])
        copy.start()
        copies.append(copy)

    def blocks(first, second):
        made = []
        for k in range(1, n):
            for which, source in ((0, first[k - 1]), (1, second[k - 1])):
                made.append(
                    pltpu.make_async_copy(
                        source,
                        local[which][1].at[pl.ds(k * rows, rows), :],
                        sems.at[which, k],
                    )
                )
        return made

    @pl.when(core == 0)
    def _():
        for copy in blocks(got, swapped):
            copy.start()

    @pl.when(core != 0)
    def _():
        for copy in blocks(swapped, got):
            copy.start()

    for copy in weight_copies + copies + blocks(got, swapped):
        copy.wait()

    scale = HD ** (-0.5)
    qkv = nn(x_full[...], w_full[:, : 3 * SLOT]).astype(BF)
    grad_att = nn(up_full[...], w_full[:, 3 * SLOT :]).astype(BF)
    key_rows = qkv[:, SLOT : 2 * SLOT]
    value_rows = qkv[:, 2 * SLOT :]
    for b in range(n):
        span = slice(b * rows, (b + 1) * rows)
        query = qkv[span, :SLOT]
        grad_out = grad_att[span]
        scores = nt(query, key_rows) * scale
        weight = jnp.exp(scores - jnp.max(scores, axis=1, keepdims=True))
        probs = (weight / jnp.sum(weight, axis=1, keepdims=True)).astype(BF)
        attended = nn(probs, value_rows).astype(BF)
        delta = jnp.sum(grad_out.astype(F32) * attended.astype(F32), axis=1, keepdims=True)
        dprobs = nt(grad_out, value_rows)
        dscores = (probs.astype(F32) * (dprobs - delta) * scale).astype(BF)
        grads_ref[span, :SLOT] = nn(dscores, key_rows).astype(BF)
        grads_ref[span, 3 * SLOT :] = attended
        key_term = tn(dscores, query).astype(BF).astype(F32)
        value_term = tn(probs, grad_out).astype(BF).astype(F32)
        if b == 0:
            term_k[...] = key_term
            term_v[...] = value_term
        else:
            term_k[...] += key_term
            term_v[...] += value_term
    grads_ref[:, SLOT : 2 * SLOT] = term_k[...].astype(BF)
    grads_ref[:, 2 * SLOT : 3 * SLOT] = term_v[...].astype(BF)
    half = rows // 2
    for b in range(n):
        span = slice(b * rows, (b + 1) * rows)
        part = nt(grads_ref[span, : 3 * SLOT], w_full[:, : 3 * SLOT]).astype(BF)

        @pl.when(core == 0)
        def _():
            keep_ref[b] = part[:half]
            give_ref[b] = part[half:]

        @pl.when(core != 0)
        def _():
            keep_ref[b] = part[half:]
            give_ref[b] = part[:half]


def weight_kernel(n, factor, x_ref, up_ref, grads_ref, keep_ref, give_ref, staged):
    me = lax.axis_index("seq")
    image = lax.axis_index("dp")
    share = keep_ref.shape[1]
    staged[:, : 3 * SLOT] = (tn(x_ref[...], grads_ref[:, : 3 * SLOT]) * factor).astype(BF)
    staged[:, 3 * SLOT :] = (tn(up_ref[...], grads_ref[:, 3 * SLOT :]) * factor).astype(BF)
    for k in range(n):
        for target, at in ((keep_ref, image), (give_ref, 1 - image)):
            first = pl.multiple_of(((me ^ k) * 2 + at) * share, 16)
            target[k] = staged[pl.ds(first, share), :]


def sum_kernel(n, mine_ref, theirs_ref, *outs):
    for k in range(n):
        outs[k][...] = (mine_ref[k].astype(F32) + theirs_ref[k].astype(F32)).astype(BF)


def final_kernel(n, x_ref, up_ref, *refs):
    parts, out_ref = refs[:n], refs[n]
    half = out_ref.shape[0]
    core = lax.axis_index("pipe")
    span = pl.ds(pl.multiple_of(core * half, half), half)
    total = parts[0][...].astype(F32)
    for part in parts[1:]:
        total += part[...].astype(F32)
    xhat, inverse_deviation = standardize(x_ref[span, :].astype(F32))
    leading = jnp.mean(total, axis=1, keepdims=True)
    trailing = jnp.mean(total * xhat, axis=1, keepdims=True)
    out_ref[...] = (
        up_ref[span, :].astype(F32) + inverse_deviation * (total - leading - xhat * trailing)
    ).astype(BF)


def join_kernel(mine_ref, theirs_ref, out_ref):
    core = lax.axis_index("pipe")
    half = mine_ref.shape[0]
    out_ref[pl.ds(pl.multiple_of(core * half, half), half), :] = mine_ref[...]
    out_ref[pl.ds(pl.multiple_of((1 - core) * half, half), half), :] = theirs_ref[...]


def unpack_kernel(n, *refs):
    parts, out_ref, staged = refs[:n], refs[n], refs[n + 1]
    me = lax.axis_index("seq")
    for k in range(n):
        staged[me ^ k] = parts[k][...]
    for head in range(n):
        for mat in range(4):
            out_ref[mat, :, head * HD : (head + 1) * HD] = staged[
                head, :, mat * SLOT : mat * SLOT + HD
            ].astype(F32)


def call(kernel, out_shape, args, scratch=(), specs=None):
    single = not isinstance(out_shape, list)
    shapes = [out_shape] if single else out_shape
    out = pl.pallas_call(
        kernel,
        out_shape=[jax.ShapeDtypeStruct(*s) for s in shapes],
        in_specs=[VMEM_SPEC] * len(args) if specs is None else specs,
        out_specs=[VMEM_SPEC] * len(shapes),
        scratch_shapes=list(scratch),
        compiler_params=PARAMS,
    )(*args)
    return out[0] if single else out


def local_heads(embeddings, upstream, attn_weights):
    n = lax.axis_size("seq")
    x, up = embeddings[0], upstream[0]
    rows, width = x.shape
    share = attn_weights.shape[1]
    patches = n * rows
    half = rows // 2

    def across(value, k):
        return lax.ppermute(value, "seq", [(i, i ^ k) for i in range(n)])

    def swap(value, axis):
        return lax.ppermute(value, axis, [(0, 1), (1, 0)])

    chunks = call(
        functools.partial(pack_kernel, n),
        [((share, 4 * SLOT), BF)] * n,
        (attn_weights,),
        [pltpu.VMEM((n, share, 4 * SLOT), BF)],
    )
    w_own = [chunks[0]] + [across(chunks[k], k) for k in range(1, n)]
    w_other = [swap(w, "dp") for w in w_own]
    normed, send = call(norm_kernel, [((rows, width), BF)] * 2, (x, up))
    got = [across(send, k) for k in range(1, n)]
    swapped = [swap(g, "pipe") for g in got]
    args = (normed, up, *got, *swapped, *w_own, *w_other)
    keep, give, grads, x_full, up_full = call(
        functools.partial(head_kernel, n),
        [
            ((n, half, width), BF),
            ((n, half, width), BF),
            ((patches, 4 * SLOT), BF),
            ((patches, width), BF),
            ((patches, width), BF),
        ],
        args,
        [
            pltpu.VMEM((width, 4 * SLOT), BF),
            pltpu.VMEM((patches, SLOT), F32),
            pltpu.VMEM((patches, SLOT), F32),
            pltpu.SemaphoreType.DMA((2, n)),
            pltpu.SemaphoreType.DMA((n, 2)),
        ],
        [ANY_SPEC] * len(args),
    )
    taken = swap(give, "pipe")
    sums = call(functools.partial(sum_kernel, n), [((half, width), BF)] * n, (keep, taken))
    parts = [sums[0]] + [across(sums[k], k) for k in range(1, n)]
    factor = 1.0 / math.sqrt(patches * lax.axis_size("dp"))
    w_keep, w_give = call(
        functools.partial(weight_kernel, n, factor),
        [((n, share, 4 * SLOT), BF)] * 2,
        (x_full, up_full, grads),
        [pltpu.VMEM((width, 4 * SLOT), BF)],
    )
    w_taken = swap(w_give, "dp")
    w_sums = call(
        functools.partial(sum_kernel, n), [((share, 4 * SLOT), BF)] * n, (w_keep, w_taken)
    )
    w_parts = [w_sums[0]] + [across(w_sums[k], k) for k in range(1, n)]
    mine = call(functools.partial(final_kernel, n), ((half, width), BF), (x, up, *parts))
    input_gradient = call(join_kernel, ((rows, width), BF), (mine, swap(mine, "pipe")))
    weight_grads = call(
        functools.partial(unpack_kernel, n),
        ((4, share, n * HD), F32),
        tuple(w_parts),
        [pltpu.VMEM((n, share, 4 * SLOT), BF)],
    )
    return (input_gradient[None], weight_grads)


def local_gathered(embeddings, upstream, attn_weights):
    tokens = embeddings[0]
    row_gradients = upstream[0]
    row_count = tokens.shape[0]
    weights = lax.all_gather(attn_weights, ("seq", "dp"), axis=1, tiled=True)
    local_width = weights.shape[2]
    head_count = local_width // HD
    score_scale = HD ** (-0.5)
    standardized_input, inverse_deviation = standardize(tokens.astype(F32))
    normalized_rows = standardized_input.astype(BF)
    proj = jnp.einsum(
        "td,cdh->cth", normalized_rows, weights[:3], preferred_element_type=F32
    ).astype(BF)
    gathered = lax.all_gather(proj[1:], "seq", axis=1, tiled=True)
    key_count = gathered.shape[1]
    query_heads = proj[0].reshape(row_count, head_count, HD).transpose(1, 0, 2)
    key_heads = gathered[0].reshape(key_count, head_count, HD).transpose(1, 0, 2)
    value_heads = gathered[1].reshape(key_count, head_count, HD).transpose(1, 0, 2)
    grad_att = jnp.dot(row_gradients, weights[3], preferred_element_type=F32).astype(BF)
    grad_heads = grad_att.reshape(row_count, head_count, HD).transpose(1, 0, 2)

    def one_head(items):
        query_rows, key_rows, value_rows, grad_out = items
        scores = nn(query_rows, key_rows.T) * score_scale
        row_max = jnp.max(scores, axis=1, keepdims=True)
        log_total = row_max + jnp.log(jnp.sum(jnp.exp(scores - row_max), axis=1, keepdims=True))
        probs = jnp.exp(scores - log_total).astype(BF)
        attended = nn(probs, value_rows).astype(BF)
        row_delta = jnp.sum(
            grad_out.astype(F32) * attended.astype(F32), axis=1, keepdims=True
        )
        dprobs = nn(grad_out, value_rows.T)
        dscores = (probs.astype(F32) * (dprobs - row_delta) * score_scale).astype(BF)
        grad_q = nn(dscores, key_rows).astype(BF)
        return (attended, grad_q, nn(dscores.T, query_rows), nn(probs.T, grad_out))

    attended_h, grad_q_h, key_h, value_h = lax.map(
        one_head, (query_heads, key_heads, value_heads, grad_heads)
    )
    attended_flat = attended_h.transpose(1, 0, 2).reshape(row_count, local_width)
    grad_q = grad_q_h.transpose(1, 0, 2).reshape(1, row_count, local_width)
    key_terms = key_h.transpose(1, 0, 2).reshape(key_count, local_width)
    value_terms = value_h.transpose(1, 0, 2).reshape(key_count, local_width)
    both_terms = jnp.stack([key_terms, value_terms])
    owned = lax.psum_scatter(both_terms.astype(BF), "seq", scatter_dimension=1, tiled=True)
    grad_qkv = jnp.concatenate([grad_q, owned], axis=0)
    token_count = row_count * lax.axis_size("seq") * lax.axis_size("dp")
    grad_factor = 1.0 / math.sqrt(token_count)
    terms_qkv = jnp.einsum("td,cth->cdh", normalized_rows, grad_qkv, preferred_element_type=F32)
    term_out = jnp.einsum("td,th->dh", row_gradients, attended_flat, preferred_element_type=F32)
    terms = jnp.concatenate([terms_qkv, term_out[None]], axis=0) * grad_factor
    seq_summed = lax.psum_scatter(terms.astype(BF), "seq", scatter_dimension=1, tiled=True)
    weight_grads = lax.psum_scatter(seq_summed, "dp", scatter_dimension=1, tiled=True).astype(F32)
    input_part = jnp.einsum("cth,cdh->td", grad_qkv, weights[:3], preferred_element_type=F32)
    reduced_total = lax.psum(input_part.astype(BF), "pipe").astype(F32)
    leading_term = jnp.mean(reduced_total, axis=1, keepdims=True)
    trailing_term = jnp.mean(reduced_total * standardized_input, axis=1, keepdims=True)
    input_gradient = (
        row_gradients.astype(F32)
        + inverse_deviation * (reduced_total - leading_term - standardized_input * trailing_term)
    ).astype(BF)
    return (input_gradient[None], weight_grads)


def local(embeddings, upstream, attn_weights):
    n = lax.axis_size("seq")
    heads = attn_weights.shape[2] // HD
    one_head_each = (
        heads == n
        and n & (n - 1) == 0
        and lax.axis_size("dp") == 2
        and lax.axis_size("pipe") == 2
        and attn_weights.shape[1] % 16 == 0
        and embeddings.shape[0] == 1
        and embeddings.shape[1] % 32 == 0
    )
    return (local_heads if one_head_each else local_gathered)(embeddings, upstream, attn_weights)


def solution(mesh):
    in_specs = (
        P(("grp", "dp"), "seq", None),
        P(("grp", "dp"), "seq", None),
        P(None, ("seq", "dp"), "pipe"),
    )
    out_specs = (P(("grp", "dp"), "seq", None), P("grp", ("seq", "dp"), "pipe"))
    return jax.shard_map(local, mesh=mesh, in_specs=in_specs, out_specs=out_specs, check_vma=False)
```

```python
import functools
import math

import jax
import jax.numpy as jnp
from jax import lax
from jax.experimental import pallas as pl
from jax.experimental.pallas import tpu as pltpu
from jax.sharding import PartitionSpec as P

HD = 104
SLOT = 128

EPSILON = 1e-06
BF = jnp.bfloat16
F32 = jnp.float32
PARAMS = pltpu.CompilerParams(vmem_limit_bytes=56 * 1024 * 1024)
VMEM_SPEC = pl.BlockSpec(memory_space=pltpu.VMEM)
ANY_SPEC = pl.BlockSpec(memory_space=pl.ANY)


def standardize(features):
    row_mean = jnp.mean(features, axis=1, keepdims=True)
    mean_removed = features - row_mean
    variance = jnp.mean(mean_removed * mean_removed, axis=1, keepdims=True)
    inverse_deviation = lax.rsqrt(variance + EPSILON)
    return mean_removed * inverse_deviation, inverse_deviation


def nt(a, b):
    return lax.dot_general(a, b, (((1,), (1,)), ((), ())), preferred_element_type=F32)


def tn(a, b):
    return lax.dot_general(a, b, (((0,), (0,)), ((), ())), preferred_element_type=F32)


def nn(a, b):
    return jnp.dot(a, b, preferred_element_type=F32)


def pack_kernel(n, w_ref, *refs):
    outs, staged = refs[:n], refs[n]
    me = lax.axis_index("seq")
    group = lax.axis_index("grp")
    rows = w_ref.shape[1]
    fill = jnp.zeros((rows, SLOT - HD), BF)
    for head in range(n):
        for mat in range(4):
            block = w_ref[mat, :, head * HD : (head + 1) * HD]
            first = (mat % 2) * SLOT
            staged[mat // 2, head, :, first : first + SLOT] = jnp.concatenate(
                [block, fill], axis=1
            )
    for k in range(n):
        outs[k][...] = staged[group, me ^ k]


def norm_kernel(x_ref, up_ref, send_ref, rest_ref, staged):
    core = lax.axis_index("pipe")
    half = x_ref.shape[0] // 2
    staged[...] = standardize(x_ref[...].astype(F32))[0].astype(BF)
    for target, at in ((send_ref, core), (rest_ref, 1 - core)):
        span = pl.ds(pl.multiple_of(at * half, half), half)
        target[:half] = staged[span, :]
        target[half:] = up_ref[span, :]


def merge_kernel(*refs):
    share = refs[0].shape[0]
    for k, ref in enumerate(refs[:-1]):
        refs[-1][k * share : (k + 1) * share] = ref[...]


def head_kernel(n, *refs):
    got, swapped = refs[:n], refs[n : 2 * n]
    pieces = refs[2 * n : 2 * n + 4]
    keep_ref, give_ref, grads_ref, x_full, up_full = refs[2 * n + 4 : 2 * n + 9]
    w_full, term_k, term_v, sems, wsems = refs[2 * n + 9 :]
    me = lax.axis_index("seq")
    image = lax.axis_index("dp")
    group = lax.axis_index("grp")
    rows = got[0].shape[0]
    half = rows // 2
    share = pieces[0].shape[0] // n

    copies = []
    for which, source in enumerate(pieces):
        at = 1 - image if which % 2 else image
        mats = 1 - group if which // 2 else group
        for k in range(n):
            first = pl.multiple_of(((me ^ k) * 2 + at) * share, 16)
            lanes = pl.multiple_of(mats * 2 * SLOT, 2 * SLOT)
            copies.append(
                pltpu.make_async_copy(
                    source.at[pl.ds(k * share, share), :],
                    w_full.at[pl.ds(first, share), pl.ds(lanes, 2 * SLOT)],
                    wsems.at[which, k],
                )
            )
    for k in range(n):
        for side, source in enumerate((got[k], swapped[k])):
            for which, target in enumerate((x_full, up_full)):
                copies.append(
                    pltpu.make_async_copy(
                        source.at[pl.ds(which * half, half), :],
                        target.at[pl.ds(k * rows + side * half, half), :],
                        sems.at[k, side, which],
                    )
                )
    for copy in copies:
        copy.start()
    for copy in copies:
        copy.wait()

    scale = HD ** (-0.5)
    qkv = nn(x_full[...], w_full[:, : 3 * SLOT]).astype(BF)
    grad_att = nn(up_full[...], w_full[:, 3 * SLOT :]).astype(BF)
    key_rows = qkv[:, SLOT : 2 * SLOT]
    value_rows = qkv[:, 2 * SLOT :]
    for b in range(n):
        span = slice(b * rows, (b + 1) * rows)
        query = qkv[span, :SLOT]
        grad_out = grad_att[span]
        scores = nt(query, key_rows) * scale
        weight = jnp.exp(scores - jnp.max(scores, axis=1, keepdims=True))
        probs = (weight / jnp.sum(weight, axis=1, keepdims=True)).astype(BF)
        attended = nn(probs, value_rows).astype(BF)
        delta = jnp.sum(grad_out.astype(F32) * attended.astype(F32), axis=1, keepdims=True)
        dprobs = nt(grad_out, value_rows)
        dscores = (probs.astype(F32) * (dprobs - delta) * scale).astype(BF)
        grads_ref[span, :SLOT] = nn(dscores, key_rows).astype(BF)
        grads_ref[span, 3 * SLOT :] = attended
        key_term = tn(dscores, query).astype(BF).astype(F32)
        value_term = tn(probs, grad_out).astype(BF).astype(F32)
        if b == 0:
            term_k[...] = key_term
            term_v[...] = value_term
        else:
            term_k[...] += key_term
            term_v[...] += value_term
    grads_ref[:, SLOT : 2 * SLOT] = term_k[...].astype(BF)
    grads_ref[:, 2 * SLOT : 3 * SLOT] = term_v[...].astype(BF)
    for b in range(n):
        span = slice(b * rows, (b + 1) * rows)
        part = nt(grads_ref[span, : 3 * SLOT], w_full[:, : 3 * SLOT]).astype(BF)
        keep_ref[b] = part[:half]
        give_ref[b] = part[half:]


def weight_kernel(n, factor, x_ref, up_ref, grads_ref, keep_ref, give_ref, staged):
    me = lax.axis_index("seq")
    image = lax.axis_index("dp")
    share = keep_ref.shape[1]
    staged[:, : 3 * SLOT] = (tn(x_ref[...], grads_ref[:, : 3 * SLOT]) * factor).astype(BF)
    staged[:, 3 * SLOT :] = (tn(up_ref[...], grads_ref[:, 3 * SLOT :]) * factor).astype(BF)
    for k in range(n):
        for target, at in ((keep_ref, image), (give_ref, 1 - image)):
            first = pl.multiple_of(((me ^ k) * 2 + at) * share, 16)
            target[k] = staged[pl.ds(first, share), :]


def sum_kernel(n, mine_ref, theirs_ref, *outs):
    for k in range(n):
        outs[k][...] = (mine_ref[k].astype(F32) + theirs_ref[k].astype(F32)).astype(BF)


def final_kernel(n, x_ref, up_ref, *refs):
    parts, out_ref = refs[:n], refs[n]
    half = out_ref.shape[0]
    core = lax.axis_index("pipe")
    span = pl.ds(pl.multiple_of(core * half, half), half)
    total = parts[0][...].astype(F32)
    for part in parts[1:]:
        total += part[...].astype(F32)
    xhat, inverse_deviation = standardize(x_ref[span, :].astype(F32))
    leading = jnp.mean(total, axis=1, keepdims=True)
    trailing = jnp.mean(total * xhat, axis=1, keepdims=True)
    out_ref[...] = (
        up_ref[span, :].astype(F32) + inverse_deviation * (total - leading - xhat * trailing)
    ).astype(BF)


def join_kernel(mine_ref, theirs_ref, out_ref):
    core = lax.axis_index("pipe")
    half = mine_ref.shape[0]
    out_ref[pl.ds(pl.multiple_of(core * half, half), half), :] = mine_ref[...]
    out_ref[pl.ds(pl.multiple_of((1 - core) * half, half), half), :] = theirs_ref[...]


def unpack_kernel(n, *refs):
    parts, out_ref, staged = refs[:n], refs[n], refs[n + 1]
    me = lax.axis_index("seq")
    for k in range(n):
        staged[me ^ k] = parts[k][...]
    for head in range(n):
        for mat in range(4):
            out_ref[mat, :, head * HD : (head + 1) * HD] = staged[
                head, :, mat * SLOT : mat * SLOT + HD
            ].astype(F32)


def call(kernel, out_shape, args, scratch=(), specs=None):
    single = not isinstance(out_shape, list)
    shapes = [out_shape] if single else out_shape
    out = pl.pallas_call(
        kernel,
        out_shape=[jax.ShapeDtypeStruct(*s) for s in shapes],
        in_specs=[VMEM_SPEC] * len(args) if specs is None else specs,
        out_specs=[VMEM_SPEC] * len(shapes),
        scratch_shapes=list(scratch),
        compiler_params=PARAMS,
    )(*args)
    return out[0] if single else out


def local_heads(embeddings, upstream, attn_weights):
    n = lax.axis_size("seq")
    x, up = embeddings[0], upstream[0]
    rows, width = x.shape
    share = attn_weights.shape[1]
    patches = n * rows
    half = rows // 2
    me = lax.axis_index("seq")

    def across(value, k):
        return lax.ppermute(value, "seq", [(i, i ^ k) for i in range(n)])

    def swap(value, axis):
        return lax.ppermute(value, axis, [(0, 1), (1, 0)])

    def near(values):
        return [pltpu.with_memory_space_constraint(v, pltpu.VMEM) for v in values]

    chunks = call(
        functools.partial(pack_kernel, n),
        [((share, 2 * SLOT), BF)] * n,
        (attn_weights,),
        [pltpu.VMEM((2, n, share, 2 * SLOT), BF)],
    )
    arrived = [across(chunks[k], k) for k in range(1, n)]
    send, rest = call(
        norm_kernel, [((rows, width), BF)] * 2, (x, up), [pltpu.VMEM((rows, width), BF)]
    )
    send, *arrived = lax.optimization_barrier((send, *arrived))
    merged = call(merge_kernel, ((n * share, 2 * SLOT), BF), (chunks[0], *near(arrived)))
    beside = swap(merged, "dp")
    above = swap(merged, "grp")
    corner = swap(above, "dp")

    second = across(send, 2)
    first = across(send, 1)
    later, second = lax.optimization_barrier((send, second))
    middle = lax.ppermute(later, "seq", [(1, 2), (2, 1)])
    passed = lax.ppermute(second, "seq", [(2, 3), (1, 0)])
    third = jnp.where((me == 0) | (me == n - 1), passed, middle)
    got = [send, first, second, third]
    swapped = [rest] + [swap(g, "pipe") for g in got[1:]]
    args = (*got[:1], *near(got[1:]), rest, *near(swapped[1:]), merged, *near((beside, above, corner)))
    keep, give, grads, x_full, up_full = call(
        functools.partial(head_kernel, n),
        [
            ((n, half, width), BF),
            ((n, half, width), BF),
            ((patches, 4 * SLOT), BF),
            ((patches, width), BF),
            ((patches, width), BF),
        ],
        args,
        [
            pltpu.VMEM((width, 4 * SLOT), BF),
            pltpu.VMEM((patches, SLOT), F32),
            pltpu.VMEM((patches, SLOT), F32),
            pltpu.SemaphoreType.DMA((n, 2, 2)),
            pltpu.SemaphoreType.DMA((4, n)),
        ],
        [ANY_SPEC] * len(args),
    )
    taken = swap(give, "pipe")
    sums = call(functools.partial(sum_kernel, n), [((half, width), BF)] * n, (keep, *near([taken])))
    parts = [sums[0]] + [across(sums[k], k) for k in range(1, n)]
    factor = 1.0 / math.sqrt(patches * lax.axis_size("dp"))
    w_keep, w_give = call(
        functools.partial(weight_kernel, n, factor),
        [((n, share, 4 * SLOT), BF)] * 2,
        (x_full, up_full, grads),
        [pltpu.VMEM((width, 4 * SLOT), BF)],
    )
    w_taken = swap(w_give, "dp")
    w_sums = call(
        functools.partial(sum_kernel, n), [((share, 4 * SLOT), BF)] * n, (w_keep, *near([w_taken]))
    )
    w_parts = [w_sums[0]] + [across(w_sums[k], k) for k in range(1, n)]
    mine = call(functools.partial(final_kernel, n), ((half, width), BF), (x, up, parts[0], *near(parts[1:])))
    input_gradient = call(join_kernel, ((rows, width), BF), (mine, *near([swap(mine, "pipe")])))
    weight_grads = call(
        functools.partial(unpack_kernel, n),
        ((4, share, n * HD), F32),
        (w_parts[0], *near(w_parts[1:])),
        [pltpu.VMEM((n, share, 4 * SLOT), BF)],
    )
    return (input_gradient[None], weight_grads)


def local_gathered(embeddings, upstream, attn_weights):
    tokens = embeddings[0]
    row_gradients = upstream[0]
    row_count = tokens.shape[0]
    weights = lax.all_gather(attn_weights, ("seq", "dp"), axis=1, tiled=True)
    local_width = weights.shape[2]
    head_count = local_width // HD
    score_scale = HD ** (-0.5)
    standardized_input, inverse_deviation = standardize(tokens.astype(F32))
    normalized_rows = standardized_input.astype(BF)
    proj = jnp.einsum(
        "td,cdh->cth", normalized_rows, weights[:3], preferred_element_type=F32
    ).astype(BF)
    gathered = lax.all_gather(proj[1:], "seq", axis=1, tiled=True)
    key_count = gathered.shape[1]
    query_heads = proj[0].reshape(row_count, head_count, HD).transpose(1, 0, 2)
    key_heads = gathered[0].reshape(key_count, head_count, HD).transpose(1, 0, 2)
    value_heads = gathered[1].reshape(key_count, head_count, HD).transpose(1, 0, 2)
    grad_att = jnp.dot(row_gradients, weights[3], preferred_element_type=F32).astype(BF)
    grad_heads = grad_att.reshape(row_count, head_count, HD).transpose(1, 0, 2)

    def one_head(items):
        query_rows, key_rows, value_rows, grad_out = items
        scores = nn(query_rows, key_rows.T) * score_scale
        row_max = jnp.max(scores, axis=1, keepdims=True)
        log_total = row_max + jnp.log(jnp.sum(jnp.exp(scores - row_max), axis=1, keepdims=True))
        probs = jnp.exp(scores - log_total).astype(BF)
        attended = nn(probs, value_rows).astype(BF)
        row_delta = jnp.sum(
            grad_out.astype(F32) * attended.astype(F32), axis=1, keepdims=True
        )
        dprobs = nn(grad_out, value_rows.T)
        dscores = (probs.astype(F32) * (dprobs - row_delta) * score_scale).astype(BF)
        grad_q = nn(dscores, key_rows).astype(BF)
        return (attended, grad_q, nn(dscores.T, query_rows), nn(probs.T, grad_out))

    attended_h, grad_q_h, key_h, value_h = lax.map(
        one_head, (query_heads, key_heads, value_heads, grad_heads)
    )
    attended_flat = attended_h.transpose(1, 0, 2).reshape(row_count, local_width)
    grad_q = grad_q_h.transpose(1, 0, 2).reshape(1, row_count, local_width)
    key_terms = key_h.transpose(1, 0, 2).reshape(key_count, local_width)
    value_terms = value_h.transpose(1, 0, 2).reshape(key_count, local_width)
    both_terms = jnp.stack([key_terms, value_terms])
    owned = lax.psum_scatter(both_terms.astype(BF), "seq", scatter_dimension=1, tiled=True)
    grad_qkv = jnp.concatenate([grad_q, owned], axis=0)
    token_count = row_count * lax.axis_size("seq") * lax.axis_size("dp")
    grad_factor = 1.0 / math.sqrt(token_count)
    terms_qkv = jnp.einsum("td,cth->cdh", normalized_rows, grad_qkv, preferred_element_type=F32)
    term_out = jnp.einsum("td,th->dh", row_gradients, attended_flat, preferred_element_type=F32)
    terms = jnp.concatenate([terms_qkv, term_out[None]], axis=0) * grad_factor
    seq_summed = lax.psum_scatter(terms.astype(BF), "seq", scatter_dimension=1, tiled=True)
    weight_grads = lax.psum_scatter(seq_summed, "dp", scatter_dimension=1, tiled=True).astype(F32)
    input_part = jnp.einsum("cth,cdh->td", grad_qkv, weights[:3], preferred_element_type=F32)
    reduced_total = lax.psum(input_part.astype(BF), "pipe").astype(F32)
    leading_term = jnp.mean(reduced_total, axis=1, keepdims=True)
    trailing_term = jnp.mean(reduced_total * standardized_input, axis=1, keepdims=True)
    input_gradient = (
        row_gradients.astype(F32)
        + inverse_deviation * (reduced_total - leading_term - standardized_input * trailing_term)
    ).astype(BF)
    return (input_gradient[None], weight_grads)


def local(embeddings, upstream, attn_weights):
    n = lax.axis_size("seq")
    heads = attn_weights.shape[2] // HD
    one_head_each = (
        heads == n
        and n == 4
        and lax.axis_size("grp") == 2
        and lax.axis_size("dp") == 2
        and lax.axis_size("pipe") == 2
        and attn_weights.shape[1] % 16 == 0
        and embeddings.shape[0] == 1
        and embeddings.shape[1] % 32 == 0
    )
    return (local_heads if one_head_each else local_gathered)(embeddings, upstream, attn_weights)


def solution(mesh):
    in_specs = (
        P(("grp", "dp"), "seq", None),
        P(("grp", "dp"), "seq", None),
        P(None, ("seq", "dp"), "pipe"),
    )
    out_specs = (P(("grp", "dp"), "seq", None), P("grp", ("seq", "dp"), "pipe"))
    return jax.shard_map(local, mesh=mesh, in_specs=in_specs, out_specs=out_specs, check_vma=False)
```

```python
import functools
import math

import jax
import jax.numpy as jnp
from jax import lax
from jax.experimental import pallas as pl
from jax.experimental.pallas import tpu as pltpu
from jax.sharding import PartitionSpec as P

HD = 104
SLOT = 128

EPSILON = 1e-06
BF = jnp.bfloat16
F32 = jnp.float32
PARAMS = pltpu.CompilerParams(vmem_limit_bytes=24 * 1024 * 1024)
VMEM_SPEC = pl.BlockSpec(memory_space=pltpu.VMEM)
ANY_SPEC = pl.BlockSpec(memory_space=pl.ANY)


def standardize(features):
    row_mean = jnp.mean(features, axis=1, keepdims=True)
    mean_removed = features - row_mean
    variance = jnp.mean(mean_removed * mean_removed, axis=1, keepdims=True)
    inverse_deviation = lax.rsqrt(variance + EPSILON)
    return mean_removed * inverse_deviation, inverse_deviation


def nt(a, b):
    return lax.dot_general(a, b, (((1,), (1,)), ((), ())), preferred_element_type=F32)


def tn(a, b):
    return lax.dot_general(a, b, (((0,), (0,)), ((), ())), preferred_element_type=F32)


def nn(a, b):
    return jnp.dot(a, b, preferred_element_type=F32)


def pack_kernel(n, w_ref, *refs):
    outs, staged = refs[:n], refs[n]
    me = lax.axis_index("seq")
    group = lax.axis_index("grp")
    rows = w_ref.shape[1]
    fill = jnp.zeros((rows, SLOT - HD), BF)
    for head in range(n):
        for mat in range(4):
            block = w_ref[mat, :, head * HD : (head + 1) * HD]
            first = (mat % 2) * SLOT
            staged[mat // 2, head, :, first : first + SLOT] = jnp.concatenate(
                [block, fill], axis=1
            )
    for k in range(n):
        outs[k][...] = staged[group, me ^ k]


def norm_kernel(x_ref, up_ref, send_ref, rest_ref, staged):
    core = lax.axis_index("pipe")
    half = x_ref.shape[0] // 2
    staged[...] = standardize(x_ref[...].astype(F32))[0].astype(BF)
    for target, at in ((send_ref, core), (rest_ref, 1 - core)):
        span = pl.ds(pl.multiple_of(at * half, half), half)
        target[:half] = staged[span, :]
        target[half:] = up_ref[span, :]


def merge_kernel(*refs):
    share = refs[0].shape[0]
    for k, ref in enumerate(refs[:-1]):
        refs[-1][k * share : (k + 1) * share] = ref[...]


def head_kernel(n, factor, *refs):
    got, swapped = refs[:n], refs[n : 2 * n]
    pieces = refs[2 * n : 2 * n + 4]
    keep_ref, give_ref, w_keep_ref, w_give_ref = refs[2 * n + 4 : 2 * n + 8]
    x_full, up_full, w_full, grads, staged, term_k, term_v, sems, wsems = refs[2 * n + 8 :]
    me = lax.axis_index("seq")
    image = lax.axis_index("dp")
    group = lax.axis_index("grp")
    rows = got[0].shape[0]
    half = rows // 2
    share = pieces[0].shape[0] // n

    copies = []
    for which, source in enumerate(pieces):
        at = 1 - image if which % 2 else image
        mats = 1 - group if which // 2 else group
        for k in range(n):
            first = pl.multiple_of(((me ^ k) * 2 + at) * share, 16)
            lanes = pl.multiple_of(mats * 2 * SLOT, 2 * SLOT)
            copies.append(
                pltpu.make_async_copy(
                    source.at[pl.ds(k * share, share), :],
                    w_full.at[pl.ds(first, share), pl.ds(lanes, 2 * SLOT)],
                    wsems.at[which, k],
                )
            )
    for k in range(n):
        for side, source in enumerate((got[k], swapped[k])):
            for which, target in enumerate((x_full, up_full)):
                copies.append(
                    pltpu.make_async_copy(
                        source.at[pl.ds(which * half, half), :],
                        target.at[pl.ds(k * rows + side * half, half), :],
                        sems.at[k, side, which],
                    )
                )
    for copy in copies:
        copy.start()
    for copy in copies:
        copy.wait()

    scale = HD ** (-0.5)
    qkv = nn(x_full[...], w_full[:, : 3 * SLOT]).astype(BF)
    grad_att = nn(up_full[...], w_full[:, 3 * SLOT :]).astype(BF)
    key_rows = qkv[:, SLOT : 2 * SLOT]
    value_rows = qkv[:, 2 * SLOT :]
    for b in range(n):
        span = slice(b * rows, (b + 1) * rows)
        query = qkv[span, :SLOT]
        grad_out = grad_att[span]
        scores = nt(query, key_rows) * scale
        weight = jnp.exp(scores - jnp.max(scores, axis=1, keepdims=True))
        probs = (weight / jnp.sum(weight, axis=1, keepdims=True)).astype(BF)
        attended = nn(probs, value_rows).astype(BF)
        delta = jnp.sum(grad_out.astype(F32) * attended.astype(F32), axis=1, keepdims=True)
        dprobs = nt(grad_out, value_rows)
        dscores = (probs.astype(F32) * (dprobs - delta) * scale).astype(BF)
        grads[span, :SLOT] = nn(dscores, key_rows).astype(BF)
        grads[span, 3 * SLOT :] = attended
        key_term = tn(dscores, query).astype(BF).astype(F32)
        value_term = tn(probs, grad_out).astype(BF).astype(F32)
        if b == 0:
            term_k[...] = key_term
            term_v[...] = value_term
        else:
            term_k[...] += key_term
            term_v[...] += value_term
    grads[:, SLOT : 2 * SLOT] = term_k[...].astype(BF)
    grads[:, 2 * SLOT : 3 * SLOT] = term_v[...].astype(BF)
    for b in range(n):
        span = slice(b * rows, (b + 1) * rows)
        part = nt(grads[span, : 3 * SLOT], w_full[:, : 3 * SLOT]).astype(BF)
        keep_ref[b] = part[:half]
        give_ref[b] = part[half:]
    staged[:, : 3 * SLOT] = (tn(x_full[...], grads[:, : 3 * SLOT]) * factor).astype(BF)
    staged[:, 3 * SLOT :] = (tn(up_full[...], grads[:, 3 * SLOT :]) * factor).astype(BF)
    for k in range(n):
        for target, at in ((w_keep_ref, image), (w_give_ref, 1 - image)):
            first = pl.multiple_of(((me ^ k) * 2 + at) * share, 16)
            target[k] = staged[pl.ds(first, share), :]


def sum_kernel(n, mine_ref, theirs_ref, *outs):
    for k in range(n):
        outs[k][...] = (mine_ref[k].astype(F32) + theirs_ref[k].astype(F32)).astype(BF)


def final_kernel(n, x_ref, up_ref, *refs):
    parts, out_ref = refs[:n], refs[n]
    half = out_ref.shape[0]
    core = lax.axis_index("pipe")
    span = pl.ds(pl.multiple_of(core * half, half), half)
    total = parts[0][...].astype(F32)
    for part in parts[1:]:
        total += part[...].astype(F32)
    xhat, inverse_deviation = standardize(x_ref[span, :].astype(F32))
    leading = jnp.mean(total, axis=1, keepdims=True)
    trailing = jnp.mean(total * xhat, axis=1, keepdims=True)
    out_ref[...] = (
        up_ref[span, :].astype(F32) + inverse_deviation * (total - leading - xhat * trailing)
    ).astype(BF)


def join_kernel(n, mine_ref, theirs_ref, *refs):
    parts, (input_ref, out_ref, staged) = refs[:n], refs[n:]
    me = lax.axis_index("seq")
    core = lax.axis_index("pipe")
    half = mine_ref.shape[0]
    input_ref[pl.ds(pl.multiple_of(core * half, half), half), :] = mine_ref[...]
    input_ref[pl.ds(pl.multiple_of((1 - core) * half, half), half), :] = theirs_ref[...]
    for k in range(n):
        staged[me ^ k] = parts[k][...]
    for head in range(n):
        for mat in range(4):
            out_ref[mat, :, head * HD : (head + 1) * HD] = staged[
                head, :, mat * SLOT : mat * SLOT + HD
            ].astype(F32)


def call(kernel, out_shape, args, scratch=(), plain=0, out_space=pltpu.VMEM):
    single = not isinstance(out_shape, list)
    shapes = [out_shape] if single else out_shape
    args = list(args[:plain]) + [
        pltpu.with_memory_space_constraint(a, pltpu.VMEM) for a in args[plain:]
    ]
    out = pl.pallas_call(
        kernel,
        out_shape=[out_space(*s) for s in shapes],
        in_specs=[VMEM_SPEC] * len(args),
        out_specs=[VMEM_SPEC] * len(shapes),
        scratch_shapes=list(scratch),
        compiler_params=PARAMS,
    )(*args)
    return out[0] if single else list(out)


def local_heads(embeddings, upstream, attn_weights):
    n = lax.axis_size("seq")
    x, up = embeddings[0], upstream[0]
    rows, width = x.shape
    share = attn_weights.shape[1]
    patches = n * rows
    half = rows // 2
    me = lax.axis_index("seq")

    def across(value, k):
        return lax.ppermute(value, "seq", [(i, i ^ k) for i in range(n)])

    def swap(value, axis):
        return lax.ppermute(value, axis, [(0, 1), (1, 0)])


    chunks = call(
        functools.partial(pack_kernel, n),
        [((share, 2 * SLOT), BF)] * n,
        (attn_weights,),
        [pltpu.VMEM((2, n, share, 2 * SLOT), BF)],
        plain=1,
    )
    arrived = [across(chunks[k], k) for k in range(1, n)]
    send, rest = call(
        norm_kernel, [((rows, width), BF)] * 2, (x, up), [pltpu.VMEM((rows, width), BF)], plain=2
    )
    send, *arrived = lax.optimization_barrier((send, *arrived))
    merged = call(merge_kernel, ((n * share, 2 * SLOT), BF), (chunks[0], *arrived))
    beside = swap(merged, "dp")
    above = swap(merged, "grp")
    second = across(send, 2)
    first = across(send, 1)
    later, second, beside, above = lax.optimization_barrier((send, second, beside, above))
    corner = swap(above, "dp")
    middle = lax.ppermute(later, "seq", [(1, 2), (2, 1)])
    passed = lax.ppermute(second, "seq", [(2, 3), (1, 0)])
    third = jnp.where((me == 0) | (me == n - 1), passed, middle)
    got = [send, first, second, third]
    swapped = [rest] + [swap(g, "pipe") for g in got[1:]]
    args = (*got, *swapped, merged, beside, above, corner)
    factor = 1.0 / math.sqrt(patches * lax.axis_size("dp"))
    keep, give, w_keep, w_give = call(
        functools.partial(head_kernel, n, factor),
        [((n, half, width), BF)] * 2 + [((n, share, 4 * SLOT), BF)] * 2,
        args,
        [
            pltpu.VMEM((patches, width), BF),
            pltpu.VMEM((patches, width), BF),
            pltpu.VMEM((width, 4 * SLOT), BF),
            pltpu.VMEM((patches, 4 * SLOT), BF),
            pltpu.VMEM((width, 4 * SLOT), BF),
            pltpu.VMEM((patches, SLOT), F32),
            pltpu.VMEM((patches, SLOT), F32),
            pltpu.SemaphoreType.DMA((n, 2, 2)),
            pltpu.SemaphoreType.DMA((4, n)),
        ],
    )
    taken = swap(give, "pipe")
    w_taken = swap(w_give, "dp")
    sums = call(functools.partial(sum_kernel, n), [((half, width), BF)] * n, (keep, taken))
    parts = [across(sums[k], k) for k in range(1, n)]
    w_taken, sums[0] = lax.optimization_barrier((w_taken, sums[0]))
    w_sums = call(
        functools.partial(sum_kernel, n), [((share, 4 * SLOT), BF)] * n, (w_keep, w_taken)
    )
    w_parts = [w_sums[0]] + [across(w_sums[k], k) for k in range(1, n)]
    mine = call(functools.partial(final_kernel, n), ((half, width), BF), (x, up, sums[0], *parts), plain=2)
    input_gradient, weight_grads = call(
        functools.partial(join_kernel, n),
        [((rows, width), BF), ((4, share, n * HD), F32)],
        (mine, swap(mine, "pipe"), *w_parts),
        [pltpu.VMEM((n, share, 4 * SLOT), BF)],
        out_space=jax.ShapeDtypeStruct,
    )
    return (input_gradient[None], weight_grads)


def local_gathered(embeddings, upstream, attn_weights):
    tokens = embeddings[0]
    row_gradients = upstream[0]
    row_count = tokens.shape[0]
    weights = lax.all_gather(attn_weights, ("seq", "dp"), axis=1, tiled=True)
    local_width = weights.shape[2]
    head_count = local_width // HD
    score_scale = HD ** (-0.5)
    standardized_input, inverse_deviation = standardize(tokens.astype(F32))
    normalized_rows = standardized_input.astype(BF)
    proj = jnp.einsum(
        "td,cdh->cth", normalized_rows, weights[:3], preferred_element_type=F32
    ).astype(BF)
    gathered = lax.all_gather(proj[1:], "seq", axis=1, tiled=True)
    key_count = gathered.shape[1]
    query_heads = proj[0].reshape(row_count, head_count, HD).transpose(1, 0, 2)
    key_heads = gathered[0].reshape(key_count, head_count, HD).transpose(1, 0, 2)
    value_heads = gathered[1].reshape(key_count, head_count, HD).transpose(1, 0, 2)
    grad_att = jnp.dot(row_gradients, weights[3], preferred_element_type=F32).astype(BF)
    grad_heads = grad_att.reshape(row_count, head_count, HD).transpose(1, 0, 2)

    def one_head(items):
        query_rows, key_rows, value_rows, grad_out = items
        scores = nn(query_rows, key_rows.T) * score_scale
        row_max = jnp.max(scores, axis=1, keepdims=True)
        log_total = row_max + jnp.log(jnp.sum(jnp.exp(scores - row_max), axis=1, keepdims=True))
        probs = jnp.exp(scores - log_total).astype(BF)
        attended = nn(probs, value_rows).astype(BF)
        row_delta = jnp.sum(
            grad_out.astype(F32) * attended.astype(F32), axis=1, keepdims=True
        )
        dprobs = nn(grad_out, value_rows.T)
        dscores = (probs.astype(F32) * (dprobs - row_delta) * score_scale).astype(BF)
        grad_q = nn(dscores, key_rows).astype(BF)
        return (attended, grad_q, nn(dscores.T, query_rows), nn(probs.T, grad_out))

    attended_h, grad_q_h, key_h, value_h = lax.map(
        one_head, (query_heads, key_heads, value_heads, grad_heads)
    )
    attended_flat = attended_h.transpose(1, 0, 2).reshape(row_count, local_width)
    grad_q = grad_q_h.transpose(1, 0, 2).reshape(1, row_count, local_width)
    key_terms = key_h.transpose(1, 0, 2).reshape(key_count, local_width)
    value_terms = value_h.transpose(1, 0, 2).reshape(key_count, local_width)
    both_terms = jnp.stack([key_terms, value_terms])
    owned = lax.psum_scatter(both_terms.astype(BF), "seq", scatter_dimension=1, tiled=True)
    grad_qkv = jnp.concatenate([grad_q, owned], axis=0)
    token_count = row_count * lax.axis_size("seq") * lax.axis_size("dp")
    grad_factor = 1.0 / math.sqrt(token_count)
    terms_qkv = jnp.einsum("td,cth->cdh", normalized_rows, grad_qkv, preferred_element_type=F32)
    term_out = jnp.einsum("td,th->dh", row_gradients, attended_flat, preferred_element_type=F32)
    terms = jnp.concatenate([terms_qkv, term_out[None]], axis=0) * grad_factor
    seq_summed = lax.psum_scatter(terms.astype(BF), "seq", scatter_dimension=1, tiled=True)
    weight_grads = lax.psum_scatter(seq_summed, "dp", scatter_dimension=1, tiled=True).astype(F32)
    input_part = jnp.einsum("cth,cdh->td", grad_qkv, weights[:3], preferred_element_type=F32)
    reduced_total = lax.psum(input_part.astype(BF), "pipe").astype(F32)
    leading_term = jnp.mean(reduced_total, axis=1, keepdims=True)
    trailing_term = jnp.mean(reduced_total * standardized_input, axis=1, keepdims=True)
    input_gradient = (
        row_gradients.astype(F32)
        + inverse_deviation * (reduced_total - leading_term - standardized_input * trailing_term)
    ).astype(BF)
    return (input_gradient[None], weight_grads)


def local(embeddings, upstream, attn_weights):
    n = lax.axis_size("seq")
    heads = attn_weights.shape[2] // HD
    one_head_each = (
        heads == n
        and n == 4
        and lax.axis_size("grp") == 2
        and lax.axis_size("dp") == 2
        and lax.axis_size("pipe") == 2
        and attn_weights.shape[1] % 16 == 0
        and embeddings.shape[0] == 1
        and embeddings.shape[1] % 32 == 0
    )
    return (local_heads if one_head_each else local_gathered)(embeddings, upstream, attn_weights)


def solution(mesh):
    in_specs = (
        P(("grp", "dp"), "seq", None),
        P(("grp", "dp"), "seq", None),
        P(None, ("seq", "dp"), "pipe"),
    )
    out_specs = (P(("grp", "dp"), "seq", None), P("grp", ("seq", "dp"), "pipe"))
    return jax.shard_map(local, mesh=mesh, in_specs=in_specs, out_specs=out_specs, check_vma=False)
```

```python
import functools
import math

import jax
import jax.numpy as jnp
from jax import lax
from jax.experimental import pallas as pl
from jax.experimental.pallas import tpu as pltpu
from jax.sharding import PartitionSpec as P

HD = 104
SLOT = 128

EPSILON = 1e-06
BF = jnp.bfloat16
F32 = jnp.float32
PARAMS = pltpu.CompilerParams(vmem_limit_bytes=24 * 1024 * 1024)
VMEM_SPEC = pl.BlockSpec(memory_space=pltpu.VMEM)
ANY_SPEC = pl.BlockSpec(memory_space=pl.ANY)


def standardize(features):
    row_mean = jnp.mean(features, axis=1, keepdims=True)
    mean_removed = features - row_mean
    variance = jnp.mean(mean_removed * mean_removed, axis=1, keepdims=True)
    inverse_deviation = lax.rsqrt(variance + EPSILON)
    return mean_removed * inverse_deviation, inverse_deviation


def nt(a, b):
    return lax.dot_general(a, b, (((1,), (1,)), ((), ())), preferred_element_type=F32)


def tn(a, b):
    return lax.dot_general(a, b, (((0,), (0,)), ((), ())), preferred_element_type=F32)


def nn(a, b):
    return jnp.dot(a, b, preferred_element_type=F32)


def pack_kernel(n, w_ref, *refs):
    outs, staged = refs[:n], refs[n]
    me = lax.axis_index("seq")
    group = lax.axis_index("grp")
    rows = w_ref.shape[1]
    fill = jnp.zeros((rows, SLOT - HD), BF)
    for head in range(n):
        for mat in range(4):
            block = w_ref[mat, :, head * HD : (head + 1) * HD]
            first = (mat % 2) * SLOT
            staged[mat // 2, head, :, first : first + SLOT] = jnp.concatenate(
                [block, fill], axis=1
            )
    for k in range(n):
        outs[k][...] = staged[group, me ^ k]


def norm_kernel(x_ref, up_ref, send_ref, rest_ref, staged):
    core = lax.axis_index("pipe")
    half = x_ref.shape[0] // 2
    staged[...] = standardize(x_ref[...].astype(F32))[0].astype(BF)
    for target, at in ((send_ref, core), (rest_ref, 1 - core)):
        span = pl.ds(pl.multiple_of(at * half, half), half)
        target[:half] = staged[span, :]
        target[half:] = up_ref[span, :]


def merge_kernel(*refs):
    share = refs[0].shape[0]
    for k, ref in enumerate(refs[:-1]):
        refs[-1][k * share : (k + 1) * share] = ref[...]


def head_kernel(n, factor, *refs):
    blocks = [(refs[2 * k], refs[2 * k + 1]) for k in range(n + 1)]
    pieces = refs[2 * n + 2 : 2 * n + 6]
    keep_ref, give_ref, w_keep_ref, w_give_ref = refs[2 * n + 6 : 2 * n + 10]
    x_full, up_full, w_full, grads, staged, term_k, term_v = refs[2 * n + 10 :]
    me = lax.axis_index("seq")
    image = lax.axis_index("dp")
    group = lax.axis_index("grp")
    rows = blocks[0][0].shape[0]
    half = rows // 2
    share = pieces[0].shape[0] // n

    for which, source in enumerate(pieces):
        at = 1 - image if which % 2 else image
        mats = 1 - group if which // 2 else group
        for k in range(n):
            first = pl.multiple_of(((me ^ k) * 2 + at) * share, 16)
            lanes = pl.multiple_of(mats * 2 * SLOT, 2 * SLOT)
            w_full[pl.ds(first, share), pl.ds(lanes, 2 * SLOT)] = source[
                k * share : (k + 1) * share, :
            ]

    def place(k, sides):
        for side, source in enumerate(sides):
            span = slice(k * rows + side * half, k * rows + (side + 1) * half)
            x_full[span, :] = source[:half, :]
            up_full[span, :] = source[half:, :]

    for k in range(n - 1):
        place(k, blocks[k])

    @pl.when((me == 0) | (me == n - 1))
    def _():
        place(n - 1, blocks[n])

    @pl.when((me != 0) & (me != n - 1))
    def _():
        place(n - 1, blocks[n - 1])

    scale = HD ** (-0.5)
    qkv = nn(x_full[...], w_full[:, : 3 * SLOT]).astype(BF)
    grad_att = nn(up_full[...], w_full[:, 3 * SLOT :]).astype(BF)
    key_rows = qkv[:, SLOT : 2 * SLOT]
    value_rows = qkv[:, 2 * SLOT :]
    for b in range(n):
        span = slice(b * rows, (b + 1) * rows)
        query = qkv[span, :SLOT]
        grad_out = grad_att[span]
        scores = nt(query, key_rows) * scale
        weight = jnp.exp(scores - jnp.max(scores, axis=1, keepdims=True))
        probs = (weight / jnp.sum(weight, axis=1, keepdims=True)).astype(BF)
        attended = nn(probs, value_rows).astype(BF)
        delta = jnp.sum(grad_out.astype(F32) * attended.astype(F32), axis=1, keepdims=True)
        dprobs = nt(grad_out, value_rows)
        dscores = (probs.astype(F32) * (dprobs - delta) * scale).astype(BF)
        grads[span, :SLOT] = nn(dscores, key_rows).astype(BF)
        grads[span, 3 * SLOT :] = attended
        key_term = tn(dscores, query).astype(BF).astype(F32)
        value_term = tn(probs, grad_out).astype(BF).astype(F32)
        if b == 0:
            term_k[...] = key_term
            term_v[...] = value_term
        else:
            term_k[...] += key_term
            term_v[...] += value_term
    grads[:, SLOT : 2 * SLOT] = term_k[...].astype(BF)
    grads[:, 2 * SLOT : 3 * SLOT] = term_v[...].astype(BF)
    for b in range(n):
        span = slice(b * rows, (b + 1) * rows)
        part = nt(grads[span, : 3 * SLOT], w_full[:, : 3 * SLOT]).astype(BF)
        keep_ref[b] = part[:half]
        give_ref[b] = part[half:]
    staged[:, : 3 * SLOT] = (tn(x_full[...], grads[:, : 3 * SLOT]) * factor).astype(BF)
    staged[:, 3 * SLOT :] = (tn(up_full[...], grads[:, 3 * SLOT :]) * factor).astype(BF)
    for k in range(n):
        for target, at in ((w_keep_ref, image), (w_give_ref, 1 - image)):
            first = pl.multiple_of(((me ^ k) * 2 + at) * share, 16)
            target[k] = staged[pl.ds(first, share), :]


def sum_kernel(n, mine_ref, theirs_ref, *outs):
    for k in range(n):
        outs[k][...] = (mine_ref[k].astype(F32) + theirs_ref[k].astype(F32)).astype(BF)


def final_kernel(n, x_ref, up_ref, *refs):
    parts, out_ref = refs[:n], refs[n]
    half = out_ref.shape[0]
    core = lax.axis_index("pipe")
    span = pl.ds(pl.multiple_of(core * half, half), half)
    total = parts[0][...].astype(F32)
    for part in parts[1:]:
        total += part[...].astype(F32)
    xhat, inverse_deviation = standardize(x_ref[span, :].astype(F32))
    leading = jnp.mean(total, axis=1, keepdims=True)
    trailing = jnp.mean(total * xhat, axis=1, keepdims=True)
    out_ref[...] = (
        up_ref[span, :].astype(F32) + inverse_deviation * (total - leading - xhat * trailing)
    ).astype(BF)


def join_kernel(n, mine_ref, theirs_ref, *refs):
    parts, (input_ref, out_ref, staged) = refs[:n], refs[n:]
    me = lax.axis_index("seq")
    core = lax.axis_index("pipe")
    half = mine_ref.shape[0]
    input_ref[pl.ds(pl.multiple_of(core * half, half), half), :] = mine_ref[...]
    input_ref[pl.ds(pl.multiple_of((1 - core) * half, half), half), :] = theirs_ref[...]
    for k in range(n):
        staged[me ^ k] = parts[k][...]
    for head in range(n):
        for mat in range(4):
            out_ref[mat, :, head * HD : (head + 1) * HD] = staged[
                head, :, mat * SLOT : mat * SLOT + HD
            ].astype(F32)


def call(kernel, out_shape, args, scratch=(), plain=0, out_space=pltpu.VMEM):
    single = not isinstance(out_shape, list)
    shapes = [out_shape] if single else out_shape
    args = list(args[:plain]) + [
        pltpu.with_memory_space_constraint(a, pltpu.VMEM) for a in args[plain:]
    ]
    out = pl.pallas_call(
        kernel,
        out_shape=[out_space(*s) for s in shapes],
        in_specs=[VMEM_SPEC] * len(args),
        out_specs=[VMEM_SPEC] * len(shapes),
        scratch_shapes=list(scratch),
        compiler_params=PARAMS,
    )(*args)
    return out[0] if single else list(out)


def local_heads(embeddings, upstream, attn_weights):
    n = lax.axis_size("seq")
    x, up = embeddings[0], upstream[0]
    rows, width = x.shape
    share = attn_weights.shape[1]
    patches = n * rows
    half = rows // 2
    me = lax.axis_index("seq")

    def across(value, k):
        return lax.ppermute(value, "seq", [(i, i ^ k) for i in range(n)])

    def swap(value, axis):
        return lax.ppermute(value, axis, [(0, 1), (1, 0)])


    chunks = call(
        functools.partial(pack_kernel, n),
        [((share, 2 * SLOT), BF)] * n,
        (attn_weights,),
        [pltpu.VMEM((2, n, share, 2 * SLOT), BF)],
        plain=1,
    )
    arrived = [across(chunks[k], k) for k in range(1, n)]
    send, rest = call(
        norm_kernel, [((rows, width), BF)] * 2, (x, up), [pltpu.VMEM((rows, width), BF)], plain=2
    )
    merged = call(merge_kernel, ((n * share, 2 * SLOT), BF), (chunks[0], *arrived))
    beside = swap(merged, "dp")
    above = swap(merged, "grp")
    second = across(send, 2)
    first = across(send, 1)
    later, second, beside, above = lax.optimization_barrier((send, second, beside, above))
    corner = swap(above, "dp")
    middle = lax.ppermute(later, "seq", [(1, 2), (2, 1)])
    passed = lax.ppermute(second, "seq", [(2, 3), (1, 0)])
    args = [send, rest]
    for block in (first, second, middle, passed):
        args += [block, swap(block, "pipe")]
    args += [merged, beside, above, corner]
    factor = 1.0 / math.sqrt(patches * lax.axis_size("dp"))
    keep, give, w_keep, w_give = call(
        functools.partial(head_kernel, n, factor),
        [((n, half, width), BF)] * 2 + [((n, share, 4 * SLOT), BF)] * 2,
        args,
        [
            pltpu.VMEM((patches, width), BF),
            pltpu.VMEM((patches, width), BF),
            pltpu.VMEM((width, 4 * SLOT), BF),
            pltpu.VMEM((patches, 4 * SLOT), BF),
            pltpu.VMEM((width, 4 * SLOT), BF),
            pltpu.VMEM((patches, SLOT), F32),
            pltpu.VMEM((patches, SLOT), F32),
        ],
    )
    taken = swap(give, "pipe")
    w_taken = swap(w_give, "dp")
    sums = call(functools.partial(sum_kernel, n), [((half, width), BF)] * n, (keep, taken))
    parts = [across(sums[k], k) for k in range(1, n)]
    w_taken, sums[0] = lax.optimization_barrier((w_taken, sums[0]))
    w_sums = call(
        functools.partial(sum_kernel, n), [((share, 4 * SLOT), BF)] * n, (w_keep, w_taken)
    )
    w_parts = [w_sums[0]] + [across(w_sums[k], k) for k in range(1, n)]
    mine = call(functools.partial(final_kernel, n), ((half, width), BF), (x, up, sums[0], *parts), plain=2)
    input_gradient, weight_grads = call(
        functools.partial(join_kernel, n),
        [((rows, width), BF), ((4, share, n * HD), F32)],
        (mine, swap(mine, "pipe"), *w_parts),
        [pltpu.VMEM((n, share, 4 * SLOT), BF)],
        out_space=jax.ShapeDtypeStruct,
    )
    return (input_gradient[None], weight_grads)


def local_gathered(embeddings, upstream, attn_weights):
    tokens = embeddings[0]
    row_gradients = upstream[0]
    row_count = tokens.shape[0]
    weights = lax.all_gather(attn_weights, ("seq", "dp"), axis=1, tiled=True)
    local_width = weights.shape[2]
    head_count = local_width // HD
    score_scale = HD ** (-0.5)
    standardized_input, inverse_deviation = standardize(tokens.astype(F32))
    normalized_rows = standardized_input.astype(BF)
    proj = jnp.einsum(
        "td,cdh->cth", normalized_rows, weights[:3], preferred_element_type=F32
    ).astype(BF)
    gathered = lax.all_gather(proj[1:], "seq", axis=1, tiled=True)
    key_count = gathered.shape[1]
    query_heads = proj[0].reshape(row_count, head_count, HD).transpose(1, 0, 2)
    key_heads = gathered[0].reshape(key_count, head_count, HD).transpose(1, 0, 2)
    value_heads = gathered[1].reshape(key_count, head_count, HD).transpose(1, 0, 2)
    grad_att = jnp.dot(row_gradients, weights[3], preferred_element_type=F32).astype(BF)
    grad_heads = grad_att.reshape(row_count, head_count, HD).transpose(1, 0, 2)

    def one_head(items):
        query_rows, key_rows, value_rows, grad_out = items
        scores = nn(query_rows, key_rows.T) * score_scale
        row_max = jnp.max(scores, axis=1, keepdims=True)
        log_total = row_max + jnp.log(jnp.sum(jnp.exp(scores - row_max), axis=1, keepdims=True))
        probs = jnp.exp(scores - log_total).astype(BF)
        attended = nn(probs, value_rows).astype(BF)
        row_delta = jnp.sum(
            grad_out.astype(F32) * attended.astype(F32), axis=1, keepdims=True
        )
        dprobs = nn(grad_out, value_rows.T)
        dscores = (probs.astype(F32) * (dprobs - row_delta) * score_scale).astype(BF)
        grad_q = nn(dscores, key_rows).astype(BF)
        return (attended, grad_q, nn(dscores.T, query_rows), nn(probs.T, grad_out))

    attended_h, grad_q_h, key_h, value_h = lax.map(
        one_head, (query_heads, key_heads, value_heads, grad_heads)
    )
    attended_flat = attended_h.transpose(1, 0, 2).reshape(row_count, local_width)
    grad_q = grad_q_h.transpose(1, 0, 2).reshape(1, row_count, local_width)
    key_terms = key_h.transpose(1, 0, 2).reshape(key_count, local_width)
    value_terms = value_h.transpose(1, 0, 2).reshape(key_count, local_width)
    both_terms = jnp.stack([key_terms, value_terms])
    owned = lax.psum_scatter(both_terms.astype(BF), "seq", scatter_dimension=1, tiled=True)
    grad_qkv = jnp.concatenate([grad_q, owned], axis=0)
    token_count = row_count * lax.axis_size("seq") * lax.axis_size("dp")
    grad_factor = 1.0 / math.sqrt(token_count)
    terms_qkv = jnp.einsum("td,cth->cdh", normalized_rows, grad_qkv, preferred_element_type=F32)
    term_out = jnp.einsum("td,th->dh", row_gradients, attended_flat, preferred_element_type=F32)
    terms = jnp.concatenate([terms_qkv, term_out[None]], axis=0) * grad_factor
    seq_summed = lax.psum_scatter(terms.astype(BF), "seq", scatter_dimension=1, tiled=True)
    weight_grads = lax.psum_scatter(seq_summed, "dp", scatter_dimension=1, tiled=True).astype(F32)
    input_part = jnp.einsum("cth,cdh->td", grad_qkv, weights[:3], preferred_element_type=F32)
    reduced_total = lax.psum(input_part.astype(BF), "pipe").astype(F32)
    leading_term = jnp.mean(reduced_total, axis=1, keepdims=True)
    trailing_term = jnp.mean(reduced_total * standardized_input, axis=1, keepdims=True)
    input_gradient = (
        row_gradients.astype(F32)
        + inverse_deviation * (reduced_total - leading_term - standardized_input * trailing_term)
    ).astype(BF)
    return (input_gradient[None], weight_grads)


def local(embeddings, upstream, attn_weights):
    n = lax.axis_size("seq")
    heads = attn_weights.shape[2] // HD
    one_head_each = (
        heads == n
        and n == 4
        and lax.axis_size("grp") == 2
        and lax.axis_size("dp") == 2
        and lax.axis_size("pipe") == 2
        and attn_weights.shape[1] % 16 == 0
        and embeddings.shape[0] == 1
        and embeddings.shape[1] % 32 == 0
    )
    return (local_heads if one_head_each else local_gathered)(embeddings, upstream, attn_weights)


def solution(mesh):
    in_specs = (
        P(("grp", "dp"), "seq", None),
        P(("grp", "dp"), "seq", None),
        P(None, ("seq", "dp"), "pipe"),
    )
    out_specs = (P(("grp", "dp"), "seq", None), P("grp", ("seq", "dp"), "pipe"))
    return jax.shard_map(local, mesh=mesh, in_specs=in_specs, out_specs=out_specs, check_vma=False)
```

```python
import functools
import math

import jax
import jax.numpy as jnp
from jax import lax
from jax.experimental import pallas as pl
from jax.experimental.pallas import tpu as pltpu
from jax.sharding import PartitionSpec as P

HD = 104
SLOT = 128

EPSILON = 1e-06
BF = jnp.bfloat16
F32 = jnp.float32
PARAMS = pltpu.CompilerParams(vmem_limit_bytes=24 * 1024 * 1024)
VMEM_SPEC = pl.BlockSpec(memory_space=pltpu.VMEM)
ANY_SPEC = pl.BlockSpec(memory_space=pl.ANY)


def standardize(features):
    row_mean = jnp.mean(features, axis=1, keepdims=True)
    mean_removed = features - row_mean
    variance = jnp.mean(mean_removed * mean_removed, axis=1, keepdims=True)
    inverse_deviation = lax.rsqrt(variance + EPSILON)
    return mean_removed * inverse_deviation, inverse_deviation


def nt(a, b):
    return lax.dot_general(a, b, (((1,), (1,)), ((), ())), preferred_element_type=F32)


def tn(a, b):
    return lax.dot_general(a, b, (((0,), (0,)), ((), ())), preferred_element_type=F32)


def nn(a, b):
    return jnp.dot(a, b, preferred_element_type=F32)


SPARE = SLOT - HD
LEFT = HD - 3 * SPARE
FOLD = SLOT // LEFT


def packed_rows(share):
    group = -(-share // (16 * FOLD)) * 16
    return 3 * share + group


def half_rows(share):
    return -(-packed_rows(share) // 32) * 16


def packed(mats):
    last = mats[3]
    share = last.shape[0]
    group = packed_rows(share) - 3 * share
    tiles = [
        jnp.concatenate([mats[j], last[:, j * SPARE : (j + 1) * SPARE]], axis=1) for j in range(3)
    ]
    tail = last[:, 3 * SPARE :]
    fill = jnp.zeros((FOLD * group - share, LEFT), BF)
    columns = [tail[j * group : (j + 1) * group] for j in range(FOLD - 1)]
    columns.append(jnp.concatenate([tail[(FOLD - 1) * group :], fill], axis=0))
    return tiles + [jnp.concatenate(columns, axis=1)]


def unpacked(ref, share):
    tiles = [ref[j * share : (j + 1) * share, :] for j in range(3)]
    rest = ref[3 * share :, :]
    group = rest.shape[0]
    columns = [rest[:, j * LEFT : (j + 1) * LEFT] for j in range(FOLD)]
    columns[-1] = columns[-1][: share - (FOLD - 1) * group]
    last = [tile[:, HD:] for tile in tiles] + [jnp.concatenate(columns, axis=0)]
    return [tile[:, :HD] for tile in tiles] + [jnp.concatenate(last, axis=1)]


def pack_kernel(n, w_ref, *refs):
    outs, staged = refs[:n], refs[n]
    me = lax.axis_index("seq")
    group = lax.axis_index("grp")
    share = w_ref.shape[1]
    count = outs[0].shape[0]
    for head in range(n):
        mats = [w_ref[mat, :, head * HD : (head + 1) * HD] for mat in range(4)]
        for j, tile in enumerate(packed(mats)):
            staged[head, j * share : j * share + tile.shape[0], :] = tile
    first = pl.multiple_of(group * (staged.shape[1] - count), 16)
    for k in range(n):
        outs[k][...] = staged[me ^ k, pl.ds(first, count), :]


def weights_kernel(n, share, *refs):
    pieces, w_ref, staged = refs[:4], refs[4], refs[5]
    me = lax.axis_index("seq")
    image = lax.axis_index("dp")
    group = lax.axis_index("grp")
    count = pieces[0].shape[0] // n
    fill = jnp.zeros((share, SPARE), BF)
    for k in range(n):
        for other in range(2):
            for piece, at in ((pieces[other], group), (pieces[2 + other], 1 - group)):
                first = pl.multiple_of(at * (staged.shape[1] - count), 16)
                staged[2 * k + other, pl.ds(first, count), :] = piece[k * count : (k + 1) * count]
            at = 1 - image if other else image
            span = pl.ds(pl.multiple_of(((me ^ k) * 2 + at) * share, 16), share)
            for mat, block in enumerate(unpacked(staged.at[2 * k + other], share)):
                w_ref[span, mat * SLOT : (mat + 1) * SLOT] = jnp.concatenate([block, fill], axis=1)


def norm_kernel(x_ref, up_ref, send_ref, rest_ref, staged):
    core = lax.axis_index("pipe")
    half = x_ref.shape[0] // 2
    staged[...] = standardize(x_ref[...].astype(F32))[0].astype(BF)
    for target, at in ((send_ref, core), (rest_ref, 1 - core)):
        span = pl.ds(pl.multiple_of(at * half, half), half)
        target[:half] = staged[span, :]
        target[half:] = up_ref[span, :]


def merge_kernel(*refs):
    share = refs[0].shape[0]
    for k, ref in enumerate(refs[:-1]):
        refs[-1][k * share : (k + 1) * share] = ref[...]


def head_kernel(n, factor, *refs):
    blocks = [(refs[2 * k], refs[2 * k + 1]) for k in range(n + 1)]
    w_full, keep_ref, give_ref, w_keep_ref, w_give_ref = refs[2 * n + 2 : 2 * n + 7]
    x_full, up_full, grads, staged, term_k, term_v = refs[2 * n + 7 :]
    me = lax.axis_index("seq")
    image = lax.axis_index("dp")
    rows = blocks[0][0].shape[0]
    half = rows // 2
    share = w_full.shape[0] // (2 * n)

    def place(k, sides):
        for side, source in enumerate(sides):
            span = slice(k * rows + side * half, k * rows + (side + 1) * half)
            x_full[span, :] = source[:half, :]
            up_full[span, :] = source[half:, :]

    for k in range(n - 1):
        place(k, blocks[k])

    @pl.when((me == 0) | (me == n - 1))
    def _():
        place(n - 1, blocks[n])

    @pl.when((me != 0) & (me != n - 1))
    def _():
        place(n - 1, blocks[n - 1])

    scale = HD ** (-0.5)
    qkv = nn(x_full[...], w_full[:, : 3 * SLOT]).astype(BF)
    grad_att = nn(up_full[...], w_full[:, 3 * SLOT :]).astype(BF)
    key_rows = qkv[:, SLOT : 2 * SLOT]
    value_rows = qkv[:, 2 * SLOT :]
    for b in range(n):
        span = slice(b * rows, (b + 1) * rows)
        query = qkv[span, :SLOT]
        grad_out = grad_att[span]
        scores = nt(query, key_rows) * scale
        weight = jnp.exp(scores - jnp.max(scores, axis=1, keepdims=True))
        probs = (weight / jnp.sum(weight, axis=1, keepdims=True)).astype(BF)
        attended = nn(probs, value_rows).astype(BF)
        delta = jnp.sum(grad_out.astype(F32) * attended.astype(F32), axis=1, keepdims=True)
        dprobs = nt(grad_out, value_rows)
        dscores = (probs.astype(F32) * (dprobs - delta) * scale).astype(BF)
        grads[span, :SLOT] = nn(dscores, key_rows).astype(BF)
        grads[span, 3 * SLOT :] = attended
        key_term = tn(dscores, query).astype(BF).astype(F32)
        value_term = tn(probs, grad_out).astype(BF).astype(F32)
        if b == 0:
            term_k[...] = key_term
            term_v[...] = value_term
        else:
            term_k[...] += key_term
            term_v[...] += value_term
    grads[:, SLOT : 2 * SLOT] = term_k[...].astype(BF)
    grads[:, 2 * SLOT : 3 * SLOT] = term_v[...].astype(BF)
    for b in range(n):
        span = slice(b * rows, (b + 1) * rows)
        part = nt(grads[span, : 3 * SLOT], w_full[:, : 3 * SLOT]).astype(BF)
        keep_ref[b] = part[:half]
        give_ref[b] = part[half:]
    staged[:, : 3 * SLOT] = (tn(x_full[...], grads[:, : 3 * SLOT]) * factor).astype(BF)
    staged[:, 3 * SLOT :] = (tn(up_full[...], grads[:, 3 * SLOT :]) * factor).astype(BF)
    for k in range(n):
        for target, at in ((w_keep_ref, image), (w_give_ref, 1 - image)):
            first = pl.multiple_of(((me ^ k) * 2 + at) * share, 16)
            mats = [
                staged[pl.ds(first, share), mat * SLOT : mat * SLOT + HD] for mat in range(4)
            ]
            for j, tile in enumerate(packed(mats)):
                target[k, j * share : j * share + tile.shape[0], :] = tile


def sum_kernel(n, mine_ref, theirs_ref, *outs):
    for k in range(n):
        outs[k][...] = (mine_ref[k].astype(F32) + theirs_ref[k].astype(F32)).astype(BF)


def final_kernel(n, x_ref, up_ref, *refs):
    parts, (out_ref, rest_ref) = refs[:n], refs[n:]
    half = 2 * out_ref.shape[0]
    core = lax.axis_index("pipe")
    span = pl.ds(pl.multiple_of(core * half, half), half)
    total = parts[0][...].astype(F32)
    for part in parts[1:]:
        total += part[...].astype(F32)
    xhat, inverse_deviation = standardize(x_ref[span, :].astype(F32))
    leading = jnp.mean(total, axis=1, keepdims=True)
    trailing = jnp.mean(total * xhat, axis=1, keepdims=True)
    result = (
        up_ref[span, :].astype(F32) + inverse_deviation * (total - leading - xhat * trailing)
    ).astype(BF)
    out_ref[...] = result[: half // 2]
    rest_ref[...] = result[half // 2 :]


def join_kernel(n, *refs):
    pairs, parts, (input_ref, out_ref, staged) = refs[:4], refs[4 : 4 + n], refs[4 + n :]
    me = lax.axis_index("seq")
    core = lax.axis_index("pipe")
    count = pairs[0].shape[0]
    for i, ref in enumerate(pairs):
        side = core if i < 2 else 1 - core
        first = pl.multiple_of((2 * side + i % 2) * count, count)
        input_ref[pl.ds(first, count), :] = ref[...]
    for k in range(n):
        staged[me ^ k] = parts[k][...]
    for head in range(n):
        for mat, block in enumerate(unpacked(staged.at[head], out_ref.shape[1])):
            out_ref[mat, :, head * HD : (head + 1) * HD] = block.astype(F32)


def call(kernel, out_shape, args, scratch=(), plain=0, out_space=pltpu.VMEM):
    single = not isinstance(out_shape, list)
    shapes = [out_shape] if single else out_shape
    args = list(args[:plain]) + [
        pltpu.with_memory_space_constraint(a, pltpu.VMEM) for a in args[plain:]
    ]
    out = pl.pallas_call(
        kernel,
        out_shape=[out_space(*s) for s in shapes],
        in_specs=[VMEM_SPEC] * len(args),
        out_specs=[VMEM_SPEC] * len(shapes),
        scratch_shapes=list(scratch),
        compiler_params=PARAMS,
    )(*args)
    return out[0] if single else list(out)


def local_heads(embeddings, upstream, attn_weights):
    n = lax.axis_size("seq")
    x, up = embeddings[0], upstream[0]
    rows, width = x.shape
    share = attn_weights.shape[1]
    patches = n * rows
    half = rows // 2
    me = lax.axis_index("seq")

    def across(value, k):
        return lax.ppermute(value, "seq", [(i, i ^ k) for i in range(n)])

    def swap(value, axis):
        return lax.ppermute(value, axis, [(0, 1), (1, 0)])


    full, count = packed_rows(share), half_rows(share)
    chunks = call(
        functools.partial(pack_kernel, n),
        [((count, SLOT), BF)] * n,
        (attn_weights,),
        [pltpu.VMEM((n, full, SLOT), BF)],
        plain=1,
    )
    arrived = [across(chunks[k], k) for k in range(1, n)]
    send, rest = call(
        norm_kernel, [((rows, width), BF)] * 2, (x, up), [pltpu.VMEM((rows, width), BF)], plain=2
    )
    send, arrived[0] = lax.optimization_barrier((send, arrived[0]))
    merged = call(merge_kernel, ((n * count, SLOT), BF), (chunks[0], *arrived))
    beside = swap(merged, "dp")
    above = swap(merged, "grp")
    second = across(send, 2)
    first = across(send, 1)
    later, first, second, beside, above = lax.optimization_barrier(
        (send, first, second, beside, above)
    )
    corner = swap(above, "dp")
    weights = call(
        functools.partial(weights_kernel, n, share),
        ((width, 4 * SLOT), BF),
        (merged, beside, above, corner),
        [pltpu.VMEM((2 * n, full, SLOT), BF)],
    )
    middle = lax.ppermute(later, "seq", [(1, 2), (2, 1)])
    passed = lax.ppermute(second, "seq", [(2, 3), (1, 0)])
    weights, middle, passed = lax.optimization_barrier((weights, middle, passed))
    args = [send, rest]
    for block in (first, second, middle, passed):
        args += [block, swap(block, "pipe")]
    args.append(weights)
    factor = 1.0 / math.sqrt(patches * lax.axis_size("dp"))
    keep, give, w_keep, w_give = call(
        functools.partial(head_kernel, n, factor),
        [((n, half, width), BF)] * 2 + [((n, full, SLOT), BF)] * 2,
        args,
        [
            pltpu.VMEM((patches, width), BF),
            pltpu.VMEM((patches, width), BF),
            pltpu.VMEM((patches, 4 * SLOT), BF),
            pltpu.VMEM((width, 4 * SLOT), BF),
            pltpu.VMEM((patches, SLOT), F32),
            pltpu.VMEM((patches, SLOT), F32),
        ],
    )
    taken = swap(give, "pipe")
    w_taken = swap(w_give, "dp")
    sums = call(functools.partial(sum_kernel, n), [((half, width), BF)] * n, (keep, taken))
    parts = [across(sums[k], k) for k in range(1, n)]
    w_taken, sums[0] = lax.optimization_barrier((w_taken, sums[0]))
    w_sums = call(
        functools.partial(sum_kernel, n), [((full, SLOT), BF)] * n, (w_keep, w_taken)
    )
    w_parts = [w_sums[0]] + [across(w_sums[k], k) for k in range(1, n)]
    mine = call(
        functools.partial(final_kernel, n),
        [((half // 2, width), BF)] * 2,
        (x, up, sums[0], *parts),
        plain=2,
    )
    input_gradient, weight_grads = call(
        functools.partial(join_kernel, n),
        [((rows, width), BF), ((4, share, n * HD), F32)],
        (*mine, *[swap(m, "pipe") for m in mine], *w_parts),
        [pltpu.VMEM((n, full, SLOT), BF)],
        out_space=jax.ShapeDtypeStruct,
    )
    return (input_gradient[None], weight_grads)


def local_gathered(embeddings, upstream, attn_weights):
    tokens = embeddings[0]
    row_gradients = upstream[0]
    row_count = tokens.shape[0]
    weights = lax.all_gather(attn_weights, ("seq", "dp"), axis=1, tiled=True)
    local_width = weights.shape[2]
    head_count = local_width // HD
    score_scale = HD ** (-0.5)
    standardized_input, inverse_deviation = standardize(tokens.astype(F32))
    normalized_rows = standardized_input.astype(BF)
    proj = jnp.einsum(
        "td,cdh->cth", normalized_rows, weights[:3], preferred_element_type=F32
    ).astype(BF)
    gathered = lax.all_gather(proj[1:], "seq", axis=1, tiled=True)
    key_count = gathered.shape[1]
    query_heads = proj[0].reshape(row_count, head_count, HD).transpose(1, 0, 2)
    key_heads = gathered[0].reshape(key_count, head_count, HD).transpose(1, 0, 2)
    value_heads = gathered[1].reshape(key_count, head_count, HD).transpose(1, 0, 2)
    grad_att = jnp.dot(row_gradients, weights[3], preferred_element_type=F32).astype(BF)
    grad_heads = grad_att.reshape(row_count, head_count, HD).transpose(1, 0, 2)

    def one_head(items):
        query_rows, key_rows, value_rows, grad_out = items
        scores = nn(query_rows, key_rows.T) * score_scale
        row_max = jnp.max(scores, axis=1, keepdims=True)
        log_total = row_max + jnp.log(jnp.sum(jnp.exp(scores - row_max), axis=1, keepdims=True))
        probs = jnp.exp(scores - log_total).astype(BF)
        attended = nn(probs, value_rows).astype(BF)
        row_delta = jnp.sum(
            grad_out.astype(F32) * attended.astype(F32), axis=1, keepdims=True
        )
        dprobs = nn(grad_out, value_rows.T)
        dscores = (probs.astype(F32) * (dprobs - row_delta) * score_scale).astype(BF)
        grad_q = nn(dscores, key_rows).astype(BF)
        return (attended, grad_q, nn(dscores.T, query_rows), nn(probs.T, grad_out))

    attended_h, grad_q_h, key_h, value_h = lax.map(
        one_head, (query_heads, key_heads, value_heads, grad_heads)
    )
    attended_flat = attended_h.transpose(1, 0, 2).reshape(row_count, local_width)
    grad_q = grad_q_h.transpose(1, 0, 2).reshape(1, row_count, local_width)
    key_terms = key_h.transpose(1, 0, 2).reshape(key_count, local_width)
    value_terms = value_h.transpose(1, 0, 2).reshape(key_count, local_width)
    both_terms = jnp.stack([key_terms, value_terms])
    owned = lax.psum_scatter(both_terms.astype(BF), "seq", scatter_dimension=1, tiled=True)
    grad_qkv = jnp.concatenate([grad_q, owned], axis=0)
    token_count = row_count * lax.axis_size("seq") * lax.axis_size("dp")
    grad_factor = 1.0 / math.sqrt(token_count)
    terms_qkv = jnp.einsum("td,cth->cdh", normalized_rows, grad_qkv, preferred_element_type=F32)
    term_out = jnp.einsum("td,th->dh", row_gradients, attended_flat, preferred_element_type=F32)
    terms = jnp.concatenate([terms_qkv, term_out[None]], axis=0) * grad_factor
    seq_summed = lax.psum_scatter(terms.astype(BF), "seq", scatter_dimension=1, tiled=True)
    weight_grads = lax.psum_scatter(seq_summed, "dp", scatter_dimension=1, tiled=True).astype(F32)
    input_part = jnp.einsum("cth,cdh->td", grad_qkv, weights[:3], preferred_element_type=F32)
    reduced_total = lax.psum(input_part.astype(BF), "pipe").astype(F32)
    leading_term = jnp.mean(reduced_total, axis=1, keepdims=True)
    trailing_term = jnp.mean(reduced_total * standardized_input, axis=1, keepdims=True)
    input_gradient = (
        row_gradients.astype(F32)
        + inverse_deviation * (reduced_total - leading_term - standardized_input * trailing_term)
    ).astype(BF)
    return (input_gradient[None], weight_grads)


def local(embeddings, upstream, attn_weights):
    n = lax.axis_size("seq")
    heads = attn_weights.shape[2] // HD
    one_head_each = (
        heads == n
        and n == 4
        and lax.axis_size("grp") == 2
        and lax.axis_size("dp") == 2
        and lax.axis_size("pipe") == 2
        and attn_weights.shape[1] % 16 == 0
        and embeddings.shape[0] == 1
        and embeddings.shape[1] % 32 == 0
    )
    return (local_heads if one_head_each else local_gathered)(embeddings, upstream, attn_weights)


def solution(mesh):
    in_specs = (
        P(("grp", "dp"), "seq", None),
        P(("grp", "dp"), "seq", None),
        P(None, ("seq", "dp"), "pipe"),
    )
    out_specs = (P(("grp", "dp"), "seq", None), P("grp", ("seq", "dp"), "pipe"))
    return jax.shard_map(local, mesh=mesh, in_specs=in_specs, out_specs=out_specs, check_vma=False)
```

```python
import functools
import math

import jax
import jax.numpy as jnp
from jax import lax
from jax.experimental import pallas as pl
from jax.experimental.pallas import tpu as pltpu
from jax.sharding import PartitionSpec as P

HD = 104
SLOT = 128

EPSILON = 1e-06
BF = jnp.bfloat16
F32 = jnp.float32
PARAMS = pltpu.CompilerParams(vmem_limit_bytes=24 * 1024 * 1024)
VMEM_SPEC = pl.BlockSpec(memory_space=pltpu.VMEM)
ANY_SPEC = pl.BlockSpec(memory_space=pl.ANY)


def standardize(features):
    row_mean = jnp.mean(features, axis=1, keepdims=True)
    mean_removed = features - row_mean
    variance = jnp.mean(mean_removed * mean_removed, axis=1, keepdims=True)
    inverse_deviation = lax.rsqrt(variance + EPSILON)
    return mean_removed * inverse_deviation, inverse_deviation


def nt(a, b):
    return lax.dot_general(a, b, (((1,), (1,)), ((), ())), preferred_element_type=F32)


def tn(a, b):
    return lax.dot_general(a, b, (((0,), (0,)), ((), ())), preferred_element_type=F32)


def nn(a, b):
    return jnp.dot(a, b, preferred_element_type=F32)


SPARE = SLOT - HD
LEFT = HD - 3 * SPARE
FOLD = SLOT // LEFT


def packed_rows(share):
    group = -(-share // (16 * FOLD)) * 16
    return 3 * share + group


def half_rows(share):
    return -(-packed_rows(share) // 32) * 16


def packed(mats):
    last = mats[3]
    share = last.shape[0]
    group = packed_rows(share) - 3 * share
    tiles = [
        jnp.concatenate([mats[j], last[:, j * SPARE : (j + 1) * SPARE]], axis=1) for j in range(3)
    ]
    tail = last[:, 3 * SPARE :]
    fill = jnp.zeros((FOLD * group - share, LEFT), BF)
    columns = [tail[j * group : (j + 1) * group] for j in range(FOLD - 1)]
    columns.append(jnp.concatenate([tail[(FOLD - 1) * group :], fill], axis=0))
    return tiles + [jnp.concatenate(columns, axis=1)]


def unpacked(ref, share):
    tiles = [ref[j * share : (j + 1) * share, :] for j in range(3)]
    rest = ref[3 * share :, :]
    group = rest.shape[0]
    columns = [rest[:, j * LEFT : (j + 1) * LEFT] for j in range(FOLD)]
    columns[-1] = columns[-1][: share - (FOLD - 1) * group]
    last = [tile[:, HD:] for tile in tiles] + [jnp.concatenate(columns, axis=0)]
    return [tile[:, :HD] for tile in tiles] + [jnp.concatenate(last, axis=1)]


def pack_kernel(n, w_ref, *refs):
    outs, staged = refs[:n], refs[n]
    me = lax.axis_index("seq")
    group = lax.axis_index("grp")
    share = w_ref.shape[1]
    count = outs[0].shape[0]
    for head in range(n):
        mats = [w_ref[mat, :, head * HD : (head + 1) * HD] for mat in range(4)]
        for j, tile in enumerate(packed(mats)):
            staged[head, j * share : j * share + tile.shape[0], :] = tile
    first = pl.multiple_of(group * (staged.shape[1] - count), 16)
    for k in range(n):
        outs[k][...] = staged[me ^ k, pl.ds(first, count), :]


def weights_kernel(n, share, *refs):
    pieces, w_ref, staged = refs[:4], refs[4], refs[5]
    me = lax.axis_index("seq")
    image = lax.axis_index("dp")
    group = lax.axis_index("grp")
    count = pieces[0].shape[0] // n
    fill = jnp.zeros((share, SPARE), BF)
    for k in range(n):
        for other in range(2):
            for piece, at in ((pieces[other], group), (pieces[2 + other], 1 - group)):
                first = pl.multiple_of(at * (staged.shape[1] - count), 16)
                staged[2 * k + other, pl.ds(first, count), :] = piece[k * count : (k + 1) * count]
            at = 1 - image if other else image
            span = pl.ds(pl.multiple_of(((me ^ k) * 2 + at) * share, 16), share)
            for mat, block in enumerate(unpacked(staged.at[2 * k + other], share)):
                w_ref[span, mat * SLOT : (mat + 1) * SLOT] = jnp.concatenate([block, fill], axis=1)


def norm_kernel(x_ref, up_ref, send_ref, rest_ref, staged):
    core = lax.axis_index("pipe")
    half = x_ref.shape[0] // 2
    staged[...] = standardize(x_ref[...].astype(F32))[0].astype(BF)
    for target, at in ((send_ref, core), (rest_ref, 1 - core)):
        span = pl.ds(pl.multiple_of(at * half, half), half)
        target[:half] = staged[span, :]
        target[half:] = up_ref[span, :]


def merge_kernel(*refs):
    share = refs[0].shape[0]
    for k, ref in enumerate(refs[:-1]):
        refs[-1][k * share : (k + 1) * share] = ref[...]


def project(x, up, w_ref):
    return [
        nn(x, w_ref[:, : 3 * SLOT]).astype(BF),
        nn(up, w_ref[:, 3 * SLOT :]).astype(BF),
    ]


def place(row, sides, x_ref, up_ref):
    half = sides[0].shape[0] // 2
    for side, source in enumerate(sides):
        span = slice(row + side * half, row + (side + 1) * half)
        x_ref[span, :] = source[:half, :]
        up_ref[span, :] = source[half:, :]


def project_kernel(n, *refs):
    w_ref, x_ref, up_ref, made_ref = refs[2 * n - 2 :]
    rows = refs[0].shape[0]
    for k in range(n - 1):
        place(k * rows, refs[2 * k : 2 * k + 2], x_ref, up_ref)
    made_ref[:, : 3 * SLOT], made_ref[:, 3 * SLOT :] = project(x_ref[...], up_ref[...], w_ref)


def head_kernel(n, *refs):
    middle, passed = refs[:2], refs[2:4]
    made_ref, w_ref, keep_ref, give_ref, grads, x_ref, up_ref = refs[4:11]
    made, term_k, term_v = refs[11:]
    me = lax.axis_index("seq")
    rows = x_ref.shape[0]
    half = rows // 2
    ready = (n - 1) * rows

    @pl.when((me == 0) | (me == n - 1))
    def _():
        place(0, passed, x_ref, up_ref)

    @pl.when((me != 0) & (me != n - 1))
    def _():
        place(0, middle, x_ref, up_ref)

    made[:ready, :] = made_ref[...]
    made[ready:, : 3 * SLOT], made[ready:, 3 * SLOT :] = project(x_ref[...], up_ref[...], w_ref)
    scale = HD ** (-0.5)
    key_rows = made[:, SLOT : 2 * SLOT]
    value_rows = made[:, 2 * SLOT : 3 * SLOT]
    for b in range(n):
        span = slice(b * rows, (b + 1) * rows)
        query = made[span, :SLOT]
        grad_out = made[span, 3 * SLOT :]
        scores = nt(query, key_rows) * scale
        weight = jnp.exp(scores - jnp.max(scores, axis=1, keepdims=True))
        probs = (weight / jnp.sum(weight, axis=1, keepdims=True)).astype(BF)
        attended = nn(probs, value_rows).astype(BF)
        delta = jnp.sum(grad_out.astype(F32) * attended.astype(F32), axis=1, keepdims=True)
        dprobs = nt(grad_out, value_rows)
        dscores = (probs.astype(F32) * (dprobs - delta) * scale).astype(BF)
        grads[span, :SLOT] = nn(dscores, key_rows).astype(BF)
        grads[span, 3 * SLOT :] = attended
        key_term = tn(dscores, query).astype(BF).astype(F32)
        value_term = tn(probs, grad_out).astype(BF).astype(F32)
        if b == 0:
            term_k[...] = key_term
            term_v[...] = value_term
        else:
            term_k[...] += key_term
            term_v[...] += value_term
    grads[:, SLOT : 2 * SLOT] = term_k[...].astype(BF)
    grads[:, 2 * SLOT : 3 * SLOT] = term_v[...].astype(BF)
    for b in range(n):
        span = slice(b * rows, (b + 1) * rows)
        part = nt(grads[span, : 3 * SLOT], w_ref[:, : 3 * SLOT]).astype(BF)
        keep_ref[b] = part[:half]
        give_ref[b] = part[half:]


def weight_kernel(n, factor, x_ref, x_last, up_ref, up_last, grads, keep_ref, give_ref, staged):
    me = lax.axis_index("seq")
    image = lax.axis_index("dp")
    ready = x_ref.shape[0]
    share = staged.shape[0] // (2 * n)
    for lanes, first, last in (
        (slice(0, 3 * SLOT), x_ref, x_last),
        (slice(3 * SLOT, 4 * SLOT), up_ref, up_last),
    ):
        total = tn(first[...], grads[:ready, lanes]) + tn(last[...], grads[ready:, lanes])
        staged[:, lanes] = (total * factor).astype(BF)
    for k in range(n):
        for target, at in ((keep_ref, image), (give_ref, 1 - image)):
            first = pl.multiple_of(((me ^ k) * 2 + at) * share, 16)
            mats = [
                staged[pl.ds(first, share), mat * SLOT : mat * SLOT + HD] for mat in range(4)
            ]
            for j, tile in enumerate(packed(mats)):
                target[k, j * share : j * share + tile.shape[0], :] = tile


def sum_kernel(n, mine_ref, theirs_ref, *outs):
    for k in range(n):
        outs[k][...] = (mine_ref[k].astype(F32) + theirs_ref[k].astype(F32)).astype(BF)


def final_kernel(n, x_ref, up_ref, *refs):
    parts, (out_ref, rest_ref) = refs[:n], refs[n:]
    half = 2 * out_ref.shape[0]
    core = lax.axis_index("pipe")
    span = pl.ds(pl.multiple_of(core * half, half), half)
    total = parts[0][...].astype(F32)
    for part in parts[1:]:
        total += part[...].astype(F32)
    xhat, inverse_deviation = standardize(x_ref[span, :].astype(F32))
    leading = jnp.mean(total, axis=1, keepdims=True)
    trailing = jnp.mean(total * xhat, axis=1, keepdims=True)
    result = (
        up_ref[span, :].astype(F32) + inverse_deviation * (total - leading - xhat * trailing)
    ).astype(BF)
    out_ref[...] = result[: half // 2]
    rest_ref[...] = result[half // 2 :]


def join_kernel(n, *refs):
    pairs, parts, (input_ref, out_ref, staged) = refs[:4], refs[4 : 4 + n], refs[4 + n :]
    me = lax.axis_index("seq")
    core = lax.axis_index("pipe")
    count = pairs[0].shape[0]
    for i, ref in enumerate(pairs):
        side = core if i < 2 else 1 - core
        first = pl.multiple_of((2 * side + i % 2) * count, count)
        input_ref[pl.ds(first, count), :] = ref[...]
    for k in range(n):
        staged[me ^ k] = parts[k][...]
    for head in range(n):
        for mat, block in enumerate(unpacked(staged.at[head], out_ref.shape[1])):
            out_ref[mat, :, head * HD : (head + 1) * HD] = block.astype(F32)


def call(kernel, out_shape, args, scratch=(), plain=0, out_space=pltpu.VMEM):
    single = not isinstance(out_shape, list)
    shapes = [out_shape] if single else out_shape
    args = list(args[:plain]) + [
        pltpu.with_memory_space_constraint(a, pltpu.VMEM) for a in args[plain:]
    ]
    out = pl.pallas_call(
        kernel,
        out_shape=[out_space(*s) for s in shapes],
        in_specs=[VMEM_SPEC] * len(args),
        out_specs=[VMEM_SPEC] * len(shapes),
        scratch_shapes=list(scratch),
        compiler_params=PARAMS,
    )(*args)
    return out[0] if single else list(out)


def local_heads(embeddings, upstream, attn_weights):
    n = lax.axis_size("seq")
    x, up = embeddings[0], upstream[0]
    rows, width = x.shape
    share = attn_weights.shape[1]
    patches = n * rows
    half = rows // 2
    me = lax.axis_index("seq")

    def across(value, k):
        return lax.ppermute(value, "seq", [(i, i ^ k) for i in range(n)])

    def swap(value, axis):
        return lax.ppermute(value, axis, [(0, 1), (1, 0)])


    full, count = packed_rows(share), half_rows(share)
    chunks = call(
        functools.partial(pack_kernel, n),
        [((count, SLOT), BF)] * n,
        (attn_weights,),
        [pltpu.VMEM((n, full, SLOT), BF)],
        plain=1,
    )
    arrived = [across(chunks[k], k) for k in range(1, n)]
    send, rest = call(
        norm_kernel, [((rows, width), BF)] * 2, (x, up), [pltpu.VMEM((rows, width), BF)], plain=2
    )
    send, arrived[0] = lax.optimization_barrier((send, arrived[0]))
    merged = call(merge_kernel, ((n * count, SLOT), BF), (chunks[0], *arrived))
    beside = swap(merged, "dp")
    above = swap(merged, "grp")
    second = across(send, 2)
    first = across(send, 1)
    later, first, second, beside, above = lax.optimization_barrier(
        (send, first, second, beside, above)
    )
    corner = swap(above, "dp")
    weights = call(
        functools.partial(weights_kernel, n, share),
        ((width, 4 * SLOT), BF),
        (merged, beside, above, corner),
        [pltpu.VMEM((2 * n, full, SLOT), BF)],
    )
    middle = lax.ppermute(later, "seq", [(1, 2), (2, 1)])
    passed = lax.ppermute(second, "seq", [(2, 3), (1, 0)])
    weights, middle, passed = lax.optimization_barrier((weights, middle, passed))
    ready = patches - rows
    x_head, up_head, made = call(
        functools.partial(project_kernel, n),
        [((ready, width), BF)] * 2 + [((ready, 4 * SLOT), BF)],
        (send, rest, first, swap(first, "pipe"), second, swap(second, "pipe"), weights),
    )
    keep, give, grads, x_last, up_last = call(
        functools.partial(head_kernel, n),
        [((n, half, width), BF)] * 2 + [((patches, 4 * SLOT), BF)] + [((rows, width), BF)] * 2,
        (middle, swap(middle, "pipe"), passed, swap(passed, "pipe"), made, weights),
        [
            pltpu.VMEM((patches, 4 * SLOT), BF),
            pltpu.VMEM((patches, SLOT), F32),
            pltpu.VMEM((patches, SLOT), F32),
        ],
    )
    factor = 1.0 / math.sqrt(patches * lax.axis_size("dp"))
    w_keep, w_give = call(
        functools.partial(weight_kernel, n, factor),
        [((n, full, SLOT), BF)] * 2,
        (x_head, x_last, up_head, up_last, grads),
        [pltpu.VMEM((width, 4 * SLOT), BF)],
    )
    taken = swap(give, "pipe")
    w_taken = swap(w_give, "dp")
    sums = call(functools.partial(sum_kernel, n), [((half, width), BF)] * n, (keep, taken))
    parts = [across(sums[k], k) for k in range(1, n)]
    w_taken, sums[0] = lax.optimization_barrier((w_taken, sums[0]))
    w_sums = call(
        functools.partial(sum_kernel, n), [((full, SLOT), BF)] * n, (w_keep, w_taken)
    )
    w_parts = [w_sums[0]] + [across(w_sums[k], k) for k in range(1, n)]
    mine = call(
        functools.partial(final_kernel, n),
        [((half // 2, width), BF)] * 2,
        (x, up, sums[0], *parts),
        plain=2,
    )
    input_gradient, weight_grads = call(
        functools.partial(join_kernel, n),
        [((rows, width), BF), ((4, share, n * HD), F32)],
        (*mine, *[swap(m, "pipe") for m in mine], *w_parts),
        [pltpu.VMEM((n, full, SLOT), BF)],
        out_space=jax.ShapeDtypeStruct,
    )
    return (input_gradient[None], weight_grads)


def local_gathered(embeddings, upstream, attn_weights):
    tokens = embeddings[0]
    row_gradients = upstream[0]
    row_count = tokens.shape[0]
    weights = lax.all_gather(attn_weights, ("seq", "dp"), axis=1, tiled=True)
    local_width = weights.shape[2]
    head_count = local_width // HD
    score_scale = HD ** (-0.5)
    standardized_input, inverse_deviation = standardize(tokens.astype(F32))
    normalized_rows = standardized_input.astype(BF)
    proj = jnp.einsum(
        "td,cdh->cth", normalized_rows, weights[:3], preferred_element_type=F32
    ).astype(BF)
    gathered = lax.all_gather(proj[1:], "seq", axis=1, tiled=True)
    key_count = gathered.shape[1]
    query_heads = proj[0].reshape(row_count, head_count, HD).transpose(1, 0, 2)
    key_heads = gathered[0].reshape(key_count, head_count, HD).transpose(1, 0, 2)
    value_heads = gathered[1].reshape(key_count, head_count, HD).transpose(1, 0, 2)
    grad_att = jnp.dot(row_gradients, weights[3], preferred_element_type=F32).astype(BF)
    grad_heads = grad_att.reshape(row_count, head_count, HD).transpose(1, 0, 2)

    def one_head(items):
        query_rows, key_rows, value_rows, grad_out = items
        scores = nn(query_rows, key_rows.T) * score_scale
        row_max = jnp.max(scores, axis=1, keepdims=True)
        log_total = row_max + jnp.log(jnp.sum(jnp.exp(scores - row_max), axis=1, keepdims=True))
        probs = jnp.exp(scores - log_total).astype(BF)
        attended = nn(probs, value_rows).astype(BF)
        row_delta = jnp.sum(
            grad_out.astype(F32) * attended.astype(F32), axis=1, keepdims=True
        )
        dprobs = nn(grad_out, value_rows.T)
        dscores = (probs.astype(F32) * (dprobs - row_delta) * score_scale).astype(BF)
        grad_q = nn(dscores, key_rows).astype(BF)
        return (attended, grad_q, nn(dscores.T, query_rows), nn(probs.T, grad_out))

    attended_h, grad_q_h, key_h, value_h = lax.map(
        one_head, (query_heads, key_heads, value_heads, grad_heads)
    )
    attended_flat = attended_h.transpose(1, 0, 2).reshape(row_count, local_width)
    grad_q = grad_q_h.transpose(1, 0, 2).reshape(1, row_count, local_width)
    key_terms = key_h.transpose(1, 0, 2).reshape(key_count, local_width)
    value_terms = value_h.transpose(1, 0, 2).reshape(key_count, local_width)
    both_terms = jnp.stack([key_terms, value_terms])
    owned = lax.psum_scatter(both_terms.astype(BF), "seq", scatter_dimension=1, tiled=True)
    grad_qkv = jnp.concatenate([grad_q, owned], axis=0)
    token_count = row_count * lax.axis_size("seq") * lax.axis_size("dp")
    grad_factor = 1.0 / math.sqrt(token_count)
    terms_qkv = jnp.einsum("td,cth->cdh", normalized_rows, grad_qkv, preferred_element_type=F32)
    term_out = jnp.einsum("td,th->dh", row_gradients, attended_flat, preferred_element_type=F32)
    terms = jnp.concatenate([terms_qkv, term_out[None]], axis=0) * grad_factor
    seq_summed = lax.psum_scatter(terms.astype(BF), "seq", scatter_dimension=1, tiled=True)
    weight_grads = lax.psum_scatter(seq_summed, "dp", scatter_dimension=1, tiled=True).astype(F32)
    input_part = jnp.einsum("cth,cdh->td", grad_qkv, weights[:3], preferred_element_type=F32)
    reduced_total = lax.psum(input_part.astype(BF), "pipe").astype(F32)
    leading_term = jnp.mean(reduced_total, axis=1, keepdims=True)
    trailing_term = jnp.mean(reduced_total * standardized_input, axis=1, keepdims=True)
    input_gradient = (
        row_gradients.astype(F32)
        + inverse_deviation * (reduced_total - leading_term - standardized_input * trailing_term)
    ).astype(BF)
    return (input_gradient[None], weight_grads)


def local(embeddings, upstream, attn_weights):
    n = lax.axis_size("seq")
    heads = attn_weights.shape[2] // HD
    one_head_each = (
        heads == n
        and n == 4
        and lax.axis_size("grp") == 2
        and lax.axis_size("dp") == 2
        and lax.axis_size("pipe") == 2
        and attn_weights.shape[1] % 16 == 0
        and embeddings.shape[0] == 1
        and embeddings.shape[1] % 32 == 0
    )
    return (local_heads if one_head_each else local_gathered)(embeddings, upstream, attn_weights)


def solution(mesh):
    in_specs = (
        P(("grp", "dp"), "seq", None),
        P(("grp", "dp"), "seq", None),
        P(None, ("seq", "dp"), "pipe"),
    )
    out_specs = (P(("grp", "dp"), "seq", None), P("grp", ("seq", "dp"), "pipe"))
    return jax.shard_map(local, mesh=mesh, in_specs=in_specs, out_specs=out_specs, check_vma=False)
```

```python
import functools
import math

import jax
import jax.numpy as jnp
from jax import lax
from jax.experimental import pallas as pl
from jax.experimental.pallas import tpu as pltpu
from jax.sharding import PartitionSpec as P

HD = 104
SLOT = 128

EPSILON = 1e-06
BF = jnp.bfloat16
F32 = jnp.float32
PARAMS = pltpu.CompilerParams(vmem_limit_bytes=24 * 1024 * 1024)
VMEM_SPEC = pl.BlockSpec(memory_space=pltpu.VMEM)
ANY_SPEC = pl.BlockSpec(memory_space=pl.ANY)


def standardize(features):
    row_mean = jnp.mean(features, axis=1, keepdims=True)
    mean_removed = features - row_mean
    variance = jnp.mean(mean_removed * mean_removed, axis=1, keepdims=True)
    inverse_deviation = lax.rsqrt(variance + EPSILON)
    return mean_removed * inverse_deviation, inverse_deviation


def nt(a, b):
    return lax.dot_general(a, b, (((1,), (1,)), ((), ())), preferred_element_type=F32)


def tn(a, b):
    return lax.dot_general(a, b, (((0,), (0,)), ((), ())), preferred_element_type=F32)


def nn(a, b):
    return jnp.dot(a, b, preferred_element_type=F32)


SPARE = SLOT - HD
ORDER = (0, 2, 3, 1)
LEFT = HD - 3 * SPARE
FOLD = SLOT // LEFT


def packed_rows(share):
    group = -(-share // (16 * FOLD)) * 16
    return 3 * share + group


def half_rows(share):
    return -(-packed_rows(share) // 32) * 16


def packed(mats):
    last = mats[3]
    share = last.shape[0]
    group = packed_rows(share) - 3 * share
    tiles = [
        jnp.concatenate([mats[j], last[:, j * SPARE : (j + 1) * SPARE]], axis=1) for j in range(3)
    ]
    tail = last[:, 3 * SPARE :]
    fill = jnp.zeros((FOLD * group - share, LEFT), BF)
    columns = [tail[j * group : (j + 1) * group] for j in range(FOLD - 1)]
    columns.append(jnp.concatenate([tail[(FOLD - 1) * group :], fill], axis=0))
    return tiles + [jnp.concatenate(columns, axis=1)]


def unpacked(ref, share):
    tiles = [ref[j * share : (j + 1) * share, :] for j in range(3)]
    rest = ref[3 * share :, :]
    group = rest.shape[0]
    columns = [rest[:, j * LEFT : (j + 1) * LEFT] for j in range(FOLD)]
    columns[-1] = columns[-1][: share - (FOLD - 1) * group]
    last = [tile[:, HD:] for tile in tiles] + [jnp.concatenate(columns, axis=0)]
    return [tile[:, :HD] for tile in tiles] + [jnp.concatenate(last, axis=1)]


def pack_kernel(n, w_ref, *refs):
    outs, staged = refs[:n], refs[n]
    me = lax.axis_index("seq")
    group = lax.axis_index("grp")
    share = w_ref.shape[1]
    count = outs[0].shape[0]
    for head in range(n):
        mats = [w_ref[mat, :, head * HD : (head + 1) * HD] for mat in range(4)]
        for j, tile in enumerate(packed(mats)):
            staged[head, j * share : j * share + tile.shape[0], :] = tile
    first = pl.multiple_of(group * (staged.shape[1] - count), 16)
    for out, k in zip(outs, ORDER):
        out[...] = staged[me ^ k, pl.ds(first, count), :]


def weights_kernel(n, share, *refs):
    pieces, w_ref, staged = refs[:4], refs[4], refs[5]
    me = lax.axis_index("seq")
    image = lax.axis_index("dp")
    group = lax.axis_index("grp")
    count = pieces[0].shape[0] // n
    fill = jnp.zeros((share, SPARE), BF)
    for k in range(n):
        for other in range(2):
            for piece, at in ((pieces[other], group), (pieces[2 + other], 1 - group)):
                first = pl.multiple_of(at * (staged.shape[1] - count), 16)
                staged[2 * k + other, pl.ds(first, count), :] = piece[k * count : (k + 1) * count]
            at = 1 - image if other else image
            span = pl.ds(pl.multiple_of(((me ^ k) * 2 + at) * share, 16), share)
            for mat, block in enumerate(unpacked(staged.at[2 * k + other], share)):
                w_ref[span, mat * SLOT : (mat + 1) * SLOT] = jnp.concatenate([block, fill], axis=1)


def norm_kernel(x_ref, up_ref, send_ref, rest_ref, staged):
    core = lax.axis_index("pipe")
    half = x_ref.shape[0] // 2
    staged[...] = standardize(x_ref[...].astype(F32))[0].astype(BF)
    for target, at in ((send_ref, core), (rest_ref, 1 - core)):
        span = pl.ds(pl.multiple_of(at * half, half), half)
        target[:half] = staged[span, :]
        target[half:] = up_ref[span, :]


def merge_kernel(*refs):
    share = refs[0].shape[0]
    for k, ref in zip(ORDER, refs[:-1]):
        refs[-1][k * share : (k + 1) * share] = ref[...]


def project(x, up, w_ref):
    return [
        nn(x, w_ref[:, : 3 * SLOT]).astype(BF),
        nn(up, w_ref[:, 3 * SLOT :]).astype(BF),
    ]


def place(row, sides, x_ref, up_ref):
    half = sides[0].shape[0] // 2
    for side, source in enumerate(sides):
        span = slice(row + side * half, row + (side + 1) * half)
        x_ref[span, :] = source[:half, :]
        up_ref[span, :] = source[half:, :]


def project_kernel(n, *refs):
    w_ref, x_ref, up_ref, made_ref = refs[2 * n - 2 :]
    rows = refs[0].shape[0]
    for k in range(n - 1):
        place(k * rows, refs[2 * k : 2 * k + 2], x_ref, up_ref)
    made_ref[:, : 3 * SLOT], made_ref[:, 3 * SLOT :] = project(x_ref[...], up_ref[...], w_ref)


def head_kernel(n, *refs):
    middle, passed = refs[:2], refs[2:4]
    made_ref, w_ref, keep_ref, give_ref, grads, x_ref, up_ref = refs[4:11]
    made, term_k, term_v = refs[11:]
    me = lax.axis_index("seq")
    rows = x_ref.shape[0]
    half = rows // 2
    ready = (n - 1) * rows

    @pl.when((me == 0) | (me == n - 1))
    def _():
        place(0, passed, x_ref, up_ref)

    @pl.when((me != 0) & (me != n - 1))
    def _():
        place(0, middle, x_ref, up_ref)

    made[:ready, :] = made_ref[...]
    made[ready:, : 3 * SLOT], made[ready:, 3 * SLOT :] = project(x_ref[...], up_ref[...], w_ref)
    scale = HD ** (-0.5)
    key_rows = made[:, SLOT : 2 * SLOT]
    value_rows = made[:, 2 * SLOT : 3 * SLOT]
    for b in range(n):
        span = slice(b * rows, (b + 1) * rows)
        query = made[span, :SLOT]
        grad_out = made[span, 3 * SLOT :]
        scores = nt(query, key_rows) * scale
        weight = jnp.exp(scores - jnp.max(scores, axis=1, keepdims=True))
        probs = (weight / jnp.sum(weight, axis=1, keepdims=True)).astype(BF)
        attended = nn(probs, value_rows).astype(BF)
        delta = jnp.sum(grad_out.astype(F32) * attended.astype(F32), axis=1, keepdims=True)
        dprobs = nt(grad_out, value_rows)
        dscores = (probs.astype(F32) * (dprobs - delta) * scale).astype(BF)
        grads[span, :SLOT] = nn(dscores, key_rows).astype(BF)
        grads[span, 3 * SLOT :] = attended
        key_term = tn(dscores, query).astype(BF).astype(F32)
        value_term = tn(probs, grad_out).astype(BF).astype(F32)
        if b == 0:
            term_k[...] = key_term
            term_v[...] = value_term
        else:
            term_k[...] += key_term
            term_v[...] += value_term
    grads[:, SLOT : 2 * SLOT] = term_k[...].astype(BF)
    grads[:, 2 * SLOT : 3 * SLOT] = term_v[...].astype(BF)
    for b in range(n):
        span = slice(b * rows, (b + 1) * rows)
        part = nt(grads[span, : 3 * SLOT], w_ref[:, : 3 * SLOT]).astype(BF)
        keep_ref[b] = part[:half]
        give_ref[b] = part[half:]


def weight_kernel(n, factor, x_ref, x_last, up_ref, up_last, grads, keep_ref, give_ref, staged):
    me = lax.axis_index("seq")
    image = lax.axis_index("dp")
    ready = x_ref.shape[0]
    share = staged.shape[0] // (2 * n)
    for lanes, first, last in (
        (slice(0, 3 * SLOT), x_ref, x_last),
        (slice(3 * SLOT, 4 * SLOT), up_ref, up_last),
    ):
        total = tn(first[...], grads[:ready, lanes]) + tn(last[...], grads[ready:, lanes])
        staged[:, lanes] = (total * factor).astype(BF)
    for k in range(n):
        for target, at in ((keep_ref, image), (give_ref, 1 - image)):
            first = pl.multiple_of(((me ^ k) * 2 + at) * share, 16)
            mats = [
                staged[pl.ds(first, share), mat * SLOT : mat * SLOT + HD] for mat in range(4)
            ]
            for j, tile in enumerate(packed(mats)):
                target[k, j * share : j * share + tile.shape[0], :] = tile


def sum_kernel(mine_ref, theirs_ref, *outs):
    for out, k in zip(outs, ORDER):
        out[...] = (mine_ref[k].astype(F32) + theirs_ref[k].astype(F32)).astype(BF)


def final_kernel(n, x_ref, up_ref, *refs):
    parts, (out_ref, rest_ref) = refs[:n], refs[n:]
    half = 2 * out_ref.shape[0]
    core = lax.axis_index("pipe")
    span = pl.ds(pl.multiple_of(core * half, half), half)
    total = parts[0][...].astype(F32)
    for part in parts[1:]:
        total += part[...].astype(F32)
    xhat, inverse_deviation = standardize(x_ref[span, :].astype(F32))
    leading = jnp.mean(total, axis=1, keepdims=True)
    trailing = jnp.mean(total * xhat, axis=1, keepdims=True)
    result = (
        up_ref[span, :].astype(F32) + inverse_deviation * (total - leading - xhat * trailing)
    ).astype(BF)
    out_ref[...] = result[: half // 2]
    rest_ref[...] = result[half // 2 :]


def join_kernel(n, *refs):
    pairs, parts, (input_ref, out_ref, staged) = refs[:4], refs[4 : 4 + n], refs[4 + n :]
    me = lax.axis_index("seq")
    core = lax.axis_index("pipe")
    count = pairs[0].shape[0]
    for i, ref in enumerate(pairs):
        side = core if i < 2 else 1 - core
        first = pl.multiple_of((2 * side + i % 2) * count, count)
        input_ref[pl.ds(first, count), :] = ref[...]
    for part, k in zip(parts, ORDER):
        staged[me ^ k] = part[...]
    for head in range(n):
        for mat, block in enumerate(unpacked(staged.at[head], out_ref.shape[1])):
            out_ref[mat, :, head * HD : (head + 1) * HD] = block.astype(F32)


def call(kernel, out_shape, args, scratch=(), plain=0, out_space=pltpu.VMEM):
    single = not isinstance(out_shape, list)
    shapes = [out_shape] if single else out_shape
    args = list(args[:plain]) + [
        pltpu.with_memory_space_constraint(a, pltpu.VMEM) for a in args[plain:]
    ]
    out = pl.pallas_call(
        kernel,
        out_shape=[out_space(*s) for s in shapes],
        in_specs=[VMEM_SPEC] * len(args),
        out_specs=[VMEM_SPEC] * len(shapes),
        scratch_shapes=list(scratch),
        compiler_params=PARAMS,
    )(*args)
    return out[0] if single else list(out)


def local_heads(embeddings, upstream, attn_weights):
    n = lax.axis_size("seq")
    x, up = embeddings[0], upstream[0]
    rows, width = x.shape
    share = attn_weights.shape[1]
    patches = n * rows
    half = rows // 2
    me = lax.axis_index("seq")

    def across(value, k):
        return lax.ppermute(value, "seq", [(i, i ^ k) for i in range(n)])

    def exchange(values):
        return [across(value, k) for value, k in zip(values[1:], ORDER[1:])]

    def swap(value, axis):
        return lax.ppermute(value, axis, [(0, 1), (1, 0)])


    full, count = packed_rows(share), half_rows(share)
    chunks = call(
        functools.partial(pack_kernel, n),
        [((count, SLOT), BF)] * n,
        (attn_weights,),
        [pltpu.VMEM((n, full, SLOT), BF)],
        plain=1,
    )
    arrived = exchange(chunks)
    send, rest = call(
        norm_kernel, [((rows, width), BF)] * 2, (x, up), [pltpu.VMEM((rows, width), BF)], plain=2
    )
    merged = call(merge_kernel, ((n * count, SLOT), BF), (chunks[0], *arrived))
    beside = swap(merged, "dp")
    above = swap(merged, "grp")
    second = across(send, 2)
    first = across(send, 1)
    later, first, second, beside, above = lax.optimization_barrier(
        (send, first, second, beside, above)
    )
    corner = swap(above, "dp")
    weights = call(
        functools.partial(weights_kernel, n, share),
        ((width, 4 * SLOT), BF),
        (merged, beside, above, corner),
        [pltpu.VMEM((2 * n, full, SLOT), BF)],
    )
    middle = lax.ppermute(later, "seq", [(1, 2), (2, 1)])
    passed = lax.ppermute(second, "seq", [(2, 3), (1, 0)])
    weights, middle, passed = lax.optimization_barrier((weights, middle, passed))
    ready = patches - rows
    x_head, up_head, made = call(
        functools.partial(project_kernel, n),
        [((ready, width), BF)] * 2 + [((ready, 4 * SLOT), BF)],
        (send, rest, first, swap(first, "pipe"), second, swap(second, "pipe"), weights),
    )
    keep, give, grads, x_last, up_last = call(
        functools.partial(head_kernel, n),
        [((n, half, width), BF)] * 2 + [((patches, 4 * SLOT), BF)] + [((rows, width), BF)] * 2,
        (middle, swap(middle, "pipe"), passed, swap(passed, "pipe"), made, weights),
        [
            pltpu.VMEM((patches, 4 * SLOT), BF),
            pltpu.VMEM((patches, SLOT), F32),
            pltpu.VMEM((patches, SLOT), F32),
        ],
    )
    factor = 1.0 / math.sqrt(patches * lax.axis_size("dp"))
    w_keep, w_give = call(
        functools.partial(weight_kernel, n, factor),
        [((n, full, SLOT), BF)] * 2,
        (x_head, x_last, up_head, up_last, grads),
        [pltpu.VMEM((width, 4 * SLOT), BF)],
    )
    taken = swap(give, "pipe")
    w_taken = swap(w_give, "dp")
    sums = call(sum_kernel, [((half, width), BF)] * n, (keep, taken))
    parts = exchange(sums)
    w_taken, sums[0] = lax.optimization_barrier((w_taken, sums[0]))
    w_sums = call(
        sum_kernel, [((full, SLOT), BF)] * n, (w_keep, w_taken)
    )
    w_parts = [w_sums[0]] + exchange(w_sums)
    mine = call(
        functools.partial(final_kernel, n),
        [((half // 2, width), BF)] * 2,
        (x, up, sums[0], *parts),
        plain=2,
    )
    input_gradient, weight_grads = call(
        functools.partial(join_kernel, n),
        [((rows, width), BF), ((4, share, n * HD), F32)],
        (*mine, *[swap(m, "pipe") for m in mine], *w_parts),
        [pltpu.VMEM((n, full, SLOT), BF)],
        out_space=jax.ShapeDtypeStruct,
    )
    return (input_gradient[None], weight_grads)


def local_gathered(embeddings, upstream, attn_weights):
    tokens = embeddings[0]
    row_gradients = upstream[0]
    row_count = tokens.shape[0]
    weights = lax.all_gather(attn_weights, ("seq", "dp"), axis=1, tiled=True)
    local_width = weights.shape[2]
    head_count = local_width // HD
    score_scale = HD ** (-0.5)
    standardized_input, inverse_deviation = standardize(tokens.astype(F32))
    normalized_rows = standardized_input.astype(BF)
    proj = jnp.einsum(
        "td,cdh->cth", normalized_rows, weights[:3], preferred_element_type=F32
    ).astype(BF)
    gathered = lax.all_gather(proj[1:], "seq", axis=1, tiled=True)
    key_count = gathered.shape[1]
    query_heads = proj[0].reshape(row_count, head_count, HD).transpose(1, 0, 2)
    key_heads = gathered[0].reshape(key_count, head_count, HD).transpose(1, 0, 2)
    value_heads = gathered[1].reshape(key_count, head_count, HD).transpose(1, 0, 2)
    grad_att = jnp.dot(row_gradients, weights[3], preferred_element_type=F32).astype(BF)
    grad_heads = grad_att.reshape(row_count, head_count, HD).transpose(1, 0, 2)

    def one_head(items):
        query_rows, key_rows, value_rows, grad_out = items
        scores = nn(query_rows, key_rows.T) * score_scale
        row_max = jnp.max(scores, axis=1, keepdims=True)
        log_total = row_max + jnp.log(jnp.sum(jnp.exp(scores - row_max), axis=1, keepdims=True))
        probs = jnp.exp(scores - log_total).astype(BF)
        attended = nn(probs, value_rows).astype(BF)
        row_delta = jnp.sum(
            grad_out.astype(F32) * attended.astype(F32), axis=1, keepdims=True
        )
        dprobs = nn(grad_out, value_rows.T)
        dscores = (probs.astype(F32) * (dprobs - row_delta) * score_scale).astype(BF)
        grad_q = nn(dscores, key_rows).astype(BF)
        return (attended, grad_q, nn(dscores.T, query_rows), nn(probs.T, grad_out))

    attended_h, grad_q_h, key_h, value_h = lax.map(
        one_head, (query_heads, key_heads, value_heads, grad_heads)
    )
    attended_flat = attended_h.transpose(1, 0, 2).reshape(row_count, local_width)
    grad_q = grad_q_h.transpose(1, 0, 2).reshape(1, row_count, local_width)
    key_terms = key_h.transpose(1, 0, 2).reshape(key_count, local_width)
    value_terms = value_h.transpose(1, 0, 2).reshape(key_count, local_width)
    both_terms = jnp.stack([key_terms, value_terms])
    owned = lax.psum_scatter(both_terms.astype(BF), "seq", scatter_dimension=1, tiled=True)
    grad_qkv = jnp.concatenate([grad_q, owned], axis=0)
    token_count = row_count * lax.axis_size("seq") * lax.axis_size("dp")
    grad_factor = 1.0 / math.sqrt(token_count)
    terms_qkv = jnp.einsum("td,cth->cdh", normalized_rows, grad_qkv, preferred_element_type=F32)
    term_out = jnp.einsum("td,th->dh", row_gradients, attended_flat, preferred_element_type=F32)
    terms = jnp.concatenate([terms_qkv, term_out[None]], axis=0) * grad_factor
    seq_summed = lax.psum_scatter(terms.astype(BF), "seq", scatter_dimension=1, tiled=True)
    weight_grads = lax.psum_scatter(seq_summed, "dp", scatter_dimension=1, tiled=True).astype(F32)
    input_part = jnp.einsum("cth,cdh->td", grad_qkv, weights[:3], preferred_element_type=F32)
    reduced_total = lax.psum(input_part.astype(BF), "pipe").astype(F32)
    leading_term = jnp.mean(reduced_total, axis=1, keepdims=True)
    trailing_term = jnp.mean(reduced_total * standardized_input, axis=1, keepdims=True)
    input_gradient = (
        row_gradients.astype(F32)
        + inverse_deviation * (reduced_total - leading_term - standardized_input * trailing_term)
    ).astype(BF)
    return (input_gradient[None], weight_grads)


def local(embeddings, upstream, attn_weights):
    n = lax.axis_size("seq")
    heads = attn_weights.shape[2] // HD
    one_head_each = (
        heads == n
        and n == 4
        and lax.axis_size("grp") == 2
        and lax.axis_size("dp") == 2
        and lax.axis_size("pipe") == 2
        and attn_weights.shape[1] % 16 == 0
        and embeddings.shape[0] == 1
        and embeddings.shape[1] % 32 == 0
    )
    return (local_heads if one_head_each else local_gathered)(embeddings, upstream, attn_weights)


def solution(mesh):
    in_specs = (
        P(("grp", "dp"), "seq", None),
        P(("grp", "dp"), "seq", None),
        P(None, ("seq", "dp"), "pipe"),
    )
    out_specs = (P(("grp", "dp"), "seq", None), P("grp", ("seq", "dp"), "pipe"))
    return jax.shard_map(local, mesh=mesh, in_specs=in_specs, out_specs=out_specs, check_vma=False)
```

```python
import functools
import math

import jax
import jax.numpy as jnp
from jax import lax
from jax.experimental import pallas as pl
from jax.experimental.pallas import tpu as pltpu
from jax.sharding import PartitionSpec as P

HD = 104
SLOT = 128

EPSILON = 1e-06
BF = jnp.bfloat16
F32 = jnp.float32
PARAMS = pltpu.CompilerParams(vmem_limit_bytes=24 * 1024 * 1024)
VMEM_SPEC = pl.BlockSpec(memory_space=pltpu.VMEM)
ANY_SPEC = pl.BlockSpec(memory_space=pl.ANY)


def standardize(features):
    row_mean = jnp.mean(features, axis=1, keepdims=True)
    mean_removed = features - row_mean
    variance = jnp.mean(mean_removed * mean_removed, axis=1, keepdims=True)
    inverse_deviation = lax.rsqrt(variance + EPSILON)
    return mean_removed * inverse_deviation, inverse_deviation


def nt(a, b):
    return lax.dot_general(a, b, (((1,), (1,)), ((), ())), preferred_element_type=F32)


def tn(a, b):
    return lax.dot_general(a, b, (((0,), (0,)), ((), ())), preferred_element_type=F32)


def nn(a, b):
    return jnp.dot(a, b, preferred_element_type=F32)


SPARE = SLOT - HD
ORDER = (0, 2, 3, 1)
LEFT = HD - 3 * SPARE
FOLD = SLOT // LEFT


def packed_rows(share):
    group = -(-share // (16 * FOLD)) * 16
    return 3 * share + group


def half_rows(share):
    return -(-packed_rows(share) // 32) * 16


def packed(mats):
    last = mats[3]
    share = last.shape[0]
    group = packed_rows(share) - 3 * share
    tiles = [
        jnp.concatenate([mats[j], last[:, j * SPARE : (j + 1) * SPARE]], axis=1) for j in range(3)
    ]
    tail = last[:, 3 * SPARE :]
    fill = jnp.zeros((FOLD * group - share, LEFT), BF)
    columns = [tail[j * group : (j + 1) * group] for j in range(FOLD - 1)]
    columns.append(jnp.concatenate([tail[(FOLD - 1) * group :], fill], axis=0))
    return tiles + [jnp.concatenate(columns, axis=1)]


def unpacked(ref, share):
    tiles = [ref[j * share : (j + 1) * share, :] for j in range(3)]
    rest = ref[3 * share :, :]
    group = rest.shape[0]
    columns = [rest[:, j * LEFT : (j + 1) * LEFT] for j in range(FOLD)]
    columns[-1] = columns[-1][: share - (FOLD - 1) * group]
    last = [tile[:, HD:] for tile in tiles] + [jnp.concatenate(columns, axis=0)]
    return [tile[:, :HD] for tile in tiles] + [jnp.concatenate(last, axis=1)]


def pack_kernel(n, w_ref, *refs):
    outs, staged = refs[:n], refs[n]
    me = lax.axis_index("seq")
    group = lax.axis_index("grp")
    share = w_ref.shape[1]
    count = outs[0].shape[0]
    for head in range(n):
        mats = [w_ref[mat, :, head * HD : (head + 1) * HD] for mat in range(4)]
        for j, tile in enumerate(packed(mats)):
            staged[head, j * share : j * share + tile.shape[0], :] = tile
    first = pl.multiple_of(group * (staged.shape[1] - count), 16)
    for k, out in enumerate(outs):
        out[...] = staged[me ^ k, pl.ds(first, count), :]


def weights_kernel(n, share, *refs):
    pieces, w_ref, staged = refs[:4], refs[4], refs[5]
    me = lax.axis_index("seq")
    image = lax.axis_index("dp")
    group = lax.axis_index("grp")
    count = pieces[0].shape[0] // n
    fill = jnp.zeros((share, SPARE), BF)
    for k in range(n):
        for other in range(2):
            for piece, at in ((pieces[other], group), (pieces[2 + other], 1 - group)):
                first = pl.multiple_of(at * (staged.shape[1] - count), 16)
                staged[2 * k + other, pl.ds(first, count), :] = piece[k * count : (k + 1) * count]
            at = 1 - image if other else image
            span = pl.ds(pl.multiple_of(((me ^ k) * 2 + at) * share, 16), share)
            for mat, block in enumerate(unpacked(staged.at[2 * k + other], share)):
                w_ref[span, mat * SLOT : (mat + 1) * SLOT] = jnp.concatenate([block, fill], axis=1)


def norm_kernel(x_ref, up_ref, send_ref, rest_ref, staged):
    core = lax.axis_index("pipe")
    half = x_ref.shape[0] // 2
    staged[...] = standardize(x_ref[...].astype(F32))[0].astype(BF)
    for target, at in ((send_ref, core), (rest_ref, 1 - core)):
        span = pl.ds(pl.multiple_of(at * half, half), half)
        target[:half] = staged[span, :]
        target[half:] = up_ref[span, :]


def merge_kernel(*refs):
    share = refs[0].shape[0]
    for k, ref in enumerate(refs[:-1]):
        refs[-1][k * share : (k + 1) * share] = ref[...]


def project(x, up, w_ref):
    return [
        nn(x, w_ref[:, : 3 * SLOT]).astype(BF),
        nn(up, w_ref[:, 3 * SLOT :]).astype(BF),
    ]


def place(row, sides, x_ref, up_ref):
    half = sides[0].shape[0] // 2
    for side, source in enumerate(sides):
        span = slice(row + side * half, row + (side + 1) * half)
        x_ref[span, :] = source[:half, :]
        up_ref[span, :] = source[half:, :]


def project_kernel(n, *refs):
    w_ref, x_ref, up_ref, made_ref = refs[2 * n - 2 :]
    rows = refs[0].shape[0]
    for k in range(n - 1):
        place(k * rows, refs[2 * k : 2 * k + 2], x_ref, up_ref)
    made_ref[:, : 3 * SLOT], made_ref[:, 3 * SLOT :] = project(x_ref[...], up_ref[...], w_ref)


def head_kernel(n, *refs):
    middle, passed = refs[:2], refs[2:4]
    made_ref, w_ref, keep_ref, give_ref, grads, x_ref, up_ref = refs[4:11]
    made, term_k, term_v = refs[11:]
    me = lax.axis_index("seq")
    rows = x_ref.shape[0]
    half = rows // 2
    ready = (n - 1) * rows

    @pl.when((me == 0) | (me == n - 1))
    def _():
        place(0, passed, x_ref, up_ref)

    @pl.when((me != 0) & (me != n - 1))
    def _():
        place(0, middle, x_ref, up_ref)

    made[:ready, :] = made_ref[...]
    made[ready:, : 3 * SLOT], made[ready:, 3 * SLOT :] = project(x_ref[...], up_ref[...], w_ref)
    scale = HD ** (-0.5)
    key_rows = made[:, SLOT : 2 * SLOT]
    value_rows = made[:, 2 * SLOT : 3 * SLOT]
    grad_out_all = made[:, 3 * SLOT :]
    scores = nt(made[:, :SLOT], key_rows) * scale
    weight = jnp.exp(scores - jnp.max(scores, axis=1, keepdims=True))
    probs_all = (weight / jnp.sum(weight, axis=1, keepdims=True)).astype(BF)
    attended = nn(probs_all, value_rows).astype(BF)
    delta = jnp.sum(grad_out_all.astype(F32) * attended.astype(F32), axis=1, keepdims=True)
    dprobs = nt(grad_out_all, value_rows)
    dscores_all = (probs_all.astype(F32) * (dprobs - delta) * scale).astype(BF)
    grads[:, :SLOT] = nn(dscores_all, key_rows).astype(BF)
    grads[:, 3 * SLOT :] = attended
    for b in range(n):
        span = slice(b * rows, (b + 1) * rows)
        key_term = tn(dscores_all[span], made[span, :SLOT]).astype(BF).astype(F32)
        value_term = tn(probs_all[span], made[span, 3 * SLOT :]).astype(BF).astype(F32)
        if b == 0:
            term_k[...] = key_term
            term_v[...] = value_term
        else:
            term_k[...] += key_term
            term_v[...] += value_term
    grads[:, SLOT : 2 * SLOT] = term_k[...].astype(BF)
    grads[:, 2 * SLOT : 3 * SLOT] = term_v[...].astype(BF)
    whole = nt(grads[:, : 3 * SLOT], w_ref[:, : 3 * SLOT]).astype(BF)
    for b in range(n):
        part = whole[b * rows : (b + 1) * rows]
        keep_ref[b] = part[:half]
        give_ref[b] = part[half:]


def weight_kernel(n, factor, x_ref, x_last, up_ref, up_last, grads, keep_ref, give_ref, staged):
    me = lax.axis_index("seq")
    image = lax.axis_index("dp")
    ready = x_ref.shape[0]
    share = staged.shape[0] // (2 * n)
    for lanes, first, last in (
        (slice(0, 3 * SLOT), x_ref, x_last),
        (slice(3 * SLOT, 4 * SLOT), up_ref, up_last),
    ):
        total = tn(first[...], grads[:ready, lanes]) + tn(last[...], grads[ready:, lanes])
        staged[:, lanes] = (total * factor).astype(BF)
    for k in range(n):
        for target, at in ((keep_ref, image), (give_ref, 1 - image)):
            first = pl.multiple_of(((me ^ k) * 2 + at) * share, 16)
            mats = [
                staged[pl.ds(first, share), mat * SLOT : mat * SLOT + HD] for mat in range(4)
            ]
            for j, tile in enumerate(packed(mats)):
                target[k, j * share : j * share + tile.shape[0], :] = tile


def sum_kernel(mine_ref, theirs_ref, *outs):
    for out, k in zip(outs, ORDER):
        out[...] = (mine_ref[k].astype(F32) + theirs_ref[k].astype(F32)).astype(BF)


def final_kernel(n, x_ref, up_ref, *refs):
    parts, (out_ref, rest_ref) = refs[:n], refs[n:]
    half = 2 * out_ref.shape[0]
    core = lax.axis_index("pipe")
    span = pl.ds(pl.multiple_of(core * half, half), half)
    total = parts[0][...].astype(F32)
    for part in parts[1:]:
        total += part[...].astype(F32)
    xhat, inverse_deviation = standardize(x_ref[span, :].astype(F32))
    leading = jnp.mean(total, axis=1, keepdims=True)
    trailing = jnp.mean(total * xhat, axis=1, keepdims=True)
    result = (
        up_ref[span, :].astype(F32) + inverse_deviation * (total - leading - xhat * trailing)
    ).astype(BF)
    out_ref[...] = result[: half // 2]
    rest_ref[...] = result[half // 2 :]


def join_kernel(n, *refs):
    pairs, parts, (input_ref, out_ref, staged) = refs[:4], refs[4 : 4 + n], refs[4 + n :]
    me = lax.axis_index("seq")
    core = lax.axis_index("pipe")
    count = pairs[0].shape[0]
    for i, ref in enumerate(pairs):
        side = core if i < 2 else 1 - core
        first = pl.multiple_of((2 * side + i % 2) * count, count)
        input_ref[pl.ds(first, count), :] = ref[...]
    for part, k in zip(parts, ORDER):
        staged[me ^ k] = part[...]
    for head in range(n):
        for mat, block in enumerate(unpacked(staged.at[head], out_ref.shape[1])):
            out_ref[mat, :, head * HD : (head + 1) * HD] = block.astype(F32)


def call(kernel, out_shape, args, scratch=(), plain=0, out_space=pltpu.VMEM):
    single = not isinstance(out_shape, list)
    shapes = [out_shape] if single else out_shape
    args = list(args[:plain]) + [
        pltpu.with_memory_space_constraint(a, pltpu.VMEM) for a in args[plain:]
    ]
    out = pl.pallas_call(
        kernel,
        out_shape=[out_space(*s) for s in shapes],
        in_specs=[VMEM_SPEC] * len(args),
        out_specs=[VMEM_SPEC] * len(shapes),
        scratch_shapes=list(scratch),
        compiler_params=PARAMS,
    )(*args)
    return out[0] if single else list(out)


def local_heads(embeddings, upstream, attn_weights):
    n = lax.axis_size("seq")
    x, up = embeddings[0], upstream[0]
    rows, width = x.shape
    share = attn_weights.shape[1]
    patches = n * rows
    half = rows // 2
    me = lax.axis_index("seq")

    def across(value, k):
        return lax.ppermute(value, "seq", [(i, i ^ k) for i in range(n)])

    def exchange(values):
        return [across(value, k) for value, k in zip(values[1:], ORDER[1:])]

    def swap(value, axis):
        return lax.ppermute(value, axis, [(0, 1), (1, 0)])


    full, count = packed_rows(share), half_rows(share)
    chunks = call(
        functools.partial(pack_kernel, n),
        [((count, SLOT), BF)] * n,
        (attn_weights,),
        [pltpu.VMEM((n, full, SLOT), BF)],
        plain=1,
    )
    arrived = [across(chunks[k], k) for k in range(1, n)]
    send, rest = call(
        norm_kernel, [((rows, width), BF)] * 2, (x, up), [pltpu.VMEM((rows, width), BF)], plain=2
    )
    send, arrived[0] = lax.optimization_barrier((send, arrived[0]))
    merged = call(merge_kernel, ((n * count, SLOT), BF), (chunks[0], *arrived))
    beside = swap(merged, "dp")
    above = swap(merged, "grp")
    second = across(send, 2)
    first = across(send, 1)
    later, first, second, beside, above = lax.optimization_barrier(
        (send, first, second, beside, above)
    )
    corner = swap(above, "dp")
    weights = call(
        functools.partial(weights_kernel, n, share),
        ((width, 4 * SLOT), BF),
        (merged, beside, above, corner),
        [pltpu.VMEM((2 * n, full, SLOT), BF)],
    )
    middle = lax.ppermute(later, "seq", [(1, 2), (2, 1)])
    passed = lax.ppermute(second, "seq", [(2, 3), (1, 0)])
    weights, middle, passed = lax.optimization_barrier((weights, middle, passed))
    ready = patches - rows
    x_head, up_head, made = call(
        functools.partial(project_kernel, n),
        [((ready, width), BF)] * 2 + [((ready, 4 * SLOT), BF)],
        (send, rest, first, swap(first, "pipe"), second, swap(second, "pipe"), weights),
    )
    keep, give, grads, x_last, up_last = call(
        functools.partial(head_kernel, n),
        [((n, half, width), BF)] * 2 + [((patches, 4 * SLOT), BF)] + [((rows, width), BF)] * 2,
        (middle, swap(middle, "pipe"), passed, swap(passed, "pipe"), made, weights),
        [
            pltpu.VMEM((patches, 4 * SLOT), BF),
            pltpu.VMEM((patches, SLOT), F32),
            pltpu.VMEM((patches, SLOT), F32),
        ],
    )
    factor = 1.0 / math.sqrt(patches * lax.axis_size("dp"))
    w_keep, w_give = call(
        functools.partial(weight_kernel, n, factor),
        [((n, full, SLOT), BF)] * 2,
        (x_head, x_last, up_head, up_last, grads),
        [pltpu.VMEM((width, 4 * SLOT), BF)],
    )
    taken = swap(give, "pipe")
    w_taken = swap(w_give, "dp")
    sums = call(sum_kernel, [((half, width), BF)] * n, (keep, taken))
    parts = exchange(sums)
    w_taken, sums[0] = lax.optimization_barrier((w_taken, sums[0]))
    w_sums = call(
        sum_kernel, [((full, SLOT), BF)] * n, (w_keep, w_taken)
    )
    w_parts = [w_sums[0]] + exchange(w_sums)
    mine = call(
        functools.partial(final_kernel, n),
        [((half // 2, width), BF)] * 2,
        (x, up, sums[0], *parts),
        plain=2,
    )
    input_gradient, weight_grads = call(
        functools.partial(join_kernel, n),
        [((rows, width), BF), ((4, share, n * HD), F32)],
        (*mine, *[swap(m, "pipe") for m in mine], *w_parts),
        [pltpu.VMEM((n, full, SLOT), BF)],
        out_space=jax.ShapeDtypeStruct,
    )
    return (input_gradient[None], weight_grads)


def local_gathered(embeddings, upstream, attn_weights):
    tokens = embeddings[0]
    row_gradients = upstream[0]
    row_count = tokens.shape[0]
    weights = lax.all_gather(attn_weights, ("seq", "dp"), axis=1, tiled=True)
    local_width = weights.shape[2]
    head_count = local_width // HD
    score_scale = HD ** (-0.5)
    standardized_input, inverse_deviation = standardize(tokens.astype(F32))
    normalized_rows = standardized_input.astype(BF)
    proj = jnp.einsum(
        "td,cdh->cth", normalized_rows, weights[:3], preferred_element_type=F32
    ).astype(BF)
    gathered = lax.all_gather(proj[1:], "seq", axis=1, tiled=True)
    key_count = gathered.shape[1]
    query_heads = proj[0].reshape(row_count, head_count, HD).transpose(1, 0, 2)
    key_heads = gathered[0].reshape(key_count, head_count, HD).transpose(1, 0, 2)
    value_heads = gathered[1].reshape(key_count, head_count, HD).transpose(1, 0, 2)
    grad_att = jnp.dot(row_gradients, weights[3], preferred_element_type=F32).astype(BF)
    grad_heads = grad_att.reshape(row_count, head_count, HD).transpose(1, 0, 2)

    def one_head(items):
        query_rows, key_rows, value_rows, grad_out = items
        scores = nn(query_rows, key_rows.T) * score_scale
        row_max = jnp.max(scores, axis=1, keepdims=True)
        log_total = row_max + jnp.log(jnp.sum(jnp.exp(scores - row_max), axis=1, keepdims=True))
        probs = jnp.exp(scores - log_total).astype(BF)
        attended = nn(probs, value_rows).astype(BF)
        row_delta = jnp.sum(
            grad_out.astype(F32) * attended.astype(F32), axis=1, keepdims=True
        )
        dprobs = nn(grad_out, value_rows.T)
        dscores = (probs.astype(F32) * (dprobs - row_delta) * score_scale).astype(BF)
        grad_q = nn(dscores, key_rows).astype(BF)
        return (attended, grad_q, nn(dscores.T, query_rows), nn(probs.T, grad_out))

    attended_h, grad_q_h, key_h, value_h = lax.map(
        one_head, (query_heads, key_heads, value_heads, grad_heads)
    )
    attended_flat = attended_h.transpose(1, 0, 2).reshape(row_count, local_width)
    grad_q = grad_q_h.transpose(1, 0, 2).reshape(1, row_count, local_width)
    key_terms = key_h.transpose(1, 0, 2).reshape(key_count, local_width)
    value_terms = value_h.transpose(1, 0, 2).reshape(key_count, local_width)
    both_terms = jnp.stack([key_terms, value_terms])
    owned = lax.psum_scatter(both_terms.astype(BF), "seq", scatter_dimension=1, tiled=True)
    grad_qkv = jnp.concatenate([grad_q, owned], axis=0)
    token_count = row_count * lax.axis_size("seq") * lax.axis_size("dp")
    grad_factor = 1.0 / math.sqrt(token_count)
    terms_qkv = jnp.einsum("td,cth->cdh", normalized_rows, grad_qkv, preferred_element_type=F32)
    term_out = jnp.einsum("td,th->dh", row_gradients, attended_flat, preferred_element_type=F32)
    terms = jnp.concatenate([terms_qkv, term_out[None]], axis=0) * grad_factor
    seq_summed = lax.psum_scatter(terms.astype(BF), "seq", scatter_dimension=1, tiled=True)
    weight_grads = lax.psum_scatter(seq_summed, "dp", scatter_dimension=1, tiled=True).astype(F32)
    input_part = jnp.einsum("cth,cdh->td", grad_qkv, weights[:3], preferred_element_type=F32)
    reduced_total = lax.psum(input_part.astype(BF), "pipe").astype(F32)
    leading_term = jnp.mean(reduced_total, axis=1, keepdims=True)
    trailing_term = jnp.mean(reduced_total * standardized_input, axis=1, keepdims=True)
    input_gradient = (
        row_gradients.astype(F32)
        + inverse_deviation * (reduced_total - leading_term - standardized_input * trailing_term)
    ).astype(BF)
    return (input_gradient[None], weight_grads)


def local(embeddings, upstream, attn_weights):
    n = lax.axis_size("seq")
    heads = attn_weights.shape[2] // HD
    one_head_each = (
        heads == n
        and n == 4
        and lax.axis_size("grp") == 2
        and lax.axis_size("dp") == 2
        and lax.axis_size("pipe") == 2
        and attn_weights.shape[1] % 16 == 0
        and embeddings.shape[0] == 1
        and embeddings.shape[1] % 32 == 0
    )
    return (local_heads if one_head_each else local_gathered)(embeddings, upstream, attn_weights)


def solution(mesh):
    in_specs = (
        P(("grp", "dp"), "seq", None),
        P(("grp", "dp"), "seq", None),
        P(None, ("seq", "dp"), "pipe"),
    )
    out_specs = (P(("grp", "dp"), "seq", None), P("grp", ("seq", "dp"), "pipe"))
    return jax.shard_map(local, mesh=mesh, in_specs=in_specs, out_specs=out_specs, check_vma=False)
```

```python
import functools
import math

import jax
import jax.numpy as jnp
from jax import lax
from jax.experimental import pallas as pl
from jax.experimental.pallas import tpu as pltpu
from jax.sharding import PartitionSpec as P

HD = 104
SLOT = 128

EPSILON = 1e-06
BF = jnp.bfloat16
F32 = jnp.float32
PARAMS = pltpu.CompilerParams(vmem_limit_bytes=24 * 1024 * 1024)
VMEM_SPEC = pl.BlockSpec(memory_space=pltpu.VMEM)
ANY_SPEC = pl.BlockSpec(memory_space=pl.ANY)


def standardize(features):
    row_mean = jnp.mean(features, axis=1, keepdims=True)
    mean_removed = features - row_mean
    variance = jnp.mean(mean_removed * mean_removed, axis=1, keepdims=True)
    inverse_deviation = lax.rsqrt(variance + EPSILON)
    return mean_removed * inverse_deviation, inverse_deviation


def nt(a, b):
    return lax.dot_general(a, b, (((1,), (1,)), ((), ())), preferred_element_type=F32)


def tn(a, b):
    return lax.dot_general(a, b, (((0,), (0,)), ((), ())), preferred_element_type=F32)


def nn(a, b):
    return jnp.dot(a, b, preferred_element_type=F32)


SPARE = SLOT - HD
ORDER = (0, 2, 3, 1)
LEFT = HD - 3 * SPARE
FOLD = SLOT // LEFT


def packed_rows(share):
    group = -(-share // (16 * FOLD)) * 16
    return 3 * share + group


def half_rows(share):
    return -(-packed_rows(share) // 32) * 16


def packed(mats):
    last = mats[3]
    share = last.shape[0]
    group = packed_rows(share) - 3 * share
    tiles = [
        jnp.concatenate([mats[j], last[:, j * SPARE : (j + 1) * SPARE]], axis=1) for j in range(3)
    ]
    tail = last[:, 3 * SPARE :]
    fill = jnp.zeros((FOLD * group - share, LEFT), BF)
    columns = [tail[j * group : (j + 1) * group] for j in range(FOLD - 1)]
    columns.append(jnp.concatenate([tail[(FOLD - 1) * group :], fill], axis=0))
    return tiles + [jnp.concatenate(columns, axis=1)]


def unpacked(ref, share):
    tiles = [ref[j * share : (j + 1) * share, :] for j in range(3)]
    rest = ref[3 * share :, :]
    group = rest.shape[0]
    columns = [rest[:, j * LEFT : (j + 1) * LEFT] for j in range(FOLD)]
    columns[-1] = columns[-1][: share - (FOLD - 1) * group]
    last = [tile[:, HD:] for tile in tiles] + [jnp.concatenate(columns, axis=0)]
    return [tile[:, :HD] for tile in tiles] + [jnp.concatenate(last, axis=1)]


def pack_kernel(n, w_ref, *refs):
    outs, staged = refs[:n], refs[n]
    me = lax.axis_index("seq")
    group = lax.axis_index("grp")
    share = w_ref.shape[1]
    count = outs[0].shape[0]
    for head in range(n):
        mats = [w_ref[mat, :, head * HD : (head + 1) * HD] for mat in range(4)]
        for j, tile in enumerate(packed(mats)):
            staged[head, j * share : j * share + tile.shape[0], :] = tile
    first = pl.multiple_of(group * (staged.shape[1] - count), 16)
    for k, out in enumerate(outs):
        out[...] = staged[me ^ k, pl.ds(first, count), :]


def weights_kernel(n, share, *refs):
    pieces, w_ref, staged = refs[:4], refs[4], refs[5]
    me = lax.axis_index("seq")
    image = lax.axis_index("dp")
    group = lax.axis_index("grp")
    count = pieces[0].shape[0] // n
    fill = jnp.zeros((share, SPARE), BF)
    for k in range(n):
        for other in range(2):
            for piece, at in ((pieces[other], group), (pieces[2 + other], 1 - group)):
                first = pl.multiple_of(at * (staged.shape[1] - count), 16)
                staged[2 * k + other, pl.ds(first, count), :] = piece[k * count : (k + 1) * count]
            at = 1 - image if other else image
            span = pl.ds(pl.multiple_of(((me ^ k) * 2 + at) * share, 16), share)
            for mat, block in enumerate(unpacked(staged.at[2 * k + other], share)):
                w_ref[span, mat * SLOT : (mat + 1) * SLOT] = jnp.concatenate([block, fill], axis=1)


def norm_kernel(x_ref, up_ref, send_ref, rest_ref, staged):
    core = lax.axis_index("pipe")
    half = x_ref.shape[0] // 2
    staged[...] = standardize(x_ref[...].astype(F32))[0].astype(BF)
    for target, at in ((send_ref, core), (rest_ref, 1 - core)):
        span = pl.ds(pl.multiple_of(at * half, half), half)
        target[:half] = staged[span, :]
        target[half:] = up_ref[span, :]


def merge_kernel(*refs):
    share = refs[0].shape[0]
    for k, ref in enumerate(refs[:-1]):
        refs[-1][k * share : (k + 1) * share] = ref[...]


def project(x, up, w_ref):
    return [
        nn(x, w_ref[:, : 3 * SLOT]).astype(BF),
        nn(up, w_ref[:, 3 * SLOT :]).astype(BF),
    ]


def place(row, sides, x_ref, up_ref):
    half = sides[0].shape[0] // 2
    for side, source in enumerate(sides):
        span = slice(row + side * half, row + (side + 1) * half)
        x_ref[span, :] = source[:half, :]
        up_ref[span, :] = source[half:, :]


def project_kernel(n, *refs):
    w_ref, x_ref, up_ref, made_ref = refs[2 * n - 2 :]
    rows = refs[0].shape[0]
    for k in range(n - 1):
        place(k * rows, refs[2 * k : 2 * k + 2], x_ref, up_ref)
    made_ref[:, : 3 * SLOT], made_ref[:, 3 * SLOT :] = project(x_ref[...], up_ref[...], w_ref)


def head_kernel(n, *refs):
    middle, passed = refs[:2], refs[2:4]
    made_ref, w_ref, keep_ref, give_ref, grads, x_ref, up_ref = refs[4:11]
    made, term_k, term_v = refs[11:]
    me = lax.axis_index("seq")
    rows = x_ref.shape[0]
    half = rows // 2
    ready = (n - 1) * rows

    @pl.when((me == 0) | (me == n - 1))
    def _():
        place(0, passed, x_ref, up_ref)

    @pl.when((me != 0) & (me != n - 1))
    def _():
        place(0, middle, x_ref, up_ref)

    made[:ready, :] = made_ref[...]
    made[ready:, : 3 * SLOT], made[ready:, 3 * SLOT :] = project(x_ref[...], up_ref[...], w_ref)
    scale = HD ** (-0.5)
    key_rows = made[:, SLOT : 2 * SLOT]
    value_rows = made[:, 2 * SLOT : 3 * SLOT]
    grad_out_all = made[:, 3 * SLOT :]
    scores = nt(made[:, :SLOT], key_rows) * scale
    weight = jnp.exp(scores - jnp.max(scores, axis=1, keepdims=True))
    probs_all = (weight / jnp.sum(weight, axis=1, keepdims=True)).astype(BF)
    attended = nn(probs_all, value_rows).astype(BF)
    delta = jnp.sum(grad_out_all.astype(F32) * attended.astype(F32), axis=1, keepdims=True)
    dprobs = nt(grad_out_all, value_rows)
    dscores_all = (probs_all.astype(F32) * (dprobs - delta) * scale).astype(BF)
    grads[:, :SLOT] = nn(dscores_all, key_rows).astype(BF)
    grads[:, 3 * SLOT :] = attended
    for b in range(n):
        span = slice(b * rows, (b + 1) * rows)
        key_term = tn(dscores_all[span], made[span, :SLOT]).astype(BF).astype(F32)
        value_term = tn(probs_all[span], made[span, 3 * SLOT :]).astype(BF).astype(F32)
        if b == 0:
            term_k[...] = key_term
            term_v[...] = value_term
        else:
            term_k[...] += key_term
            term_v[...] += value_term
    grads[:, SLOT : 2 * SLOT] = term_k[...].astype(BF)
    grads[:, 2 * SLOT : 3 * SLOT] = term_v[...].astype(BF)
    whole = nt(grads[:, : 3 * SLOT], w_ref[:, : 3 * SLOT]).astype(BF)
    for b in range(n):
        part = whole[b * rows : (b + 1) * rows]
        keep_ref[b] = part[:half]
        give_ref[b] = part[half:]


def weight_kernel(n, factor, x_ref, x_last, up_ref, up_last, grads, keep_ref, give_ref, staged):
    me = lax.axis_index("seq")
    image = lax.axis_index("dp")
    ready = x_ref.shape[0]
    share = staged.shape[0] // (2 * n)
    for lanes, first, last in (
        (slice(0, 3 * SLOT), x_ref, x_last),
        (slice(3 * SLOT, 4 * SLOT), up_ref, up_last),
    ):
        total = tn(first[...], grads[:ready, lanes]) + tn(last[...], grads[ready:, lanes])
        staged[:, lanes] = (total * factor).astype(BF)
    for k in range(n):
        for target, at in ((keep_ref, image), (give_ref, 1 - image)):
            first = pl.multiple_of(((me ^ k) * 2 + at) * share, 16)
            mats = [
                staged[pl.ds(first, share), mat * SLOT : mat * SLOT + HD] for mat in range(4)
            ]
            for j, tile in enumerate(packed(mats)):
                target[k, j * share : j * share + tile.shape[0], :] = tile


def sum_kernel(mine_ref, theirs_ref, *outs):
    for out, k in zip(outs, ORDER):
        out[...] = (mine_ref[k].astype(F32) + theirs_ref[k].astype(F32)).astype(BF)


def final_kernel(n, x_ref, up_ref, *refs):
    parts, (out_ref, rest_ref) = refs[:n], refs[n:]
    half = 2 * out_ref.shape[0]
    core = lax.axis_index("pipe")
    span = pl.ds(pl.multiple_of(core * half, half), half)
    total = parts[0][...].astype(F32)
    for part in parts[1:]:
        total += part[...].astype(F32)
    xhat, inverse_deviation = standardize(x_ref[span, :].astype(F32))
    leading = jnp.mean(total, axis=1, keepdims=True)
    trailing = jnp.mean(total * xhat, axis=1, keepdims=True)
    result = (
        up_ref[span, :].astype(F32) + inverse_deviation * (total - leading - xhat * trailing)
    ).astype(BF)
    out_ref[...] = result[: half // 2]
    rest_ref[...] = result[half // 2 :]


def join_kernel(n, *refs):
    pairs, parts = refs[:4], refs[4 : 4 + n]
    input_ref, out_ref, staged, joined, made, sems = refs[4 + n :]
    me = lax.axis_index("seq")
    core = lax.axis_index("pipe")
    share = made.shape[1]
    count = pairs[0].shape[0]
    for i, ref in enumerate(pairs):
        side = core if i < 2 else 1 - core
        first = pl.multiple_of((2 * side + i % 2) * count, count)
        joined[pl.ds(first, count), :] = ref[...]
    copies = [pltpu.make_async_copy(joined, input_ref, sems.at[4])]
    copies[0].start()
    for part, k in zip(parts, ORDER):
        staged[me ^ k] = part[...]
    for mat in range(4):
        for head in range(n):
            lanes = slice(head * HD, (head + 1) * HD)
            if mat < 3:
                block = staged[head, mat * share : (mat + 1) * share, :HD]
            else:
                block = unpacked(staged.at[head], share)[3]
            made[mat, :, lanes] = block.astype(F32)
        copies.append(pltpu.make_async_copy(made.at[mat], out_ref.at[mat], sems.at[mat]))
        copies[-1].start()
    for copy in copies:
        copy.wait()


def call(kernel, out_shape, args, scratch=(), plain=0, out_space=pltpu.VMEM):
    single = not isinstance(out_shape, list)
    shapes = [out_shape] if single else out_shape
    args = list(args[:plain]) + [
        pltpu.with_memory_space_constraint(a, pltpu.VMEM) for a in args[plain:]
    ]
    out = pl.pallas_call(
        kernel,
        out_shape=[out_space(*s) for s in shapes],
        in_specs=[VMEM_SPEC] * len(args),
        out_specs=[VMEM_SPEC if out_space is pltpu.VMEM else ANY_SPEC] * len(shapes),
        scratch_shapes=list(scratch),
        compiler_params=PARAMS,
    )(*args)
    return out[0] if single else list(out)


def local_heads(embeddings, upstream, attn_weights):
    n = lax.axis_size("seq")
    x, up = embeddings[0], upstream[0]
    rows, width = x.shape
    share = attn_weights.shape[1]
    patches = n * rows
    half = rows // 2
    me = lax.axis_index("seq")

    def across(value, k):
        return lax.ppermute(value, "seq", [(i, i ^ k) for i in range(n)])

    def exchange(values):
        return [across(value, k) for value, k in zip(values[1:], ORDER[1:])]

    def swap(value, axis):
        return lax.ppermute(value, axis, [(0, 1), (1, 0)])


    full, count = packed_rows(share), half_rows(share)
    chunks = call(
        functools.partial(pack_kernel, n),
        [((count, SLOT), BF)] * n,
        (attn_weights,),
        [pltpu.VMEM((n, full, SLOT), BF)],
        plain=1,
    )
    arrived = [across(chunks[k], k) for k in range(1, n)]
    send, rest = call(
        norm_kernel, [((rows, width), BF)] * 2, (x, up), [pltpu.VMEM((rows, width), BF)], plain=2
    )
    send, arrived[0] = lax.optimization_barrier((send, arrived[0]))
    merged = call(merge_kernel, ((n * count, SLOT), BF), (chunks[0], *arrived))
    beside = swap(merged, "dp")
    above = swap(merged, "grp")
    second = across(send, 2)
    first = across(send, 1)
    later, first, second, beside, above = lax.optimization_barrier(
        (send, first, second, beside, above)
    )
    corner = swap(above, "dp")
    weights = call(
        functools.partial(weights_kernel, n, share),
        ((width, 4 * SLOT), BF),
        (merged, beside, above, corner),
        [pltpu.VMEM((2 * n, full, SLOT), BF)],
    )
    middle = lax.ppermute(later, "seq", [(1, 2), (2, 1)])
    passed = lax.ppermute(second, "seq", [(2, 3), (1, 0)])
    weights, middle, passed = lax.optimization_barrier((weights, middle, passed))
    ready = patches - rows
    x_head, up_head, made = call(
        functools.partial(project_kernel, n),
        [((ready, width), BF)] * 2 + [((ready, 4 * SLOT), BF)],
        (send, rest, first, swap(first, "pipe"), second, swap(second, "pipe"), weights),
    )
    keep, give, grads, x_last, up_last = call(
        functools.partial(head_kernel, n),
        [((n, half, width), BF)] * 2 + [((patches, 4 * SLOT), BF)] + [((rows, width), BF)] * 2,
        (middle, swap(middle, "pipe"), passed, swap(passed, "pipe"), made, weights),
        [
            pltpu.VMEM((patches, 4 * SLOT), BF),
            pltpu.VMEM((patches, SLOT), F32),
            pltpu.VMEM((patches, SLOT), F32),
        ],
    )
    factor = 1.0 / math.sqrt(patches * lax.axis_size("dp"))
    w_keep, w_give = call(
        functools.partial(weight_kernel, n, factor),
        [((n, full, SLOT), BF)] * 2,
        (x_head, x_last, up_head, up_last, grads),
        [pltpu.VMEM((width, 4 * SLOT), BF)],
    )
    taken = swap(give, "pipe")
    w_taken = swap(w_give, "dp")
    sums = call(sum_kernel, [((half, width), BF)] * n, (keep, taken))
    parts = exchange(sums)
    w_taken, sums[0] = lax.optimization_barrier((w_taken, sums[0]))
    w_sums = call(
        sum_kernel, [((full, SLOT), BF)] * n, (w_keep, w_taken)
    )
    w_parts = [w_sums[0]] + exchange(w_sums)
    mine = call(
        functools.partial(final_kernel, n),
        [((half // 2, width), BF)] * 2,
        (x, up, sums[0], *parts),
        plain=2,
    )
    input_gradient, weight_grads = call(
        functools.partial(join_kernel, n),
        [((rows, width), BF), ((4, share, n * HD), F32)],
        (*mine, *[swap(m, "pipe") for m in mine], *w_parts),
        [
            pltpu.VMEM((n, full, SLOT), BF),
            pltpu.VMEM((rows, width), BF),
            pltpu.VMEM((4, share, n * HD), F32),
            pltpu.SemaphoreType.DMA((5,)),
        ],
        out_space=jax.ShapeDtypeStruct,
    )
    return (input_gradient[None], weight_grads)


def local_gathered(embeddings, upstream, attn_weights):
    tokens = embeddings[0]
    row_gradients = upstream[0]
    row_count = tokens.shape[0]
    weights = lax.all_gather(attn_weights, ("seq", "dp"), axis=1, tiled=True)
    local_width = weights.shape[2]
    head_count = local_width // HD
    score_scale = HD ** (-0.5)
    standardized_input, inverse_deviation = standardize(tokens.astype(F32))
    normalized_rows = standardized_input.astype(BF)
    proj = jnp.einsum(
        "td,cdh->cth", normalized_rows, weights[:3], preferred_element_type=F32
    ).astype(BF)
    gathered = lax.all_gather(proj[1:], "seq", axis=1, tiled=True)
    key_count = gathered.shape[1]
    query_heads = proj[0].reshape(row_count, head_count, HD).transpose(1, 0, 2)
    key_heads = gathered[0].reshape(key_count, head_count, HD).transpose(1, 0, 2)
    value_heads = gathered[1].reshape(key_count, head_count, HD).transpose(1, 0, 2)
    grad_att = jnp.dot(row_gradients, weights[3], preferred_element_type=F32).astype(BF)
    grad_heads = grad_att.reshape(row_count, head_count, HD).transpose(1, 0, 2)

    def one_head(items):
        query_rows, key_rows, value_rows, grad_out = items
        scores = nn(query_rows, key_rows.T) * score_scale
        row_max = jnp.max(scores, axis=1, keepdims=True)
        log_total = row_max + jnp.log(jnp.sum(jnp.exp(scores - row_max), axis=1, keepdims=True))
        probs = jnp.exp(scores - log_total).astype(BF)
        attended = nn(probs, value_rows).astype(BF)
        row_delta = jnp.sum(
            grad_out.astype(F32) * attended.astype(F32), axis=1, keepdims=True
        )
        dprobs = nn(grad_out, value_rows.T)
        dscores = (probs.astype(F32) * (dprobs - row_delta) * score_scale).astype(BF)
        grad_q = nn(dscores, key_rows).astype(BF)
        return (attended, grad_q, nn(dscores.T, query_rows), nn(probs.T, grad_out))

    attended_h, grad_q_h, key_h, value_h = lax.map(
        one_head, (query_heads, key_heads, value_heads, grad_heads)
    )
    attended_flat = attended_h.transpose(1, 0, 2).reshape(row_count, local_width)
    grad_q = grad_q_h.transpose(1, 0, 2).reshape(1, row_count, local_width)
    key_terms = key_h.transpose(1, 0, 2).reshape(key_count, local_width)
    value_terms = value_h.transpose(1, 0, 2).reshape(key_count, local_width)
    both_terms = jnp.stack([key_terms, value_terms])
    owned = lax.psum_scatter(both_terms.astype(BF), "seq", scatter_dimension=1, tiled=True)
    grad_qkv = jnp.concatenate([grad_q, owned], axis=0)
    token_count = row_count * lax.axis_size("seq") * lax.axis_size("dp")
    grad_factor = 1.0 / math.sqrt(token_count)
    terms_qkv = jnp.einsum("td,cth->cdh", normalized_rows, grad_qkv, preferred_element_type=F32)
    term_out = jnp.einsum("td,th->dh", row_gradients, attended_flat, preferred_element_type=F32)
    terms = jnp.concatenate([terms_qkv, term_out[None]], axis=0) * grad_factor
    seq_summed = lax.psum_scatter(terms.astype(BF), "seq", scatter_dimension=1, tiled=True)
    weight_grads = lax.psum_scatter(seq_summed, "dp", scatter_dimension=1, tiled=True).astype(F32)
    input_part = jnp.einsum("cth,cdh->td", grad_qkv, weights[:3], preferred_element_type=F32)
    reduced_total = lax.psum(input_part.astype(BF), "pipe").astype(F32)
    leading_term = jnp.mean(reduced_total, axis=1, keepdims=True)
    trailing_term = jnp.mean(reduced_total * standardized_input, axis=1, keepdims=True)
    input_gradient = (
        row_gradients.astype(F32)
        + inverse_deviation * (reduced_total - leading_term - standardized_input * trailing_term)
    ).astype(BF)
    return (input_gradient[None], weight_grads)


def local(embeddings, upstream, attn_weights):
    n = lax.axis_size("seq")
    heads = attn_weights.shape[2] // HD
    one_head_each = (
        heads == n
        and n == 4
        and lax.axis_size("grp") == 2
        and lax.axis_size("dp") == 2
        and lax.axis_size("pipe") == 2
        and attn_weights.shape[1] % 16 == 0
        and embeddings.shape[0] == 1
        and embeddings.shape[1] % 32 == 0
    )
    return (local_heads if one_head_each else local_gathered)(embeddings, upstream, attn_weights)


def solution(mesh):
    in_specs = (
        P(("grp", "dp"), "seq", None),
        P(("grp", "dp"), "seq", None),
        P(None, ("seq", "dp"), "pipe"),
    )
    out_specs = (P(("grp", "dp"), "seq", None), P("grp", ("seq", "dp"), "pipe"))
    return jax.shard_map(local, mesh=mesh, in_specs=in_specs, out_specs=out_specs, check_vma=False)
```

```python
import functools
import math

import jax
import jax.numpy as jnp
from jax import lax
from jax.experimental import pallas as pl
from jax.experimental.pallas import tpu as pltpu
from jax.sharding import PartitionSpec as P

HD = 104
SLOT = 128

EPSILON = 1e-06
BF = jnp.bfloat16
F32 = jnp.float32
PARAMS = pltpu.CompilerParams(vmem_limit_bytes=24 * 1024 * 1024)
VMEM_SPEC = pl.BlockSpec(memory_space=pltpu.VMEM)
ANY_SPEC = pl.BlockSpec(memory_space=pl.ANY)


def standardize(features):
    row_mean = jnp.mean(features, axis=1, keepdims=True)
    mean_removed = features - row_mean
    variance = jnp.mean(mean_removed * mean_removed, axis=1, keepdims=True)
    inverse_deviation = lax.rsqrt(variance + EPSILON)
    return mean_removed * inverse_deviation, inverse_deviation


def nt(a, b):
    return lax.dot_general(a, b, (((1,), (1,)), ((), ())), preferred_element_type=F32)


def tn(a, b):
    return lax.dot_general(a, b, (((0,), (0,)), ((), ())), preferred_element_type=F32)


def nn(a, b):
    return jnp.dot(a, b, preferred_element_type=F32)


SPARE = SLOT - HD
ORDER = (0, 2, 3, 1)
LEFT = HD - 3 * SPARE
FOLD = SLOT // LEFT


def packed_rows(share):
    group = -(-share // (16 * FOLD)) * 16
    return 3 * share + group


def half_rows(share):
    return -(-packed_rows(share) // 32) * 16


def packed(mats):
    last = mats[3]
    share = last.shape[0]
    group = packed_rows(share) - 3 * share
    tiles = [
        jnp.concatenate([mats[j], last[:, j * SPARE : (j + 1) * SPARE]], axis=1) for j in range(3)
    ]
    tail = last[:, 3 * SPARE :]
    fill = jnp.zeros((FOLD * group - share, LEFT), BF)
    columns = [tail[j * group : (j + 1) * group] for j in range(FOLD - 1)]
    columns.append(jnp.concatenate([tail[(FOLD - 1) * group :], fill], axis=0))
    return tiles + [jnp.concatenate(columns, axis=1)]


def unpacked(ref, share):
    tiles = [ref[j * share : (j + 1) * share, :] for j in range(3)]
    rest = ref[3 * share :, :]
    group = rest.shape[0]
    columns = [rest[:, j * LEFT : (j + 1) * LEFT] for j in range(FOLD)]
    columns[-1] = columns[-1][: share - (FOLD - 1) * group]
    last = [tile[:, HD:] for tile in tiles] + [jnp.concatenate(columns, axis=0)]
    return [tile[:, :HD] for tile in tiles] + [jnp.concatenate(last, axis=1)]


def pack_kernel(n, w_ref, *refs):
    outs, staged = refs[:n], refs[n]
    me = lax.axis_index("seq")
    group = lax.axis_index("grp")
    share = w_ref.shape[1]
    count = outs[0].shape[0]
    for head in range(n):
        mats = [w_ref[mat, :, head * HD : (head + 1) * HD] for mat in range(4)]
        for j, tile in enumerate(packed(mats)):
            staged[head, j * share : j * share + tile.shape[0], :] = tile
    first = pl.multiple_of(group * (staged.shape[1] - count), 16)
    for k, out in enumerate(outs):
        out[...] = staged[me ^ k, pl.ds(first, count), :]


def weights_kernel(n, share, *refs):
    pieces, w_ref, staged = refs[:4], refs[4], refs[5]
    me = lax.axis_index("seq")
    image = lax.axis_index("dp")
    group = lax.axis_index("grp")
    count = pieces[0].shape[0] // n
    fill = jnp.zeros((share, SPARE), BF)
    for k in range(n):
        for other in range(2):
            for piece, at in ((pieces[other], group), (pieces[2 + other], 1 - group)):
                first = pl.multiple_of(at * (staged.shape[1] - count), 16)
                staged[2 * k + other, pl.ds(first, count), :] = piece[k * count : (k + 1) * count]
            at = 1 - image if other else image
            span = pl.ds(pl.multiple_of(((me ^ k) * 2 + at) * share, 16), share)
            for mat, block in enumerate(unpacked(staged.at[2 * k + other], share)):
                w_ref[span, mat * SLOT : (mat + 1) * SLOT] = jnp.concatenate([block, fill], axis=1)


def norm_kernel(x_ref, up_ref, send_ref, rest_ref, staged):
    core = lax.axis_index("pipe")
    half = x_ref.shape[0] // 2
    staged[...] = standardize(x_ref[...].astype(F32))[0].astype(BF)
    for target, at in ((send_ref, core), (rest_ref, 1 - core)):
        span = pl.ds(pl.multiple_of(at * half, half), half)
        target[:half] = staged[span, :]
        target[half:] = up_ref[span, :]


def merge_kernel(*refs):
    share = refs[0].shape[0]
    for k, ref in enumerate(refs[:-1]):
        refs[-1][k * share : (k + 1) * share] = ref[...]


def project(x, up, w_ref):
    return [
        nn(x, w_ref[:, : 3 * SLOT]).astype(BF),
        nn(up, w_ref[:, 3 * SLOT :]).astype(BF),
    ]


def place(row, sides, x_ref, up_ref):
    half = sides[0].shape[0] // 2
    for side, source in enumerate(sides):
        span = slice(row + side * half, row + (side + 1) * half)
        x_ref[span, :] = source[:half, :]
        up_ref[span, :] = source[half:, :]


def project_kernel(n, *refs):
    w_ref, x_ref, up_ref, made_ref = refs[2 * n - 2 :]
    rows = refs[0].shape[0]
    for k in range(n - 1):
        place(k * rows, refs[2 * k : 2 * k + 2], x_ref, up_ref)
    made_ref[:, : 3 * SLOT], made_ref[:, 3 * SLOT :] = project(x_ref[...], up_ref[...], w_ref)


def head_kernel(n, *refs):
    third = refs[:2]
    made_ref, w_ref, keep_ref, give_ref, grads, x_ref, up_ref = refs[2:9]
    made, term_k, term_v = refs[9:]
    rows = x_ref.shape[0]
    half = rows // 2
    ready = (n - 1) * rows

    place(0, third, x_ref, up_ref)
    made[:ready, :] = made_ref[...]
    made[ready:, : 3 * SLOT], made[ready:, 3 * SLOT :] = project(x_ref[...], up_ref[...], w_ref)
    scale = HD ** (-0.5)
    key_rows = made[:, SLOT : 2 * SLOT]
    value_rows = made[:, 2 * SLOT : 3 * SLOT]
    grad_out_all = made[:, 3 * SLOT :]
    scores = nt(made[:, :SLOT], key_rows) * scale
    weight = jnp.exp(scores - jnp.max(scores, axis=1, keepdims=True))
    probs_all = (weight / jnp.sum(weight, axis=1, keepdims=True)).astype(BF)
    attended = nn(probs_all, value_rows).astype(BF)
    delta = jnp.sum(grad_out_all.astype(F32) * attended.astype(F32), axis=1, keepdims=True)
    dprobs = nt(grad_out_all, value_rows)
    dscores_all = (probs_all.astype(F32) * (dprobs - delta) * scale).astype(BF)
    grads[:, :SLOT] = nn(dscores_all, key_rows).astype(BF)
    grads[:, 3 * SLOT :] = attended
    for b in range(n):
        span = slice(b * rows, (b + 1) * rows)
        key_term = tn(dscores_all[span], made[span, :SLOT]).astype(BF).astype(F32)
        value_term = tn(probs_all[span], made[span, 3 * SLOT :]).astype(BF).astype(F32)
        if b == 0:
            term_k[...] = key_term
            term_v[...] = value_term
        else:
            term_k[...] += key_term
            term_v[...] += value_term
    grads[:, SLOT : 2 * SLOT] = term_k[...].astype(BF)
    grads[:, 2 * SLOT : 3 * SLOT] = term_v[...].astype(BF)
    whole = nt(grads[:, : 3 * SLOT], w_ref[:, : 3 * SLOT]).astype(BF)
    for b in range(n):
        part = whole[b * rows : (b + 1) * rows]
        keep_ref[b] = part[:half]
        give_ref[b] = part[half:]


def weight_kernel(n, factor, x_ref, x_last, up_ref, up_last, grads, keep_ref, give_ref, staged):
    me = lax.axis_index("seq")
    image = lax.axis_index("dp")
    ready = x_ref.shape[0]
    share = staged.shape[0] // (2 * n)
    for lanes, first, last in (
        (slice(0, 3 * SLOT), x_ref, x_last),
        (slice(3 * SLOT, 4 * SLOT), up_ref, up_last),
    ):
        total = tn(first[...], grads[:ready, lanes]) + tn(last[...], grads[ready:, lanes])
        staged[:, lanes] = (total * factor).astype(BF)
    for k in range(n):
        for target, at in ((keep_ref, image), (give_ref, 1 - image)):
            first = pl.multiple_of(((me ^ k) * 2 + at) * share, 16)
            mats = [
                staged[pl.ds(first, share), mat * SLOT : mat * SLOT + HD] for mat in range(4)
            ]
            for j, tile in enumerate(packed(mats)):
                target[k, j * share : j * share + tile.shape[0], :] = tile


def sum_kernel(mine_ref, theirs_ref, *outs):
    for out, k in zip(outs, ORDER):
        out[...] = (mine_ref[k].astype(F32) + theirs_ref[k].astype(F32)).astype(BF)


def final_kernel(n, x_ref, up_ref, *refs):
    parts, (out_ref, rest_ref) = refs[:n], refs[n:]
    half = 2 * out_ref.shape[0]
    core = lax.axis_index("pipe")
    span = pl.ds(pl.multiple_of(core * half, half), half)
    total = parts[0][...].astype(F32)
    for part in parts[1:]:
        total += part[...].astype(F32)
    xhat, inverse_deviation = standardize(x_ref[span, :].astype(F32))
    leading = jnp.mean(total, axis=1, keepdims=True)
    trailing = jnp.mean(total * xhat, axis=1, keepdims=True)
    result = (
        up_ref[span, :].astype(F32) + inverse_deviation * (total - leading - xhat * trailing)
    ).astype(BF)
    out_ref[...] = result[: half // 2]
    rest_ref[...] = result[half // 2 :]


def join_kernel(n, *refs):
    pairs, parts = refs[:4], refs[4 : 4 + n]
    input_ref, out_ref, staged, joined, made, sems = refs[4 + n :]
    me = lax.axis_index("seq")
    core = lax.axis_index("pipe")
    share = made.shape[1]
    count = pairs[0].shape[0]
    for i, ref in enumerate(pairs):
        side = core if i < 2 else 1 - core
        first = pl.multiple_of((2 * side + i % 2) * count, count)
        joined[pl.ds(first, count), :] = ref[...]
    copies = [pltpu.make_async_copy(joined, input_ref, sems.at[4])]
    copies[0].start()
    for part, k in zip(parts, ORDER):
        staged[me ^ k] = part[...]
    for mat in range(4):
        for head in range(n):
            lanes = slice(head * HD, (head + 1) * HD)
            if mat < 3:
                block = staged[head, mat * share : (mat + 1) * share, :HD]
            else:
                block = unpacked(staged.at[head], share)[3]
            made[mat, :, lanes] = block.astype(F32)
        copies.append(pltpu.make_async_copy(made.at[mat], out_ref.at[mat], sems.at[mat]))
        copies[-1].start()
    for copy in copies:
        copy.wait()


def call(kernel, out_shape, args, scratch=(), plain=0, out_space=pltpu.VMEM):
    single = not isinstance(out_shape, list)
    shapes = [out_shape] if single else out_shape
    args = list(args[:plain]) + [
        pltpu.with_memory_space_constraint(a, pltpu.VMEM) for a in args[plain:]
    ]
    out = pl.pallas_call(
        kernel,
        out_shape=[out_space(*s) for s in shapes],
        in_specs=[VMEM_SPEC] * len(args),
        out_specs=[VMEM_SPEC if out_space is pltpu.VMEM else ANY_SPEC] * len(shapes),
        scratch_shapes=list(scratch),
        compiler_params=PARAMS,
    )(*args)
    return out[0] if single else list(out)


def local_heads(embeddings, upstream, attn_weights):
    n = lax.axis_size("seq")
    x, up = embeddings[0], upstream[0]
    rows, width = x.shape
    share = attn_weights.shape[1]
    patches = n * rows
    half = rows // 2
    me = lax.axis_index("seq")

    def across(value, k):
        return lax.ppermute(value, "seq", [(i, i ^ k) for i in range(n)])

    def exchange(values):
        return [across(value, k) for value, k in zip(values[1:], ORDER[1:])]

    def swap(value, axis):
        return lax.ppermute(value, axis, [(0, 1), (1, 0)])


    full, count = packed_rows(share), half_rows(share)
    chunks = call(
        functools.partial(pack_kernel, n),
        [((count, SLOT), BF)] * n,
        (attn_weights,),
        [pltpu.VMEM((n, full, SLOT), BF)],
        plain=1,
    )
    arrived = [across(chunks[k], k) for k in range(1, n)]
    send, rest = call(
        norm_kernel, [((rows, width), BF)] * 2, (x, up), [pltpu.VMEM((rows, width), BF)], plain=2
    )
    send, arrived[0] = lax.optimization_barrier((send, arrived[0]))
    merged = call(merge_kernel, ((n * count, SLOT), BF), (chunks[0], *arrived))
    beside = swap(merged, "dp")
    above = swap(merged, "grp")
    second = across(send, 2)
    first = across(send, 1)
    first, second, beside, above = lax.optimization_barrier((first, second, beside, above))
    corner = swap(above, "dp")
    weights = call(
        functools.partial(weights_kernel, n, share),
        ((width, 4 * SLOT), BF),
        (merged, beside, above, corner),
        [pltpu.VMEM((2 * n, full, SLOT), BF)],
    )
    third = across(second, 1)
    weights, third = lax.optimization_barrier((weights, third))
    ready = patches - rows
    x_head, up_head, made = call(
        functools.partial(project_kernel, n),
        [((ready, width), BF)] * 2 + [((ready, 4 * SLOT), BF)],
        (send, rest, first, swap(first, "pipe"), second, swap(second, "pipe"), weights),
    )
    keep, give, grads, x_last, up_last = call(
        functools.partial(head_kernel, n),
        [((n, half, width), BF)] * 2 + [((patches, 4 * SLOT), BF)] + [((rows, width), BF)] * 2,
        (third, swap(third, "pipe"), made, weights),
        [
            pltpu.VMEM((patches, 4 * SLOT), BF),
            pltpu.VMEM((patches, SLOT), F32),
            pltpu.VMEM((patches, SLOT), F32),
        ],
    )
    factor = 1.0 / math.sqrt(patches * lax.axis_size("dp"))
    w_keep, w_give = call(
        functools.partial(weight_kernel, n, factor),
        [((n, full, SLOT), BF)] * 2,
        (x_head, x_last, up_head, up_last, grads),
        [pltpu.VMEM((width, 4 * SLOT), BF)],
    )
    taken = swap(give, "pipe")
    w_taken = swap(w_give, "dp")
    sums = call(sum_kernel, [((half, width), BF)] * n, (keep, taken))
    parts = exchange(sums)
    w_taken, sums[0] = lax.optimization_barrier((w_taken, sums[0]))
    w_sums = call(
        sum_kernel, [((full, SLOT), BF)] * n, (w_keep, w_taken)
    )
    w_parts = [w_sums[0]] + exchange(w_sums)
    mine = call(
        functools.partial(final_kernel, n),
        [((half // 2, width), BF)] * 2,
        (x, up, sums[0], *parts),
        plain=2,
    )
    input_gradient, weight_grads = call(
        functools.partial(join_kernel, n),
        [((rows, width), BF), ((4, share, n * HD), F32)],
        (*mine, *[swap(m, "pipe") for m in mine], *w_parts),
        [
            pltpu.VMEM((n, full, SLOT), BF),
            pltpu.VMEM((rows, width), BF),
            pltpu.VMEM((4, share, n * HD), F32),
            pltpu.SemaphoreType.DMA((5,)),
        ],
        out_space=jax.ShapeDtypeStruct,
    )
    return (input_gradient[None], weight_grads)


def local_gathered(embeddings, upstream, attn_weights):
    tokens = embeddings[0]
    row_gradients = upstream[0]
    row_count = tokens.shape[0]
    weights = lax.all_gather(attn_weights, ("seq", "dp"), axis=1, tiled=True)
    local_width = weights.shape[2]
    head_count = local_width // HD
    score_scale = HD ** (-0.5)
    standardized_input, inverse_deviation = standardize(tokens.astype(F32))
    normalized_rows = standardized_input.astype(BF)
    proj = jnp.einsum(
        "td,cdh->cth", normalized_rows, weights[:3], preferred_element_type=F32
    ).astype(BF)
    gathered = lax.all_gather(proj[1:], "seq", axis=1, tiled=True)
    key_count = gathered.shape[1]
    query_heads = proj[0].reshape(row_count, head_count, HD).transpose(1, 0, 2)
    key_heads = gathered[0].reshape(key_count, head_count, HD).transpose(1, 0, 2)
    value_heads = gathered[1].reshape(key_count, head_count, HD).transpose(1, 0, 2)
    grad_att = jnp.dot(row_gradients, weights[3], preferred_element_type=F32).astype(BF)
    grad_heads = grad_att.reshape(row_count, head_count, HD).transpose(1, 0, 2)

    def one_head(items):
        query_rows, key_rows, value_rows, grad_out = items
        scores = nn(query_rows, key_rows.T) * score_scale
        row_max = jnp.max(scores, axis=1, keepdims=True)
        log_total = row_max + jnp.log(jnp.sum(jnp.exp(scores - row_max), axis=1, keepdims=True))
        probs = jnp.exp(scores - log_total).astype(BF)
        attended = nn(probs, value_rows).astype(BF)
        row_delta = jnp.sum(
            grad_out.astype(F32) * attended.astype(F32), axis=1, keepdims=True
        )
        dprobs = nn(grad_out, value_rows.T)
        dscores = (probs.astype(F32) * (dprobs - row_delta) * score_scale).astype(BF)
        grad_q = nn(dscores, key_rows).astype(BF)
        return (attended, grad_q, nn(dscores.T, query_rows), nn(probs.T, grad_out))

    attended_h, grad_q_h, key_h, value_h = lax.map(
        one_head, (query_heads, key_heads, value_heads, grad_heads)
    )
    attended_flat = attended_h.transpose(1, 0, 2).reshape(row_count, local_width)
    grad_q = grad_q_h.transpose(1, 0, 2).reshape(1, row_count, local_width)
    key_terms = key_h.transpose(1, 0, 2).reshape(key_count, local_width)
    value_terms = value_h.transpose(1, 0, 2).reshape(key_count, local_width)
    both_terms = jnp.stack([key_terms, value_terms])
    owned = lax.psum_scatter(both_terms.astype(BF), "seq", scatter_dimension=1, tiled=True)
    grad_qkv = jnp.concatenate([grad_q, owned], axis=0)
    token_count = row_count * lax.axis_size("seq") * lax.axis_size("dp")
    grad_factor = 1.0 / math.sqrt(token_count)
    terms_qkv = jnp.einsum("td,cth->cdh", normalized_rows, grad_qkv, preferred_element_type=F32)
    term_out = jnp.einsum("td,th->dh", row_gradients, attended_flat, preferred_element_type=F32)
    terms = jnp.concatenate([terms_qkv, term_out[None]], axis=0) * grad_factor
    seq_summed = lax.psum_scatter(terms.astype(BF), "seq", scatter_dimension=1, tiled=True)
    weight_grads = lax.psum_scatter(seq_summed, "dp", scatter_dimension=1, tiled=True).astype(F32)
    input_part = jnp.einsum("cth,cdh->td", grad_qkv, weights[:3], preferred_element_type=F32)
    reduced_total = lax.psum(input_part.astype(BF), "pipe").astype(F32)
    leading_term = jnp.mean(reduced_total, axis=1, keepdims=True)
    trailing_term = jnp.mean(reduced_total * standardized_input, axis=1, keepdims=True)
    input_gradient = (
        row_gradients.astype(F32)
        + inverse_deviation * (reduced_total - leading_term - standardized_input * trailing_term)
    ).astype(BF)
    return (input_gradient[None], weight_grads)


def local(embeddings, upstream, attn_weights):
    n = lax.axis_size("seq")
    heads = attn_weights.shape[2] // HD
    one_head_each = (
        heads == n
        and n == 4
        and lax.axis_size("grp") == 2
        and lax.axis_size("dp") == 2
        and lax.axis_size("pipe") == 2
        and attn_weights.shape[1] % 16 == 0
        and embeddings.shape[0] == 1
        and embeddings.shape[1] % 32 == 0
    )
    return (local_heads if one_head_each else local_gathered)(embeddings, upstream, attn_weights)


def solution(mesh):
    in_specs = (
        P(("grp", "dp"), "seq", None),
        P(("grp", "dp"), "seq", None),
        P(None, ("seq", "dp"), "pipe"),
    )
    out_specs = (P(("grp", "dp"), "seq", None), P("grp", ("seq", "dp"), "pipe"))
    return jax.shard_map(local, mesh=mesh, in_specs=in_specs, out_specs=out_specs, check_vma=False)
```

```python
import functools
import math

import jax
import jax.numpy as jnp
from jax import lax
from jax.experimental import pallas as pl
from jax.experimental.pallas import tpu as pltpu
from jax.sharding import PartitionSpec as P

HD = 104
SLOT = 128

EPSILON = 1e-06
BF = jnp.bfloat16
F32 = jnp.float32
PARAMS = pltpu.CompilerParams(vmem_limit_bytes=24 * 1024 * 1024)
VMEM_SPEC = pl.BlockSpec(memory_space=pltpu.VMEM)
ANY_SPEC = pl.BlockSpec(memory_space=pl.ANY)


def standardize(features):
    row_mean = jnp.mean(features, axis=1, keepdims=True)
    mean_removed = features - row_mean
    variance = jnp.mean(mean_removed * mean_removed, axis=1, keepdims=True)
    inverse_deviation = lax.rsqrt(variance + EPSILON)
    return mean_removed * inverse_deviation, inverse_deviation


def nt(a, b):
    return lax.dot_general(a, b, (((1,), (1,)), ((), ())), preferred_element_type=F32)


def tn(a, b):
    return lax.dot_general(a, b, (((0,), (0,)), ((), ())), preferred_element_type=F32)


def nn(a, b):
    return jnp.dot(a, b, preferred_element_type=F32)


SPARE = SLOT - HD
W_ORDER = (0, 2, 3, 1)
X_ORDER = (0, 2, 3, 1)
ORDER = (0, 2, 3, 1)
LEFT = HD - 3 * SPARE
FOLD = SLOT // LEFT


def packed_rows(share):
    group = -(-share // (16 * FOLD)) * 16
    return 3 * share + group


def half_rows(share):
    return -(-packed_rows(share) // 32) * 16


def packed(mats):
    last = mats[3]
    share = last.shape[0]
    group = packed_rows(share) - 3 * share
    tiles = [
        jnp.concatenate([mats[j], last[:, j * SPARE : (j + 1) * SPARE]], axis=1) for j in range(3)
    ]
    tail = last[:, 3 * SPARE :]
    fill = jnp.zeros((FOLD * group - share, LEFT), BF)
    columns = [tail[j * group : (j + 1) * group] for j in range(FOLD - 1)]
    columns.append(jnp.concatenate([tail[(FOLD - 1) * group :], fill], axis=0))
    return tiles + [jnp.concatenate(columns, axis=1)]


def unpacked(ref, share):
    tiles = [ref[j * share : (j + 1) * share, :] for j in range(3)]
    rest = ref[3 * share :, :]
    group = rest.shape[0]
    columns = [rest[:, j * LEFT : (j + 1) * LEFT] for j in range(FOLD)]
    columns[-1] = columns[-1][: share - (FOLD - 1) * group]
    last = [tile[:, HD:] for tile in tiles] + [jnp.concatenate(columns, axis=0)]
    return [tile[:, :HD] for tile in tiles] + [jnp.concatenate(last, axis=1)]


def pack_kernel(n, w_ref, *refs):
    outs, staged = refs[:n], refs[n]
    me = lax.axis_index("seq")
    group = lax.axis_index("grp")
    share = w_ref.shape[1]
    count = outs[0].shape[0]
    for head in range(n):
        mats = [w_ref[mat, :, head * HD : (head + 1) * HD] for mat in range(4)]
        for j, tile in enumerate(packed(mats)):
            staged[head, j * share : j * share + tile.shape[0], :] = tile
    first = pl.multiple_of(group * (staged.shape[1] - count), 16)
    for k, out in zip(W_ORDER, outs):
        out[...] = staged[me ^ k, pl.ds(first, count), :]


def weights_kernel(n, share, *refs):
    pieces, w_ref, staged = refs[:4], refs[4], refs[5]
    me = lax.axis_index("seq")
    image = lax.axis_index("dp")
    group = lax.axis_index("grp")
    count = pieces[0].shape[0] // n
    fill = jnp.zeros((share, SPARE), BF)
    for k in range(n):
        for other in range(2):
            for piece, at in ((pieces[other], group), (pieces[2 + other], 1 - group)):
                first = pl.multiple_of(at * (staged.shape[1] - count), 16)
                staged[2 * k + other, pl.ds(first, count), :] = piece[k * count : (k + 1) * count]
            at = 1 - image if other else image
            span = pl.ds(pl.multiple_of(((me ^ k) * 2 + at) * share, 16), share)
            for mat, block in enumerate(unpacked(staged.at[2 * k + other], share)):
                w_ref[span, mat * SLOT : (mat + 1) * SLOT] = jnp.concatenate([block, fill], axis=1)


def norm_kernel(x_ref, up_ref, send_ref, rest_ref, staged):
    core = lax.axis_index("pipe")
    half = x_ref.shape[0] // 2
    staged[...] = standardize(x_ref[...].astype(F32))[0].astype(BF)
    for target, at in ((send_ref, core), (rest_ref, 1 - core)):
        span = pl.ds(pl.multiple_of(at * half, half), half)
        target[:half] = staged[span, :]
        target[half:] = up_ref[span, :]


def merge_kernel(*refs):
    share = refs[0].shape[0]
    for k, ref in zip(W_ORDER, refs[:-1]):
        refs[-1][k * share : (k + 1) * share] = ref[...]


def project(x, up, w_ref):
    return [
        nn(x, w_ref[:, : 3 * SLOT]).astype(BF),
        nn(up, w_ref[:, 3 * SLOT :]).astype(BF),
    ]


def place(row, sides, x_ref, up_ref):
    half = sides[0].shape[0] // 2
    for side, source in enumerate(sides):
        span = slice(row + side * half, row + (side + 1) * half)
        x_ref[span, :] = source[:half, :]
        up_ref[span, :] = source[half:, :]


def project_kernel(n, *refs):
    w_ref, x_ref, up_ref, made_ref = refs[2 * n - 2 :]
    rows = refs[0].shape[0]
    for k in range(n - 1):
        place(k * rows, refs[2 * k : 2 * k + 2], x_ref, up_ref)
    made_ref[:, : 3 * SLOT], made_ref[:, 3 * SLOT :] = project(x_ref[...], up_ref[...], w_ref)


def head_kernel(n, *refs):
    third = refs[:2]
    made_ref, w_ref, keep_ref, give_ref, grads, x_ref, up_ref = refs[2:9]
    made, term_k, term_v = refs[9:]
    rows = x_ref.shape[0]
    half = rows // 2
    ready = (n - 1) * rows

    place(0, third, x_ref, up_ref)
    made[:ready, :] = made_ref[...]
    made[ready:, : 3 * SLOT], made[ready:, 3 * SLOT :] = project(x_ref[...], up_ref[...], w_ref)
    scale = HD ** (-0.5)
    key_rows = made[:, SLOT : 2 * SLOT]
    value_rows = made[:, 2 * SLOT : 3 * SLOT]
    grad_out_all = made[:, 3 * SLOT :]
    scores = nt(made[:, :SLOT], key_rows) * scale
    weight = jnp.exp(scores - jnp.max(scores, axis=1, keepdims=True))
    probs_all = (weight * (1.0 / jnp.sum(weight, axis=1, keepdims=True))).astype(BF)
    attended = nn(probs_all, value_rows).astype(BF)
    delta = jnp.sum(grad_out_all.astype(F32) * attended.astype(F32), axis=1, keepdims=True)
    dprobs = nt(grad_out_all, value_rows)
    dscores_all = (probs_all.astype(F32) * (dprobs - delta) * scale).astype(BF)
    grads[:, :SLOT] = nn(dscores_all, key_rows).astype(BF)
    grads[:, 3 * SLOT :] = attended
    for b in range(n):
        span = slice(b * rows, (b + 1) * rows)
        key_term = tn(dscores_all[span], made[span, :SLOT]).astype(BF).astype(F32)
        value_term = tn(probs_all[span], made[span, 3 * SLOT :]).astype(BF).astype(F32)
        if b == 0:
            term_k[...] = key_term
            term_v[...] = value_term
        else:
            term_k[...] += key_term
            term_v[...] += value_term
    grads[:, SLOT : 2 * SLOT] = term_k[...].astype(BF)
    grads[:, 2 * SLOT : 3 * SLOT] = term_v[...].astype(BF)
    whole = nt(grads[:, : 3 * SLOT], w_ref[:, : 3 * SLOT]).astype(BF)
    for b in range(n):
        part = whole[b * rows : (b + 1) * rows]
        keep_ref[b] = part[:half]
        give_ref[b] = part[half:]


def weight_kernel(n, factor, x_ref, x_last, up_ref, up_last, grads, keep_ref, give_ref, staged):
    me = lax.axis_index("seq")
    image = lax.axis_index("dp")
    ready = x_ref.shape[0]
    share = staged.shape[0] // (2 * n)
    for lanes, first, last in (
        (slice(0, 3 * SLOT), x_ref, x_last),
        (slice(3 * SLOT, 4 * SLOT), up_ref, up_last),
    ):
        total = tn(first[...], grads[:ready, lanes]) + tn(last[...], grads[ready:, lanes])
        staged[:, lanes] = (total * factor).astype(BF)
    for k in range(n):
        for target, at in ((keep_ref, image), (give_ref, 1 - image)):
            first = pl.multiple_of(((me ^ k) * 2 + at) * share, 16)
            mats = [
                staged[pl.ds(first, share), mat * SLOT : mat * SLOT + HD] for mat in range(4)
            ]
            for j, tile in enumerate(packed(mats)):
                target[k, j * share : j * share + tile.shape[0], :] = tile


def sum_kernel(order, mine_ref, theirs_ref, *outs):
    for out, k in zip(outs, order):
        out[...] = (mine_ref[k].astype(F32) + theirs_ref[k].astype(F32)).astype(BF)


def final_kernel(n, x_ref, up_ref, *refs):
    parts, (out_ref, rest_ref) = refs[:n], refs[n:]
    half = 2 * out_ref.shape[0]
    core = lax.axis_index("pipe")
    span = pl.ds(pl.multiple_of(core * half, half), half)
    total = parts[0][...].astype(F32)
    for part in parts[1:]:
        total += part[...].astype(F32)
    xhat, inverse_deviation = standardize(x_ref[span, :].astype(F32))
    leading = jnp.mean(total, axis=1, keepdims=True)
    trailing = jnp.mean(total * xhat, axis=1, keepdims=True)
    result = (
        up_ref[span, :].astype(F32) + inverse_deviation * (total - leading - xhat * trailing)
    ).astype(BF)
    out_ref[...] = result[: half // 2]
    rest_ref[...] = result[half // 2 :]


def join_kernel(n, *refs):
    pairs, parts = refs[:4], refs[4 : 4 + n]
    input_ref, out_ref, staged, joined, made, sems = refs[4 + n :]
    me = lax.axis_index("seq")
    core = lax.axis_index("pipe")
    share = made.shape[1]
    count = pairs[0].shape[0]
    for i, ref in enumerate(pairs):
        side = core if i < 2 else 1 - core
        first = pl.multiple_of((2 * side + i % 2) * count, count)
        joined[pl.ds(first, count), :] = ref[...]
    copies = [pltpu.make_async_copy(joined, input_ref, sems.at[4])]
    copies[0].start()
    for part, k in zip(parts, ORDER):
        staged[me ^ k] = part[...]
    for mat in range(4):
        for head in range(n):
            lanes = slice(head * HD, (head + 1) * HD)
            if mat < 3:
                block = staged[head, mat * share : (mat + 1) * share, :HD]
            else:
                block = unpacked(staged.at[head], share)[3]
            made[mat, :, lanes] = block.astype(F32)
        copies.append(pltpu.make_async_copy(made.at[mat], out_ref.at[mat], sems.at[mat]))
        copies[-1].start()
    for copy in copies:
        copy.wait()


def call(kernel, out_shape, args, scratch=(), plain=0, out_space=pltpu.VMEM):
    single = not isinstance(out_shape, list)
    shapes = [out_shape] if single else out_shape
    args = list(args[:plain]) + [
        pltpu.with_memory_space_constraint(a, pltpu.VMEM) for a in args[plain:]
    ]
    out = pl.pallas_call(
        kernel,
        out_shape=[out_space(*s) for s in shapes],
        in_specs=[VMEM_SPEC] * len(args),
        out_specs=[VMEM_SPEC if out_space is pltpu.VMEM else ANY_SPEC] * len(shapes),
        scratch_shapes=list(scratch),
        compiler_params=PARAMS,
    )(*args)
    return out[0] if single else list(out)


def local_heads(embeddings, upstream, attn_weights):
    n = lax.axis_size("seq")
    x, up = embeddings[0], upstream[0]
    rows, width = x.shape
    share = attn_weights.shape[1]
    patches = n * rows
    half = rows // 2
    me = lax.axis_index("seq")

    def across(value, k):
        return lax.ppermute(value, "seq", [(i, i ^ k) for i in range(n)])

    def exchange(values, order):
        return [across(value, k) for value, k in zip(values[1:], order[1:])]

    def swap(value, axis):
        return lax.ppermute(value, axis, [(0, 1), (1, 0)])


    full, count = packed_rows(share), half_rows(share)
    chunks = call(
        functools.partial(pack_kernel, n),
        [((count, SLOT), BF)] * n,
        (attn_weights,),
        [pltpu.VMEM((n, full, SLOT), BF)],
        plain=1,
    )
    arrived = [across(c, k) for c, k in zip(chunks[1:], W_ORDER[1:])]
    send, rest = call(
        norm_kernel, [((rows, width), BF)] * 2, (x, up), [pltpu.VMEM((rows, width), BF)], plain=2
    )
    send, arrived[2] = lax.optimization_barrier((send, arrived[2]))
    merged = call(merge_kernel, ((n * count, SLOT), BF), (chunks[0], *arrived))
    beside = swap(merged, "dp")
    above = swap(merged, "grp")
    corner = swap(above, "dp")
    second = across(send, 2)
    first = across(send, 1)
    first, second, beside, above = lax.optimization_barrier((first, second, beside, above))
    weights = call(
        functools.partial(weights_kernel, n, share),
        ((width, 4 * SLOT), BF),
        (merged, beside, above, corner),
        [pltpu.VMEM((2 * n, full, SLOT), BF)],
    )
    third = across(second, 1)
    weights, third = lax.optimization_barrier((weights, third))
    ready = patches - rows
    x_head, up_head, made = call(
        functools.partial(project_kernel, n),
        [((ready, width), BF)] * 2 + [((ready, 4 * SLOT), BF)],
        (send, rest, first, swap(first, "pipe"), second, swap(second, "pipe"), weights),
    )
    keep, give, grads, x_last, up_last = call(
        functools.partial(head_kernel, n),
        [((n, half, width), BF)] * 2 + [((patches, 4 * SLOT), BF)] + [((rows, width), BF)] * 2,
        (third, swap(third, "pipe"), made, weights),
        [
            pltpu.VMEM((patches, 4 * SLOT), BF),
            pltpu.VMEM((patches, SLOT), F32),
            pltpu.VMEM((patches, SLOT), F32),
        ],
    )
    factor = 1.0 / math.sqrt(patches * lax.axis_size("dp"))
    w_keep, w_give = call(
        functools.partial(weight_kernel, n, factor),
        [((n, full, SLOT), BF)] * 2,
        (x_head, x_last, up_head, up_last, grads),
        [pltpu.VMEM((width, 4 * SLOT), BF)],
    )
    taken = swap(give, "pipe")
    w_taken = swap(w_give, "dp")
    sums = call(functools.partial(sum_kernel, X_ORDER), [((half, width), BF)] * n, (keep, taken))
    parts = exchange(sums, X_ORDER)
    w_taken, sums[0] = lax.optimization_barrier((w_taken, sums[0]))
    w_sums = call(
        functools.partial(sum_kernel, ORDER), [((full, SLOT), BF)] * n, (w_keep, w_taken)
    )
    w_parts = [w_sums[0]] + exchange(w_sums, ORDER)
    mine = call(
        functools.partial(final_kernel, n),
        [((half // 2, width), BF)] * 2,
        (x, up, sums[0], *parts),
        plain=2,
    )
    input_gradient, weight_grads = call(
        functools.partial(join_kernel, n),
        [((rows, width), BF), ((4, share, n * HD), F32)],
        (*mine, *[swap(m, "pipe") for m in mine], *w_parts),
        [
            pltpu.VMEM((n, full, SLOT), BF),
            pltpu.VMEM((rows, width), BF),
            pltpu.VMEM((4, share, n * HD), F32),
            pltpu.SemaphoreType.DMA((5,)),
        ],
        out_space=jax.ShapeDtypeStruct,
    )
    return (input_gradient[None], weight_grads)


def local_gathered(embeddings, upstream, attn_weights):
    tokens = embeddings[0]
    row_gradients = upstream[0]
    row_count = tokens.shape[0]
    weights = lax.all_gather(attn_weights, ("seq", "dp"), axis=1, tiled=True)
    local_width = weights.shape[2]
    head_count = local_width // HD
    score_scale = HD ** (-0.5)
    standardized_input, inverse_deviation = standardize(tokens.astype(F32))
    normalized_rows = standardized_input.astype(BF)
    proj = jnp.einsum(
        "td,cdh->cth", normalized_rows, weights[:3], preferred_element_type=F32
    ).astype(BF)
    gathered = lax.all_gather(proj[1:], "seq", axis=1, tiled=True)
    key_count = gathered.shape[1]
    query_heads = proj[0].reshape(row_count, head_count, HD).transpose(1, 0, 2)
    key_heads = gathered[0].reshape(key_count, head_count, HD).transpose(1, 0, 2)
    value_heads = gathered[1].reshape(key_count, head_count, HD).transpose(1, 0, 2)
    grad_att = jnp.dot(row_gradients, weights[3], preferred_element_type=F32).astype(BF)
    grad_heads = grad_att.reshape(row_count, head_count, HD).transpose(1, 0, 2)

    def one_head(items):
        query_rows, key_rows, value_rows, grad_out = items
        scores = nn(query_rows, key_rows.T) * score_scale
        row_max = jnp.max(scores, axis=1, keepdims=True)
        log_total = row_max + jnp.log(jnp.sum(jnp.exp(scores - row_max), axis=1, keepdims=True))
        probs = jnp.exp(scores - log_total).astype(BF)
        attended = nn(probs, value_rows).astype(BF)
        row_delta = jnp.sum(
            grad_out.astype(F32) * attended.astype(F32), axis=1, keepdims=True
        )
        dprobs = nn(grad_out, value_rows.T)
        dscores = (probs.astype(F32) * (dprobs - row_delta) * score_scale).astype(BF)
        grad_q = nn(dscores, key_rows).astype(BF)
        return (attended, grad_q, nn(dscores.T, query_rows), nn(probs.T, grad_out))

    attended_h, grad_q_h, key_h, value_h = lax.map(
        one_head, (query_heads, key_heads, value_heads, grad_heads)
    )
    attended_flat = attended_h.transpose(1, 0, 2).reshape(row_count, local_width)
    grad_q = grad_q_h.transpose(1, 0, 2).reshape(1, row_count, local_width)
    key_terms = key_h.transpose(1, 0, 2).reshape(key_count, local_width)
    value_terms = value_h.transpose(1, 0, 2).reshape(key_count, local_width)
    both_terms = jnp.stack([key_terms, value_terms])
    owned = lax.psum_scatter(both_terms.astype(BF), "seq", scatter_dimension=1, tiled=True)
    grad_qkv = jnp.concatenate([grad_q, owned], axis=0)
    token_count = row_count * lax.axis_size("seq") * lax.axis_size("dp")
    grad_factor = 1.0 / math.sqrt(token_count)
    terms_qkv = jnp.einsum("td,cth->cdh", normalized_rows, grad_qkv, preferred_element_type=F32)
    term_out = jnp.einsum("td,th->dh", row_gradients, attended_flat, preferred_element_type=F32)
    terms = jnp.concatenate([terms_qkv, term_out[None]], axis=0) * grad_factor
    seq_summed = lax.psum_scatter(terms.astype(BF), "seq", scatter_dimension=1, tiled=True)
    weight_grads = lax.psum_scatter(seq_summed, "dp", scatter_dimension=1, tiled=True).astype(F32)
    input_part = jnp.einsum("cth,cdh->td", grad_qkv, weights[:3], preferred_element_type=F32)
    reduced_total = lax.psum(input_part.astype(BF), "pipe").astype(F32)
    leading_term = jnp.mean(reduced_total, axis=1, keepdims=True)
    trailing_term = jnp.mean(reduced_total * standardized_input, axis=1, keepdims=True)
    input_gradient = (
        row_gradients.astype(F32)
        + inverse_deviation * (reduced_total - leading_term - standardized_input * trailing_term)
    ).astype(BF)
    return (input_gradient[None], weight_grads)


def local(embeddings, upstream, attn_weights):
    n = lax.axis_size("seq")
    heads = attn_weights.shape[2] // HD
    one_head_each = (
        heads == n
        and n == 4
        and lax.axis_size("grp") == 2
        and lax.axis_size("dp") == 2
        and lax.axis_size("pipe") == 2
        and attn_weights.shape[1] % 16 == 0
        and embeddings.shape[0] == 1
        and embeddings.shape[1] % 32 == 0
    )
    return (local_heads if one_head_each else local_gathered)(embeddings, upstream, attn_weights)


def solution(mesh):
    in_specs = (
        P(("grp", "dp"), "seq", None),
        P(("grp", "dp"), "seq", None),
        P(None, ("seq", "dp"), "pipe"),
    )
    out_specs = (P(("grp", "dp"), "seq", None), P("grp", ("seq", "dp"), "pipe"))
    return jax.shard_map(local, mesh=mesh, in_specs=in_specs, out_specs=out_specs, check_vma=False)
```
